256 devices in a mesh: lat: 16 (over y_lo, x, core), lon: 16 (over y_hi, z).
Axes of the slice: x: 4, y: 4 (y_hi: 2, y_lo: 2; y = y_hi * 2 + y_lo), z: 8, core: 2. Of those that a mesh axis runs over, the one named last changes fastest.
Arguments:
- state: bfloat16 [64, 128, 4320], P(None, 'lat', 'lon'), may hold values from -6 to 6
- land_sea: int32 [128, 4320], P('lat', 'lon'), may hold values 0 or 1
- cotangent: bfloat16 [64, 128, 4320], P(None, 'lat', 'lon'), may hold values from -6 to 6
- kernel: float32 [64, 7, 7], replicated, may hold values from -0.875 to 0.875
- conv_bias: float32 [64], replicated, may hold values from -4 to 4
- ln_gain: float32 [64], replicated, may hold values from 0.1 to 1.9
- ln_bias: float32 [64], replicated, may hold values from -3 to 3
- w_expand: bfloat16 [64, 256], replicated, may hold values from -0.75 to 0.75
- b_expand: float32 [256], replicated, may hold values from -3 to 3
- w_project: bfloat16 [256, 64], replicated, may hold values from -0.375 to 0.375
Outputs:
- state_grad: bfloat16 [64, 128, 4320], P(None, 'lat', 'lon')
- kernel_grad: float32 [64, 7, 7], replicated
- conv_bias_grad: float32 [64], replicated
- gain_grad: float32 [64], replicated
- ln_bias_grad: float32 [64], replicated
- expand_grad: float32 [64, 256], replicated
- b_expand_grad: float32 [256], replicated
- project_grad: float32 [256, 64], replicated
- b_project_grad: float32 [64], replicated
The draws below stay inside these ranges and needn't reach their ends.
Inputs may be any that keep to these rules, and one draw needn't show every extreme that they name: `land_sea`: 1 marks an ocean cell, 0 a land cell.
All inputs are finite; a program needn't handle non-finite values. No bound on the sum of `land_sea` on one device may be relied on, other than what follows from the above.
Results may differ from the reference program's by a relative error of at most 0.0064.
Values may be sent and summed in bfloat16 or wider, within the bound.
A program may use at most 64 MiB of HBM per device.

```python
import math
import jax
import jax.numpy as jnp
from jax import lax

CHAN = 64
EXPAND = 256
TAPS = 7
ROWS_DEV = 8
NLAT = 128
NLON = 4320
N_LAT = 16


def plant(array, key, least, top_value):
    shape = array.shape
    index_at = [jax.random.randint(jax.random.fold_in(key, axis), (), 0, shape[axis]) for axis in range(len(shape))]
    array = array.at[tuple(index_at)].set(least)
    longest = shape.index(max(shape))
    index_at[longest] = (index_at[longest] + 1) % shape[longest]
    return array.at[tuple(index_at)].set(top_value)


def steps_of(key, dims, cuts, smallest, top_value):
    def one(dim, shards_of):
        steps = jax.random.uniform(jax.random.fold_in(jax.random.fold_in(key, 6), dim), (shards_of,), jnp.float32, smallest / len(cuts), top_value / len(cuts))
        return jnp.repeat(jnp.exp(steps), dims[dim] // shards_of).reshape((-1,) + (1,) * (len(dims) - dim - 1))

    gain = one(*cuts[0])
    for cut in cuts[1:]:
        gain = gain * one(*cut)
    return gain


def gaussian(own_key, shape, deviation, reach, cuts=(), kind=jnp.bfloat16):
    loudness = steps_of(own_key, shape, cuts, -0.22, 0.18) if cuts else 1.0
    result = jax.random.normal(own_key, shape, jnp.float32) * deviation * loudness
    return jnp.minimum(jnp.maximum(result, -reach), reach).astype(kind)


def setup_inputs(seed: int = 0) -> dict:
    splits = jax.random.split(jax.random.key(seed), 11)
    state = gaussian(splits[0], (CHAN, NLAT, NLON), 1.0, 6.0, ((1, 16), (2, 16)))
    land_sea = plant((jax.random.randint(splits[1], (NLAT, NLON), 0, 4) < 3).astype(jnp.int32), jax.random.fold_in(splits[1], 1), 0, 1)
    cotangent = gaussian(splits[2], (CHAN, NLAT, NLON), 1.0, 6.0, ((1, 16), (2, 16)))
    kernel = gaussian(splits[3], (CHAN, TAPS, TAPS), (TAPS * TAPS) ** -0.5, 0.875, (), jnp.float32)
    conv_bias = gaussian(splits[4], (CHAN,), 1.0, 4.0, (), jnp.float32)
    ln_gain = jnp.clip(1.0 + 0.18 * jax.random.normal(splits[5], (CHAN,), jnp.float32), 0.1, 1.9)
    ln_bias = gaussian(splits[6], (CHAN,), 0.5, 3.0, (), jnp.float32)
    w_expand = gaussian(splits[7], (CHAN, EXPAND), CHAN ** -0.5, 0.75)
    b_expand = gaussian(splits[8], (EXPAND,), 0.5, 3.0, (), jnp.float32)
    w_project = gaussian(splits[9], (EXPAND, CHAN), EXPAND ** -0.5, 0.375)
    return {"state": state, "land_sea": land_sea, "cotangent": cotangent, "kernel": kernel, "conv_bias": conv_bias, "ln_gain": ln_gain, "ln_bias": ln_bias, "w_expand": w_expand, "b_expand": b_expand, "w_project": w_project}


ln_eps = 1e-06
root_half = 0.7071067811865476
inv_root_tau = 0.3989422804014327
highest = lax.Precision.HIGHEST

def gelu_value(values):
    return 0.5 * values * (1.0 + lax.erf(values * root_half))

def gelu_slope(values):
    return 0.5 * (1.0 + lax.erf(values * root_half)) + values * jnp.exp(-0.5 * values * values) * inv_root_tau

def pad_field(field):
    padded = jnp.pad(field, ((0, 0), (3, 3), (0, 0)))
    return jnp.concatenate([padded[:, :, -3:], padded, padded[:, :, :3]], axis=2)

def depthwise(padded, kernel, n_rows, n_cols):
    total = jnp.zeros((padded.shape[0], n_rows, n_cols), jnp.float32)
    for row_tap in range(TAPS):
        for col_tap in range(TAPS):
            total = total + kernel[:, row_tap, col_tap][:, None, None] * padded[:, row_tap:row_tap + n_rows, col_tap:col_tap + n_cols]
    return total

def transpose_conv(padded, kernel, n_rows, n_cols):
    total = jnp.zeros((padded.shape[0], n_rows, n_cols), jnp.float32)
    for row_tap in range(TAPS):
        for col_tap in range(TAPS):
            total = total + kernel[:, row_tap, col_tap][:, None, None] * padded[:, 6 - row_tap:6 - row_tap + n_rows, 6 - col_tap:6 - col_tap + n_cols]
    return total

def kernel_sums(dconv, padded, n_rows, n_cols):
    taps = []
    for row_tap in range(TAPS):
        for col_tap in range(TAPS):
            taps.append(lax.optimization_barrier(jnp.sum(dconv * padded[:, row_tap:row_tap + n_rows, col_tap:col_tap + n_cols], axis=(1, 2))))
    return jnp.stack(taps, axis=1).reshape(dconv.shape[0], TAPS, TAPS)

def cell_terms(conv_out, wet_cot, ln_gain, ln_bias, w_expand, b_expand, w_project):
    center = conv_out - lax.optimization_barrier(jnp.mean(conv_out, axis=0, keepdims=True))
    rstd = lax.rsqrt(lax.optimization_barrier(jnp.mean(center * center, axis=0, keepdims=True)) + ln_eps)
    normed = center * rstd
    zed = (normed * ln_gain[:, None, None] + ln_bias[:, None, None]).astype(jnp.bfloat16)
    pre = jnp.einsum('chw,ce->ehw', zed.astype(jnp.float32), w_expand.astype(jnp.float32), precision=highest) + b_expand[:, None, None]
    act = gelu_value(pre).astype(jnp.bfloat16)
    dact = jnp.einsum('chw,ec->ehw', wet_cot.astype(jnp.float32), w_project.astype(jnp.float32), precision=highest)
    dhid = (dact * gelu_slope(pre)).astype(jnp.bfloat16)
    dzed = jnp.einsum('ehw,ce->chw', dhid.astype(jnp.float32), w_expand.astype(jnp.float32), precision=highest)
    dnorm = dzed * ln_gain[:, None, None]
    dconv = rstd * (dnorm - lax.optimization_barrier(jnp.mean(dnorm, axis=0, keepdims=True)) - normed * lax.optimization_barrier(jnp.mean(dnorm * normed, axis=0, keepdims=True)))
    return (zed, act, dhid, normed, dzed, dconv)

def pointwise_sums(zed, act, dhid, normed, dzed, wet_cot):
    expand_sum = jnp.einsum('chw,ehw->ce', zed.astype(jnp.float32), dhid.astype(jnp.float32), precision=highest)
    b_expand_sum = lax.optimization_barrier(jnp.sum(dhid.astype(jnp.float32), axis=(1, 2)))
    project_sum = jnp.einsum('ehw,chw->ec', act.astype(jnp.float32), wet_cot.astype(jnp.float32), precision=highest)
    b_project_sum = lax.optimization_barrier(jnp.sum(wet_cot.astype(jnp.float32), axis=(1, 2)))
    gain_sum = lax.optimization_barrier(jnp.sum(dzed * normed, axis=(1, 2)))
    bias_sum = lax.optimization_barrier(jnp.sum(dzed, axis=(1, 2)))
    return (expand_sum, b_expand_sum, project_sum, b_project_sum, gain_sum, bias_sum)

def reference(state, land_sea, cotangent, kernel, conv_bias, ln_gain, ln_bias, w_expand, b_expand, w_project):
    state_pad = pad_field(state.astype(jnp.float32))
    conv_out = depthwise(state_pad, kernel, NLAT, NLON) + conv_bias[:, None, None]
    wet_cot = cotangent * land_sea[None].astype(cotangent.dtype)
    conv_blocks = conv_out.reshape(CHAN, N_LAT, ROWS_DEV, NLON).transpose(1, 0, 2, 3)
    cot_blocks = wet_cot.reshape(CHAN, N_LAT, ROWS_DEV, NLON).transpose(1, 0, 2, 3)

    def step(carry, pieces):
        terms = cell_terms(pieces[0], pieces[1], ln_gain, ln_bias, w_expand, b_expand, w_project)
        sums = pointwise_sums(terms[0], terms[1], terms[2], terms[3], terms[4], pieces[1])
        return (tuple((old + new for old, new in zip(carry, sums))), terms[5])
    start = (jnp.zeros((CHAN, EXPAND), jnp.float32), jnp.zeros((EXPAND,), jnp.float32), jnp.zeros((EXPAND, CHAN), jnp.float32), jnp.zeros((CHAN,), jnp.float32), jnp.zeros((CHAN,), jnp.float32), jnp.zeros((CHAN,), jnp.float32))
    sums, dconv_blocks = lax.scan(step, start, (conv_blocks, cot_blocks))
    dconv = dconv_blocks.transpose(1, 0, 2, 3).reshape(CHAN, NLAT, NLON)
    scale = 1.0 / math.sqrt(NLAT * NLON)
    kernel_grad = kernel_sums(dconv, state_pad, NLAT, NLON) * scale
    conv_bias_grad = lax.optimization_barrier(jnp.sum(dconv, axis=(1, 2))) * scale
    state_grad = (cotangent.astype(jnp.float32) + transpose_conv(pad_field(dconv), kernel, NLAT, NLON)).astype(jnp.bfloat16)
    return (state_grad, kernel_grad, conv_bias_grad, sums[4] * scale, sums[5] * scale, sums[0] * scale, sums[1] * scale, sums[2] * scale, sums[3] * scale)
```

```python
import math

import jax
import jax.numpy as jnp
from jax import lax
from jax.experimental import pallas as pl
from jax.experimental.pallas import tpu as pltpu
from jax.sharding import PartitionSpec as P

TAPS = 7


ln_eps = 1e-06
root_half = 0.7071067811865476
inv_root_tau = 0.3989422804014327


def extended(shard, sides, width, wrap):
    for axis, dim in sides:
        size, length = (lax.axis_size(axis), shard.shape[dim])
        up = [(i, (i + 1) % size) for i in range(size if wrap else size - 1)]
        down = [(j, i) for i, j in up]
        last = lax.slice_in_dim(shard, length - width, length, axis=dim)
        first = lax.slice_in_dim(shard, 0, width, axis=dim)
        before = lax.ppermute(last, axis, up)
        after = lax.ppermute(first, axis, down)
        shard = jnp.concatenate([before, shard, after], axis=dim)
    return shard


def gelu_value(values):
    return 0.5 * values * (1.0 + lax.erf(values * root_half))


def gelu_slope(values):
    return (
        0.5 * (1.0 + lax.erf(values * root_half))
        + values * jnp.exp(-0.5 * values * values) * inv_root_tau
    )


def extend_in(field, rim_width):
    row_rim = extended(field, (("lat", 1),), rim_width, False)
    return extended(row_rim, (("lon", 2),), rim_width, True)


def extend_back(field):
    row_rim = extended(field, (("lat", 1),), 3, False)
    return extended(row_rim, (("lon", 2),), 3, True)


def depthwise(padded, kernel, n_rows, n_cols):
    total = jnp.zeros((padded.shape[0], n_rows, n_cols), jnp.float32)
    for row_tap in range(TAPS):
        for col_tap in range(TAPS):
            total = (
                total
                + kernel[:, row_tap, col_tap][:, None, None]
                * padded[:, row_tap : row_tap + n_rows, col_tap : col_tap + n_cols]
            )
    return total


def transpose_conv(padded, kernel, n_rows, n_cols):
    total = jnp.zeros((padded.shape[0], n_rows, n_cols), jnp.float32)
    for row_tap in range(TAPS):
        for col_tap in range(TAPS):
            total = (
                total
                + kernel[:, row_tap, col_tap][:, None, None]
                * padded[:, 6 - row_tap : 6 - row_tap + n_rows, 6 - col_tap : 6 - col_tap + n_cols]
            )
    return total


def kernel_sums(dconv, padded, n_rows, n_cols):
    taps = []
    for row_tap in range(TAPS):
        for col_tap in range(TAPS):
            taps.append(
                jnp.sum(
                    dconv * padded[:, row_tap : row_tap + n_rows, col_tap : col_tap + n_cols],
                    axis=(1, 2),
                )
            )
    return jnp.stack(taps, axis=1).reshape(dconv.shape[0], TAPS, TAPS)


def cell_terms(conv_out, wet_cot, ln_gain, ln_bias, w_expand, b_expand, w_project):
    center = conv_out - jnp.mean(conv_out, axis=0, keepdims=True)
    rstd = lax.rsqrt(jnp.mean(center * center, axis=0, keepdims=True) + ln_eps)
    normed = center * rstd
    zed = (normed * ln_gain[:, None, None] + ln_bias[:, None, None]).astype(jnp.bfloat16)
    pre = (
        jnp.einsum("chw,ce->ehw", zed, w_expand, preferred_element_type=jnp.float32)
        + b_expand[:, None, None]
    )
    act = gelu_value(pre).astype(jnp.bfloat16)
    dact = jnp.einsum("chw,ec->ehw", wet_cot, w_project, preferred_element_type=jnp.float32)
    dhid = (dact * gelu_slope(pre)).astype(jnp.bfloat16)
    dzed = jnp.einsum("ehw,ce->chw", dhid, w_expand, preferred_element_type=jnp.float32)
    dnorm = dzed * ln_gain[:, None, None]
    dconv = rstd * (
        dnorm
        - jnp.mean(dnorm, axis=0, keepdims=True)
        - normed * jnp.mean(dnorm * normed, axis=0, keepdims=True)
    )
    return (zed, act, dhid, normed, dzed, dconv)


def pointwise_sums(zed, act, dhid, normed, dzed, wet_cot):
    expand_sum = jnp.einsum("chw,ehw->ce", zed, dhid, preferred_element_type=jnp.float32)
    b_expand_sum = jnp.sum(dhid.astype(jnp.float32), axis=(1, 2))
    project_sum = jnp.einsum("ehw,chw->ec", act, wet_cot, preferred_element_type=jnp.float32)
    b_project_sum = jnp.sum(wet_cot.astype(jnp.float32), axis=(1, 2))
    gain_sum = jnp.sum(dzed * normed, axis=(1, 2))
    bias_sum = jnp.sum(dzed, axis=(1, 2))
    return (expand_sum, b_expand_sum, project_sum, b_project_sum, gain_sum, bias_sum)


N_GROUP = 16
CHUNK = 18
MESH = pl.DeviceIdType.MESH


def reduce_kernel(x_ref, o_ref, part, gather, s1, r1, s2, r2, s3, r3):
    la = lax.axis_index("lat")
    lo = lax.axis_index("lon")

    def lat_peer(k):
        return {"lat": lax.rem(la + k, N_GROUP), "lon": lo}

    def lon_peer(k):
        return {"lat": la, "lon": lax.rem(lo + k, N_GROUP)}

    barrier = pltpu.get_barrier_semaphore()
    for k in range(1, N_GROUP):
        pl.semaphore_signal(barrier, inc=1, device_id=lat_peer(k), device_id_type=MESH)
        pl.semaphore_signal(barrier, inc=1, device_id=lon_peer(k), device_id_type=MESH)
    pl.semaphore_wait(barrier, 2 * (N_GROUP - 1))

    copies = []
    for k in range(1, N_GROUP):
        copy = pltpu.make_async_remote_copy(
            src_ref=x_ref.at[lax.rem(la + k, N_GROUP)],
            dst_ref=part.at[k],
            send_sem=s1.at[k],
            recv_sem=r1.at[k],
            device_id=lat_peer(k),
            device_id_type=MESH,
        )
        copy.start()
        copies.append(copy)
    total = x_ref[la]
    for k in range(1, N_GROUP):
        copies[k - 1].wait()
        total = total + part[k]
    gather[lo] = total

    copies = []
    for k in range(1, N_GROUP):
        copy = pltpu.make_async_remote_copy(
            src_ref=gather.at[lo],
            dst_ref=gather.at[lo],
            send_sem=s2.at[k],
            recv_sem=r2.at[k],
            device_id=lon_peer(k),
            device_id_type=MESH,
        )
        copy.start()
        copies.append(copy)
    for copy in copies:
        copy.wait()
    total = gather[0]
    for k in range(1, N_GROUP):
        total = total + gather[k]
    o_ref[la] = total

    copies = []
    for k in range(1, N_GROUP):
        copy = pltpu.make_async_remote_copy(
            src_ref=o_ref.at[la],
            dst_ref=o_ref.at[la],
            send_sem=s3.at[k],
            recv_sem=r3.at[k],
            device_id=lat_peer(k),
            device_id_type=MESH,
        )
        copy.start()
        copies.append(copy)
    for copy in copies:
        copy.wait()


def reduce_all(parts):
    flat = jnp.concatenate([p.reshape(-1) for p in parts])
    room = N_GROUP * CHUNK * 128
    block = jnp.pad(flat, (0, room - flat.shape[0])).reshape(N_GROUP, CHUNK, 128)
    shape = (N_GROUP, CHUNK, 128)
    out = pl.pallas_call(
        reduce_kernel,
        out_shape=jax.ShapeDtypeStruct(shape, jnp.float32),
        in_specs=[pl.BlockSpec(memory_space=pltpu.VMEM)],
        out_specs=pl.BlockSpec(memory_space=pltpu.VMEM),
        scratch_shapes=[pltpu.VMEM(shape, jnp.float32)] * 2
        + [pltpu.SemaphoreType.DMA((N_GROUP,))] * 6,
        compiler_params=pltpu.CompilerParams(collective_id=0, has_side_effects=True),
    )(block)
    flat = out.reshape(-1)
    outs, at = [], 0
    for p in parts:
        outs.append(flat[at : at + p.size].reshape(p.shape))
        at += p.size
    return outs


def body(
    state, land_sea, cotangent, kernel, conv_bias, ln_gain, ln_bias, w_expand, b_expand, w_project
):
    n_chan, n_rows, n_cols = state.shape
    wet_cot = cotangent * land_sea[None].astype(jnp.bfloat16)
    state_ext = extend_in(state, 3).astype(jnp.float32)
    conv_out = depthwise(state_ext, kernel, n_rows, n_cols) + conv_bias[:, None, None]
    terms = cell_terms(conv_out, wet_cot, ln_gain, ln_bias, w_expand, b_expand, w_project)
    point = pointwise_sums(terms[0], terms[1], terms[2], terms[3], terms[4], wet_cot)
    dconv = terms[5]
    dconv_ext = extend_back(dconv)
    tap_sum = kernel_sums(dconv, state_ext, n_rows, n_cols)
    bias_conv_sum = jnp.sum(dconv, axis=(1, 2))
    totals = reduce_all(
        (point[0], point[1], point[2], point[3], point[4], point[5], tap_sum, bias_conv_sum)
    )
    state_grad = (
        cotangent.astype(jnp.float32) + transpose_conv(dconv_ext, kernel, n_rows, n_cols)
    ).astype(jnp.bfloat16)
    scale = 1.0 / math.sqrt(n_rows * lax.axis_size("lat") * n_cols * lax.axis_size("lon"))
    return (
        state_grad,
        totals[6] * scale,
        totals[7] * scale,
        totals[4] * scale,
        totals[5] * scale,
        totals[0] * scale,
        totals[1] * scale,
        totals[2] * scale,
        totals[3] * scale,
    )


def solution(mesh):
    in_specs = (
        P(None, "lat", "lon"),
        P("lat", "lon"),
        P(None, "lat", "lon"),
        P(),
        P(),
        P(),
        P(),
        P(),
        P(),
        P(),
    )
    out_specs = (P(None, "lat", "lon"), P(), P(), P(), P(), P(), P(), P(), P())
    return jax.shard_map(body, mesh=mesh, in_specs=in_specs, out_specs=out_specs, check_vma=False)
```

```python
import math

import jax
import jax.numpy as jnp
from jax import lax
from jax.experimental import pallas as pl
from jax.experimental.pallas import tpu as pltpu
from jax.sharding import PartitionSpec as P

TAPS = 7
CHAN = 64
EXPAND = 256
ROWS = 8
COLS = 270
HALF = 135
PITCH = 136
TILES = 17
CELLS = ROWS * PITCH
EXT_ROWS = 14
EXT_COLS = 144
STEP = 272
N_GROUP = 16
CHUNK = 18
MESH = pl.DeviceIdType.MESH

ln_eps = 1e-06
root_half = 0.7071067811865476
inv_root_tau = 0.3989422804014327

f32 = jnp.float32
bf16 = jnp.bfloat16


def dot(a, b, dims):
    return lax.dot_general(a, b, (dims, ((), ())), preferred_element_type=f32)


NN = ((1,), (0,))
NT = ((1,), (1,))
TN = ((0,), (0,))


def split(x):
    hi = x.astype(bf16)
    lo = (x - hi.astype(f32)).astype(bf16)
    return jnp.concatenate([hi, lo], axis=1)


def kernel_body(
    state_hbm,
    cot_hbm,
    land_ref,
    prm_ref,
    be_ref,
    we_ref,
    wp_ref,
    grad_ref,
    expand_ref,
    project_ref,
    small_ref,
    state_in,
    cot_in,
    planes,
    turned,
    s_ext,
    d_ext,
    wet32,
    wet16,
    x_ref,
    norm_ref,
    rstd_ref,
    zed_ref,
    pre_ref,
    dact_ref,
    act_ref,
    dhid_ref,
    taps_ref,
    wbd,
    wpbd,
    mean_ref,
    eg_ref,
    pg_ref,
    acc_ref,
    tap_out,
    pay,
    part,
    gather,
    total_ref,
    row_send,
    row_recv,
    col_send,
    col_recv,
    in_sem,
    row_ssem,
    row_rsem,
    col_ssem,
    col_rsem,
    s1,
    r1,
    s2,
    r2,
    s3,
    r3,
):
    la = lax.axis_index("lat")
    lo = lax.axis_index("lon")
    east = lax.rem(lo + 1, N_GROUP)
    west = lax.rem(lo + N_GROUP - 1, N_GROUP)
    has_north = la > 0
    has_south = la < N_GROUP - 1

    state_copy = pltpu.make_async_copy(state_hbm, state_in, in_sem.at[0])
    state_copy.start()
    cot_copy = pltpu.make_async_copy(cot_hbm, cot_in, in_sem.at[1])
    cot_copy.start()

    def lat_peer(k):
        return {"lat": lax.rem(la + k, N_GROUP), "lon": lo}

    def lon_peer(k):
        return {"lat": la, "lon": lax.rem(lo + k, N_GROUP)}

    barrier = pltpu.get_barrier_semaphore()
    for k in range(1, N_GROUP):
        pl.semaphore_signal(barrier, inc=1, device_id=lat_peer(k), device_id_type=MESH)
        pl.semaphore_signal(barrier, inc=1, device_id=lon_peer(k), device_id_type=MESH)
    for side in (east, west):

        @pl.when(has_north)
        def _():
            pl.semaphore_signal(
                barrier, inc=1, device_id={"lat": la - 1, "lon": side}, device_id_type=MESH
            )

        @pl.when(has_south)
        def _():
            pl.semaphore_signal(
                barrier, inc=1, device_id={"lat": la + 1, "lon": side}, device_id_type=MESH
            )

    lane = lax.broadcasted_iota(jnp.int32, (ROWS, 8, 128), 2)
    sub = lax.broadcasted_iota(jnp.int32, (ROWS, 8, 128), 1)

    for i in range(TAPS * TAPS):
        taps_ref[i] = jnp.broadcast_to(prm_ref[i : i + 1, :], (8, 128))
    wbd[...] = jnp.zeros((128, 512), bf16)
    wbd[0:64, 0:256] = we_ref[...]
    wbd[64:128, 256:512] = we_ref[...]
    nothing = jnp.zeros((EXPAND, CHAN), bf16)
    wpbd[0:256, :] = jnp.concatenate([wp_ref[...], nothing], axis=1)
    wpbd[256:512, :] = jnp.concatenate([nothing, wp_ref[...]], axis=1)
    at_row = lax.broadcasted_iota(jnp.int32, (256, 128), 0)
    at_col = lax.broadcasted_iota(jnp.int32, (256, 128), 1)
    same = lax.rem(at_row, 128) // 64 == at_col // 64
    mean_ref[...] = jnp.where(same, 1.0 / CHAN, 0.0).astype(bf16)

    conv_bias = prm_ref[49:50, :]
    gain = prm_ref[50:51, :]
    ln_bias = prm_ref[51:52, :]

    s_ext[:, 136:144, :] = jnp.zeros((EXT_ROWS, 8, 128), f32)
    d_ext[:, 136:144, :] = jnp.zeros((EXT_ROWS, 8, 128), f32)
    for ref in (s_ext, d_ext):

        @pl.when(jnp.logical_not(has_north))
        def _():
            ref[0:3] = jnp.zeros((3, EXT_COLS, 128), f32)

        @pl.when(jnp.logical_not(has_south))
        def _():
            ref[11:14] = jnp.zeros((3, EXT_COLS, 128), f32)

    planes[2] = jnp.zeros((CHAN * ROWS, 128), f32)

    def to_planes(load):
        def step(i, carry):
            at = pl.ds(pl.multiple_of(i * 8, 8), 8)
            x = load(at)
            to = pl.ds(pl.multiple_of(i * 64, 64), 64)
            planes[0, to, :] = x[:, :, 0:128].reshape(64, 128)
            planes[1, to, :] = x[:, :, 128:256].reshape(64, 128)
            planes[2, to, 0:14] = x[:, :, 256:270].reshape(64, 14)
            return carry

        lax.fori_loop(0, 8, step, 0)

    half_lane = lax.broadcasted_iota(jnp.int32, (PITCH, 128), 1) < 64

    def turn_in(put):
        def step(p, carry):
            r = p * 2
            for k in range(3):
                both = jnp.concatenate(
                    [
                        planes[k, pl.ds(r, CHAN, stride=ROWS), :],
                        planes[k, pl.ds(r + 1, CHAN, stride=ROWS), :],
                    ],
                    axis=0,
                )
                turned[128 * k : 128 * k + 128, :] = both.T
            h0 = turned[0:PITCH, :]
            h1 = turned[HALF : HALF + PITCH, :]
            put(r, jnp.where(half_lane, h0, pltpu.roll(h1, 64, axis=1)))
            put(r + 1, jnp.where(half_lane, pltpu.roll(h0, 64, axis=1), h1))
            return carry

        lax.fori_loop(0, ROWS // 2, step, 0)

    def exchange(ext, n):
        to_east = pltpu.roll(ext[3:11, 135:143, :], 64, axis=2)
        to_west = pltpu.roll(ext[3:11, 1:9, :], 64, axis=2)
        col_send[n, 0] = to_east
        col_send[n, 1] = to_west
        ext[3:11, 0:8, :] = jnp.where((sub < 3) & (lane >= 64), to_east, ext[3:11, 0:8, :])
        ext[3:11, 136:144, :] = jnp.where(
            (sub >= 2) & (sub < 5) & (lane < 64), to_west, ext[3:11, 136:144, :]
        )
        row_send[n, 0] = ext[3:6].astype(bf16)
        row_send[n, 1] = ext[8:11].astype(bf16)

    def rows_copy(n, way):
        return pltpu.make_async_remote_copy(
            src_ref=row_send.at[n, way],
            dst_ref=row_recv.at[n, way],
            send_sem=row_ssem.at[n, way],
            recv_sem=row_rsem.at[n, way],
            device_id={"lat": la - 1 + 2 * way, "lon": lo},
            device_id_type=MESH,
        )

    def cols_copy(n, way, turn):
        src = col_send.at[n, way]
        dst = col_recv.at[n, way]
        if turn == 1:
            src, dst = src.at[0:3], dst.at[11:14]
        elif turn == 2:
            src, dst = src.at[5:8], dst.at[0:3]
        else:
            dst = dst.at[3:11]
        return pltpu.make_async_remote_copy(
            src_ref=src,
            dst_ref=dst,
            send_sem=col_ssem.at[n, way, turn],
            recv_sem=col_rsem.at[n, way, turn],
            device_id={
                "lat": la + (0, -1, 1)[turn],
                "lon": (east, west)[way],
            },
            device_id_type=MESH,
        )

    def start_copies(n):
        @pl.when(has_north)
        def _():
            rows_copy(n, 0).start()
            cols_copy(n, 0, 1).start()
            cols_copy(n, 1, 1).start()

        @pl.when(has_south)
        def _():
            rows_copy(n, 1).start()
            cols_copy(n, 0, 2).start()
            cols_copy(n, 1, 2).start()

        cols_copy(n, 0, 0).start()
        cols_copy(n, 1, 0).start()

    def finish_copies(ext, n):
        @pl.when(has_north)
        def _():
            rows_copy(n, 0).wait_send()
            cols_copy(n, 0, 1).wait_send()
            cols_copy(n, 1, 1).wait_send()
            rows_copy(n, 1).wait_recv()
            cols_copy(n, 0, 2).wait_recv()
            cols_copy(n, 1, 2).wait_recv()
            ext[0:3] = row_recv[n, 1].astype(f32)

        @pl.when(has_south)
        def _():
            rows_copy(n, 1).wait_send()
            cols_copy(n, 0, 2).wait_send()
            cols_copy(n, 1, 2).wait_send()
            rows_copy(n, 0).wait_recv()
            cols_copy(n, 0, 1).wait_recv()
            cols_copy(n, 1, 1).wait_recv()
            ext[11:14] = row_recv[n, 0].astype(f32)

        cols_copy(n, 0, 0).wait()
        cols_copy(n, 1, 0).wait()

        def fill(first, last):
            from_west = col_recv[n, 0, first:last]
            from_east = col_recv[n, 1, first:last]
            m = last - first
            ext[first:last, 0:8, :] = jnp.where(
                (sub[:m] < 3) & (lane[:m] < 64), from_west, ext[first:last, 0:8, :]
            )
            ext[first:last, 136:144, :] = jnp.where(
                (sub[:m] >= 2) & (sub[:m] < 5) & (lane[:m] >= 64),
                from_east,
                ext[first:last, 136:144, :],
            )

        fill(3, 11)

        @pl.when(has_north)
        def _():
            fill(0, 3)

        @pl.when(has_south)
        def _():
            fill(11, 14)

    def convolve(ext, flip, bias):
        def step(t, carry):
            at = pl.multiple_of(t * 8, 8)
            acc = jnp.zeros((ROWS, 8, 128), f32)
            if bias is not None:
                acc = acc + bias[None]
            for b in range(TAPS):
                x = ext[:, pl.ds(at + b, 8), :]
                for a in range(TAPS):
                    i = a * TAPS + b
                    acc = acc + taps_ref[48 - i if flip else i][None] * x[a : a + ROWS]
            for r in range(ROWS):
                x_ref[pl.ds(at + r * PITCH, 8), :] = acc[r]
            return carry

        lax.fori_loop(0, TILES, step, 0)

    state_copy.wait()
    to_planes(lambda at: state_in[at].astype(f32))

    def put_state(r, value):
        s_ext[r + 3, 3 : 3 + PITCH, :] = value

    turn_in(put_state)
    exchange(s_ext, 0)
    pl.semaphore_wait(
        barrier,
        2 * (N_GROUP - 1)
        + 2 * has_north.astype(jnp.int32)
        + 2 * has_south.astype(jnp.int32),
    )
    start_copies(0)

    cot_copy.wait()
    land = land_ref[...].astype(f32)
    to_planes(lambda at: cot_in[at].astype(f32) * land[None])

    def put_wet(r, value):
        wet32[pl.ds(pl.multiple_of(r * PITCH, 8), PITCH), :] = value
        wet32[pl.ds(r * PITCH + HALF, 1), :] = jnp.zeros((1, 128), f32)

    turn_in(put_wet)
    acc_ref[...] = jnp.zeros((5, 8, 512), f32)
    eg_ref[...] = jnp.zeros((128, 512), f32)
    pg_ref[...] = jnp.zeros((128, 512), f32)

    def narrow(i, carry):
        at = pl.ds(pl.multiple_of(i * 16, 16), 16)
        w = wet32[at, :]
        wet16[at, :] = w.astype(bf16)
        return carry + w[0:8] + w[8:16]

    acc_ref[0, :, 0:128] = lax.fori_loop(0, CELLS // 16, narrow, jnp.zeros((8, 128), f32))

    finish_copies(s_ext, 0)
    convolve(s_ext, False, conv_bias)

    def fold(x):
        return jnp.sum(x.reshape(-1, 8, x.shape[-1]), axis=0)

    def pointwise(q, carry):
        at = pl.ds(pl.multiple_of(q * STEP, STEP), STEP)
        x = x_ref[at, :]
        cen = x - dot(split(x), mean_ref[...], NN)
        rstd = lax.rsqrt(dot(split(cen * cen), mean_ref[...], NN) + ln_eps)
        normed = cen * rstd
        zed = (normed * gain + ln_bias).astype(bf16)
        norm_ref[...] = normed
        rstd_ref[...] = rstd
        zed_ref[...] = zed
        pre_ref[...] = dot(zed, wbd[...], NN)
        wet = wet16[at, :]
        dact_ref[...] = dot(wet, wpbd[...], NT)

        def gelu(i, total):
            rows = pl.ds(pl.multiple_of(i * 16, 16), 16)
            for k in range(4):
                cols = slice(128 * k, 128 * k + 128)
                pre = pre_ref[rows, cols] + be_ref[0:1, cols]
                grow = jnp.exp(-0.5 * pre * pre)
                t = 1.0 / (1.0 + (0.3275911 * root_half) * jnp.abs(pre))
                poly = 0.5 * 1.061405429 * t - 0.5 * 1.453152027
                poly = poly * t + 0.5 * 1.421413741
                poly = poly * t - 0.5 * 0.284496736
                poly = poly * t + 0.5 * 0.254829592
                tail = poly * t * grow
                phi = jnp.where(pre >= 0, 1.0 - tail, tail)
                slope = phi + pre * grow * inv_root_tau
                act_ref[rows, cols] = (pre * phi).astype(bf16)
                dhid = (dact_ref[rows, cols] * slope).astype(bf16)
                dhid_ref[rows, cols] = dhid
                wide = dhid.astype(f32)
                acc_ref[1, :, cols] += wide[0:8] + wide[8:16]
            return total

        lax.fori_loop(0, STEP // 16, gelu, 0)
        dhid = dhid_ref[...]
        dzed = dot(dhid, wbd[...], NT)
        normed = norm_ref[...]
        acc_ref[2, :, 0:128] += fold(dzed * normed)
        acc_ref[3, :, 0:128] += fold(dzed)
        dnorm = dzed * gain
        m1 = dot(split(dnorm), mean_ref[...], NN)
        m2 = dot(split(dnorm * normed), mean_ref[...], NN)
        dconv = rstd_ref[...] * (dnorm - m1 - normed * m2)
        x_ref[at, :] = dconv
        acc_ref[4, :, 0:128] += fold(dconv)
        eg_ref[...] += dot(zed_ref[...], dhid, TN)
        pg_ref[...] += dot(wet16[at, :], act_ref[...], TN)
        return carry

    lax.fori_loop(0, CELLS // STEP, pointwise, 0)

    def place(r, carry):
        d_ext[r + 3, 3 : 3 + PITCH, :] = x_ref[pl.ds(pl.multiple_of(r * PITCH, 8), PITCH), :]
        return carry

    lax.fori_loop(0, ROWS, place, 0)
    exchange(d_ext, 1)
    start_copies(1)

    for b in range(TAPS):

        def tap_step(t, acc):
            at = pl.multiple_of(t * 8, 8)
            x = s_ext[:, pl.ds(at + b, 8), :]
            d = [x_ref[pl.ds(at + r * PITCH, 8), :] for r in range(ROWS)]
            new = []
            for a in range(TAPS):
                s = acc[a]
                for r in range(ROWS):
                    s = s + d[r] * x[r + a]
                new.append(s)
            return tuple(new)

        zero = jnp.zeros((8, 128), f32)
        acc = lax.fori_loop(0, TILES, tap_step, (zero,) * TAPS)
        for a in range(TAPS):
            tap_out[a * TAPS + b] = acc[a]

    def halves(x):
        return x + pltpu.roll(x, 64, axis=1)

    first_half = lax.broadcasted_iota(jnp.int32, (1, 128), 1) < 64
    for i in range(N_GROUP):
        c, e = 8 * (i // 2), 128 * (i % 2)
        pay[i, 0:8, :] = (
            eg_ref[c : c + 8, e : e + 128] + eg_ref[64 + c : 72 + c, 256 + e : 384 + e]
        )
        pay[i, 8:16, :] = (
            pg_ref[c : c + 8, e : e + 128] + pg_ref[64 + c : 72 + c, 256 + e : 384 + e]
        )

    def sums_of(x):
        return halves(jnp.sum(x, axis=0, keepdims=True))

    rows = []
    for i in range(25):
        one = sums_of(tap_out[i])
        two = sums_of(tap_out[25 + i]) if i < 24 else jnp.zeros((1, 128), f32)
        rows.append(jnp.where(first_half, one, two))
    wide = jnp.sum(acc_ref[1], axis=0, keepdims=True)
    wide = wide[:, 0:256] + wide[:, 256:512]
    rows.append(wide[:, 0:128])
    rows.append(wide[:, 128:256])
    rows.append(
        jnp.where(first_half, sums_of(acc_ref[4, :, 0:128]), sums_of(acc_ref[2, :, 0:128]))
    )
    rows.append(
        jnp.where(first_half, sums_of(acc_ref[3, :, 0:128]), sums_of(acc_ref[0, :, 0:128]))
    )
    while len(rows) < 32:
        rows.append(jnp.zeros((1, 128), f32))
    for i in range(N_GROUP):
        pay[i, 16:17, :] = rows[2 * i]
        pay[i, 17:18, :] = rows[2 * i + 1]

    copies1 = []
    for k in range(1, N_GROUP):
        copy = pltpu.make_async_remote_copy(
            src_ref=pay.at[lax.rem(la + k, N_GROUP)],
            dst_ref=part.at[k],
            send_sem=s1.at[k],
            recv_sem=r1.at[k],
            device_id=lat_peer(k),
            device_id_type=MESH,
        )
        copy.start()
        copies1.append(copy)

    finish_copies(d_ext, 1)
    convolve(d_ext, True, None)

    total = pay[la]
    for k in range(1, N_GROUP):
        copies1[k - 1].wait()
        total = total + part[k]
    gather[lo] = total
    copies2 = []
    for k in range(1, N_GROUP):
        copy = pltpu.make_async_remote_copy(
            src_ref=gather.at[lo],
            dst_ref=gather.at[lo],
            send_sem=s2.at[k],
            recv_sem=r2.at[k],
            device_id=lon_peer(k),
            device_id_type=MESH,
        )
        copy.start()
        copies2.append(copy)

    def turn_out(p, carry):
        r = p * 2
        g0 = x_ref[pl.ds(pl.multiple_of(r * PITCH, 8), PITCH), :]
        g1 = x_ref[pl.ds(pl.multiple_of(r * PITCH + PITCH, 8), PITCH), :]
        turned[0:PITCH, :] = jnp.where(half_lane, g0, pltpu.roll(g1, 64, axis=1))
        turned[HALF : HALF + PITCH, :] = jnp.where(half_lane, pltpu.roll(g0, 64, axis=1), g1)
        for k in range(3):
            back = turned[128 * k : 128 * k + 128, :].T
            planes[k, pl.ds(r, CHAN, stride=ROWS), :] = back[0:64]
            planes[k, pl.ds(r + 1, CHAN, stride=ROWS), :] = back[64:128]
        return carry

    lax.fori_loop(0, ROWS // 2, turn_out, 0)

    def write_out(i, carry):
        at = pl.ds(pl.multiple_of(i * 8, 8), 8)
        of = pl.ds(pl.multiple_of(i * 64, 64), 64)
        for k in range(3):
            cols = slice(128 * k, min(128 * k + 128, COLS))
            width = cols.stop - cols.start
            value = planes[k, of, 0:width].reshape(8, 8, width)
            grad_ref[at, :, cols] = (cot_in[at, :, cols].astype(f32) + value).astype(bf16)
        return carry

    lax.fori_loop(0, 8, write_out, 0)

    for copy in copies2:
        copy.wait()
    total = gather[0]
    for k in range(1, N_GROUP):
        total = total + gather[k]
    scale = 1.0 / math.sqrt(ROWS * N_GROUP * COLS * N_GROUP)
    total_ref[la] = total * scale
    copies3 = []
    for k in range(1, N_GROUP):
        copy = pltpu.make_async_remote_copy(
            src_ref=total_ref.at[la],
            dst_ref=total_ref.at[la],
            send_sem=s3.at[k],
            recv_sem=r3.at[k],
            device_id=lat_peer(k),
            device_id_type=MESH,
        )
        copy.start()
        copies3.append(copy)
    for copy in copies3:
        copy.wait()

    for e in range(2):
        pieces = []
        for c in range(8):
            i = 2 * c + e
            expand_ref[8 * c : 8 * c + 8, 128 * e : 128 * e + 128] = total_ref[i, 0:8, :]
            pieces.append(total_ref[i, 8:16, :])
        pieces.append(jnp.zeros((64, 128), f32))
        project_ref[128 * e : 128 * e + 128, :] = jnp.concatenate(pieces, axis=0).T[:, 0:64]
    for i in range(N_GROUP):
        small_ref[2 * i : 2 * i + 2, :] = total_ref[i, 16:18, :]


def body(
    state, land_sea, cotangent, kernel, conv_bias, ln_gain, ln_bias, w_expand, b_expand, w_project
):
    taps = kernel.reshape(CHAN, TAPS * TAPS).T
    prm = jnp.concatenate(
        [taps, conv_bias[None], ln_gain[None], ln_bias[None], jnp.zeros((4, CHAN), f32)], axis=0
    )
    prm = jnp.concatenate([prm, prm], axis=1)
    be = jnp.concatenate([b_expand, b_expand])[None]
    vmem = pl.BlockSpec(memory_space=pltpu.VMEM)
    anyw = pl.BlockSpec(memory_space=pl.ANY)
    sds = jax.ShapeDtypeStruct
    sem = pltpu.SemaphoreType.DMA
    piece = (N_GROUP, CHUNK, 128)
    grad, expand, project, small = pl.pallas_call(
        kernel_body,
        out_shape=(
            sds((CHAN, ROWS, COLS), bf16),
            sds((CHAN, EXPAND), f32),
            sds((EXPAND, CHAN), f32),
            sds((32, 128), f32),
        ),
        in_specs=[anyw, anyw, vmem, vmem, vmem, vmem, vmem],
        out_specs=(vmem, vmem, vmem, vmem),
        scratch_shapes=[
            pltpu.VMEM((CHAN, ROWS, COLS), bf16),
            pltpu.VMEM((CHAN, ROWS, COLS), bf16),
            pltpu.VMEM((3, CHAN * ROWS, 128), f32),
            pltpu.VMEM((384, 128), f32),
            pltpu.VMEM((EXT_ROWS, EXT_COLS, 128), f32),
            pltpu.VMEM((EXT_ROWS, EXT_COLS, 128), f32),
            pltpu.VMEM((CELLS, 128), f32),
            pltpu.VMEM((CELLS, 128), bf16),
            pltpu.VMEM((CELLS, 128), f32),
            pltpu.VMEM((STEP, 128), f32),
            pltpu.VMEM((STEP, 128), f32),
            pltpu.VMEM((STEP, 128), bf16),
            pltpu.VMEM((STEP, 512), f32),
            pltpu.VMEM((STEP, 512), f32),
            pltpu.VMEM((STEP, 512), bf16),
            pltpu.VMEM((STEP, 512), bf16),
            pltpu.VMEM((TAPS * TAPS, 8, 128), f32),
            pltpu.VMEM((128, 512), bf16),
            pltpu.VMEM((512, 128), bf16),
            pltpu.VMEM((256, 128), bf16),
            pltpu.VMEM((128, 512), f32),
            pltpu.VMEM((128, 512), f32),
            pltpu.VMEM((5, 8, 512), f32),
            pltpu.VMEM((TAPS * TAPS, 8, 128), f32),
            pltpu.VMEM(piece, f32),
            pltpu.VMEM(piece, f32),
            pltpu.VMEM(piece, f32),
            pltpu.VMEM(piece, f32),
            pltpu.VMEM((2, 2, 3, EXT_COLS, 128), bf16),
            pltpu.VMEM((2, 2, 3, EXT_COLS, 128), bf16),
            pltpu.VMEM((2, 2, ROWS, 8, 128), f32),
            pltpu.VMEM((2, 2, EXT_ROWS, 8, 128), f32),
            sem((2,)),
            sem((2, 2)),
            sem((2, 2)),
            sem((2, 2, 3)),
            sem((2, 2, 3)),
            sem((N_GROUP,)),
            sem((N_GROUP,)),
            sem((N_GROUP,)),
            sem((N_GROUP,)),
            sem((N_GROUP,)),
            sem((N_GROUP,)),
        ],
        compiler_params=pltpu.CompilerParams(
            collective_id=0, has_side_effects=True, vmem_limit_bytes=48 * 2**20
        ),
    )(state, cotangent, land_sea, prm, be, w_expand, w_project)
    tap_rows = jnp.concatenate([small[0:25, 0:64], small[0:24, 64:128]], axis=0)
    kernel_grad = tap_rows.T.reshape(CHAN, TAPS, TAPS)
    return (
        grad,
        kernel_grad,
        small[27, 0:64],
        small[27, 64:128],
        small[28, 0:64],
        expand,
        small[25:27].reshape(EXPAND),
        project,
        small[28, 64:128],
    )


def solution(mesh):
    in_specs = (
        P(None, "lat", "lon"),
        P("lat", "lon"),
        P(None, "lat", "lon"),
        P(),
        P(),
        P(),
        P(),
        P(),
        P(),
        P(),
    )
    out_specs = (P(None, "lat", "lon"), P(), P(), P(), P(), P(), P(), P(), P())
    return jax.shard_map(body, mesh=mesh, in_specs=in_specs, out_specs=out_specs, check_vma=False)
```

```python
import math

import jax
import jax.numpy as jnp
from jax import lax
from jax.experimental import pallas as pl
from jax.experimental.pallas import tpu as pltpu
from jax.sharding import PartitionSpec as P

TAPS = 7
CHAN = 64
EXPAND = 256
ROWS = 8
COLS = 270
HALF = 135
PITCH = 136
TILES = 17
CELLS = ROWS * PITCH
EXT_ROWS = 14
EXT_COLS = 144
STEP = 272
N_GROUP = 16
MESH = pl.DeviceIdType.MESH

ln_eps = 1e-06
root_half = 0.7071067811865476
inv_root_tau = 0.3989422804014327
half_log2e = -0.7213475204444817

f32 = jnp.float32
bf16 = jnp.bfloat16


def dot(a, b, dims):
    return lax.dot_general(a, b, (dims, ((), ())), preferred_element_type=f32)


NN = ((1,), (0,))
NT = ((1,), (1,))
TN = ((0,), (0,))


def split(x):
    hi = x.astype(bf16)
    lo = (x - hi.astype(f32)).astype(bf16)
    return jnp.concatenate([hi, lo], axis=1)


def kernel_body(
    state_hbm,
    cot_hbm,
    land_hbm,
    kern_hbm,
    cb_hbm,
    gain_hbm,
    lb_hbm,
    we_hbm,
    be_hbm,
    wp_hbm,
    grad_ref,
    big_ref,
    small_ref,
    state_in,
    cot_in,
    land_ref,
    kern_ref,
    cb_ref,
    gain_ref,
    lb_ref,
    we_ref,
    be_ref,
    wp_ref,
    planes,
    turned,
    s_ext,
    d_ext,
    wet32,
    wet16,
    x_ref,
    norm_ref,
    rstd_ref,
    zed_ref,
    pre_ref,
    dact_ref,
    act_ref,
    dhid_ref,
    taps_ref,
    wbd,
    wpbd,
    mean_ref,
    mean2_ref,
    eg_ref,
    pg_ref,
    acc_ref,
    tap_out,
    pay_b,
    part_b,
    gather_b,
    pay_s,
    part_s,
    gather_s,
    row_send,
    row_recv,
    col_send,
    col_recv,
    in_sem,
    row_ssem,
    row_rsem,
    col_ssem,
    col_rsem,
    sb1,
    rb1,
    sb2,
    rb2,
    sb3,
    rb3,
    ss1,
    rs1,
    ss2,
    rs2,
    ss3,
    rs3,
):
    la = lax.axis_index("lat")
    lo = lax.axis_index("lon")
    east = lax.rem(lo + 1, N_GROUP)
    west = lax.rem(lo + N_GROUP - 1, N_GROUP)
    has_north = la > 0
    has_south = la < N_GROUP - 1

    inputs = [
        pltpu.make_async_copy(src, dst, in_sem.at[i])
        for i, (src, dst) in enumerate(
            (
                (state_hbm, state_in),
                (cot_hbm, cot_in),
                (land_hbm, land_ref),
                (kern_hbm, kern_ref),
                (cb_hbm, cb_ref),
                (gain_hbm, gain_ref),
                (lb_hbm, lb_ref),
                (we_hbm, we_ref),
                (be_hbm, be_ref),
                (wp_hbm, wp_ref),
            )
        )
    ]
    for copy in inputs:
        copy.start()

    def lat_peer(k):
        return {"lat": lax.rem(la + k, N_GROUP), "lon": lo}

    def lon_peer(k):
        return {"lat": la, "lon": lax.rem(lo + k, N_GROUP)}

    barrier = pltpu.get_barrier_semaphore()
    for k in range(1, N_GROUP):
        pl.semaphore_signal(barrier, inc=1, device_id=lat_peer(k), device_id_type=MESH)
        pl.semaphore_signal(barrier, inc=1, device_id=lon_peer(k), device_id_type=MESH)
    for side in (east, west):

        @pl.when(has_north)
        def _():
            pl.semaphore_signal(
                barrier, inc=1, device_id={"lat": la - 1, "lon": side}, device_id_type=MESH
            )

        @pl.when(has_south)
        def _():
            pl.semaphore_signal(
                barrier, inc=1, device_id={"lat": la + 1, "lon": side}, device_id_type=MESH
            )

    lane = lax.broadcasted_iota(jnp.int32, (ROWS, 8, 128), 2)
    sub = lax.broadcasted_iota(jnp.int32, (ROWS, 8, 128), 1)

    s_ext[:, 136:144, :] = jnp.zeros((EXT_ROWS, 8, 128), f32)
    d_ext[:, 136:144, :] = jnp.zeros((EXT_ROWS, 8, 128), f32)
    for ref in (s_ext, d_ext):

        @pl.when(jnp.logical_not(has_north))
        def _():
            ref[0:3] = jnp.zeros((3, EXT_COLS, 128), f32)

        @pl.when(jnp.logical_not(has_south))
        def _():
            ref[11:14] = jnp.zeros((3, EXT_COLS, 128), f32)

    planes[2] = jnp.zeros((CHAN * ROWS, 128), f32)

    def to_planes(load):
        def step(i, carry):
            at = pl.ds(pl.multiple_of(i * 8, 8), 8)
            x = load(at)
            to = pl.ds(pl.multiple_of(i * 64, 64), 64)
            planes[0, to, :] = x[:, :, 0:128].reshape(64, 128)
            planes[1, to, :] = x[:, :, 128:256].reshape(64, 128)
            planes[2, to, 0:14] = x[:, :, 256:270].reshape(64, 14)
            return carry

        lax.fori_loop(0, 8, step, 0)

    half_lane = lax.broadcasted_iota(jnp.int32, (PITCH, 128), 1) < 64

    def turn_in(put):
        def step(p, carry):
            r = p * 2
            for k in range(3):
                both = jnp.concatenate(
                    [
                        planes[k, pl.ds(r, CHAN, stride=ROWS), :],
                        planes[k, pl.ds(r + 1, CHAN, stride=ROWS), :],
                    ],
                    axis=0,
                )
                turned[128 * k : 128 * k + 128, :] = both.T
            h0 = turned[0:PITCH, :]
            h1 = turned[HALF : HALF + PITCH, :]
            put(r, jnp.where(half_lane, h0, pltpu.roll(h1, 64, axis=1)))
            put(r + 1, jnp.where(half_lane, pltpu.roll(h0, 64, axis=1), h1))
            return carry

        lax.fori_loop(0, ROWS // 2, step, 0)

    def exchange(ext, n):
        to_east = pltpu.roll(ext[3:11, 135:143, :], 64, axis=2)
        to_west = pltpu.roll(ext[3:11, 1:9, :], 64, axis=2)
        col_send[n, 0] = to_east
        col_send[n, 1] = to_west
        ext[3:11, 0:8, :] = jnp.where((sub < 3) & (lane >= 64), to_east, ext[3:11, 0:8, :])
        ext[3:11, 136:144, :] = jnp.where(
            (sub >= 2) & (sub < 5) & (lane < 64), to_west, ext[3:11, 136:144, :]
        )
        row_send[n, 0] = ext[3:6].astype(bf16)
        row_send[n, 1] = ext[8:11].astype(bf16)

    def rows_copy(n, way):
        return pltpu.make_async_remote_copy(
            src_ref=row_send.at[n, way],
            dst_ref=row_recv.at[n, way],
            send_sem=row_ssem.at[n, way],
            recv_sem=row_rsem.at[n, way],
            device_id={"lat": la - 1 + 2 * way, "lon": lo},
            device_id_type=MESH,
        )

    def cols_copy(n, way, turn):
        src = col_send.at[n, way]
        dst = col_recv.at[n, way]
        if turn == 1:
            src, dst = src.at[0:3], dst.at[11:14]
        elif turn == 2:
            src, dst = src.at[5:8], dst.at[0:3]
        else:
            dst = dst.at[3:11]
        return pltpu.make_async_remote_copy(
            src_ref=src,
            dst_ref=dst,
            send_sem=col_ssem.at[n, way, turn],
            recv_sem=col_rsem.at[n, way, turn],
            device_id={
                "lat": la + (0, -1, 1)[turn],
                "lon": (east, west)[way],
            },
            device_id_type=MESH,
        )

    def start_copies(n):
        @pl.when(has_north)
        def _():
            rows_copy(n, 0).start()
            cols_copy(n, 0, 1).start()
            cols_copy(n, 1, 1).start()

        @pl.when(has_south)
        def _():
            rows_copy(n, 1).start()
            cols_copy(n, 0, 2).start()
            cols_copy(n, 1, 2).start()

        cols_copy(n, 0, 0).start()
        cols_copy(n, 1, 0).start()

    def finish_copies(ext, n):
        @pl.when(has_north)
        def _():
            rows_copy(n, 0).wait_send()
            cols_copy(n, 0, 1).wait_send()
            cols_copy(n, 1, 1).wait_send()
            rows_copy(n, 1).wait_recv()
            cols_copy(n, 0, 2).wait_recv()
            cols_copy(n, 1, 2).wait_recv()
            ext[0:3] = row_recv[n, 1].astype(f32)

        @pl.when(has_south)
        def _():
            rows_copy(n, 1).wait_send()
            cols_copy(n, 0, 2).wait_send()
            cols_copy(n, 1, 2).wait_send()
            rows_copy(n, 0).wait_recv()
            cols_copy(n, 0, 1).wait_recv()
            cols_copy(n, 1, 1).wait_recv()
            ext[11:14] = row_recv[n, 0].astype(f32)

        cols_copy(n, 0, 0).wait()
        cols_copy(n, 1, 0).wait()

        def fill(first, last):
            from_west = col_recv[n, 0, first:last]
            from_east = col_recv[n, 1, first:last]
            m = last - first
            ext[first:last, 0:8, :] = jnp.where(
                (sub[:m] < 3) & (lane[:m] < 64), from_west, ext[first:last, 0:8, :]
            )
            ext[first:last, 136:144, :] = jnp.where(
                (sub[:m] >= 2) & (sub[:m] < 5) & (lane[:m] >= 64),
                from_east,
                ext[first:last, 136:144, :],
            )

        fill(3, 11)

        @pl.when(has_north)
        def _():
            fill(0, 3)

        @pl.when(has_south)
        def _():
            fill(11, 14)

    def convolve(ext, flip, bias):
        def step(t, carry):
            at = pl.multiple_of(t * 8, 8)
            acc = jnp.zeros((ROWS, 8, 128), f32)
            if bias is not None:
                acc = acc + bias[None]
            for b in range(TAPS):
                x = ext[:, pl.ds(at + b, 8), :]
                for a in range(TAPS):
                    i = a * TAPS + b
                    acc = acc + taps_ref[48 - i if flip else i][None] * x[a : a + ROWS]
            for r in range(ROWS):
                x_ref[pl.ds(at + r * PITCH, 8), :] = acc[r]
            return carry

        lax.fori_loop(0, TILES, step, 0)

    inputs[0].wait()
    to_planes(lambda at: state_in[at].astype(f32))

    def put_state(r, value):
        s_ext[r + 3, 3 : 3 + PITCH, :] = value

    turn_in(put_state)
    exchange(s_ext, 0)
    pl.semaphore_wait(
        barrier,
        2 * (N_GROUP - 1)
        + 2 * has_north.astype(jnp.int32)
        + 2 * has_south.astype(jnp.int32),
    )
    start_copies(0)

    inputs[1].wait()
    inputs[2].wait()
    land = land_ref[...].astype(f32)
    to_planes(lambda at: cot_in[at].astype(f32) * land[None])

    def put_wet(r, value):
        wet32[pl.ds(pl.multiple_of(r * PITCH, 8), PITCH), :] = value
        wet32[pl.ds(r * PITCH + HALF, 1), :] = jnp.zeros((1, 128), f32)

    turn_in(put_wet)
    acc_ref[...] = jnp.zeros((5, 8, 512), f32)

    def narrow(i, carry):
        at = pl.ds(pl.multiple_of(i * 16, 16), 16)
        w = wet32[at, :]
        wet16[at, :] = w.astype(bf16)
        return carry + w[0:8] + w[8:16]

    acc_ref[0, :, 0:128] = lax.fori_loop(0, CELLS // 16, narrow, jnp.zeros((8, 128), f32))

    for copy in inputs[3:]:
        copy.wait()
    for a in range(TAPS):
        for b in range(TAPS):
            one = kern_ref[a, b : b + 1, :]
            taps_ref[a * TAPS + b] = jnp.broadcast_to(
                jnp.concatenate([one, one], axis=1), (8, 128)
            )
    wbd[...] = jnp.zeros((128, 512), bf16)
    wbd[0:64, 0:256] = we_ref[...]
    wbd[64:128, 256:512] = we_ref[...]
    wpbd[...] = jnp.zeros((128, 512), bf16)
    wpbd[0:64, 0:256] = wp_ref[...]
    wpbd[64:128, 256:512] = wp_ref[...]
    at_row = lax.broadcasted_iota(jnp.int32, (256, 256), 0) // 64
    at_col = lax.broadcasted_iota(jnp.int32, (256, 256), 1) // 64
    mean2_ref[...] = jnp.where(at_row == at_col, 1.0 / CHAN, 0.0).astype(bf16)
    mean_ref[0:128, :] = mean2_ref[0:128, 0:128]
    mean_ref[128:256, :] = mean2_ref[0:128, 0:128]

    def twice(ref):
        return jnp.concatenate([ref[...], ref[...]], axis=1)

    conv_bias = twice(cb_ref)
    gain = twice(gain_ref)
    ln_bias = twice(lb_ref)
    be = twice(be_ref)

    finish_copies(s_ext, 0)
    convolve(s_ext, False, conv_bias)

    def fold(x):
        return jnp.sum(x.reshape(-1, 8, x.shape[-1]), axis=0)

    def pointwise(q, carry):
        at = pl.ds(pl.multiple_of(q * STEP, STEP), STEP)
        x = x_ref[at, :]
        cen = x - dot(split(x), mean_ref[...], NN)
        var = dot((cen * cen).astype(bf16), mean_ref[0:128, :], NN)
        rstd = lax.rsqrt(var + ln_eps)
        normed = cen * rstd
        zed = (normed * gain + ln_bias).astype(bf16)
        norm_ref[...] = normed
        rstd_ref[...] = rstd
        zed_ref[at, :] = zed
        pre_ref[...] = dot(zed, wbd[...], NN)
        dact_ref[...] = dot(wet16[at, :], wpbd[...], NN)

        def gelu(i, total):
            rows = pl.ds(pl.multiple_of(i * 16, 16), 16)
            to = pl.ds(pl.multiple_of(q * STEP + i * 16, 16), 16)
            for k in range(4):
                cols = slice(128 * k, 128 * k + 128)
                pre = pre_ref[rows, cols] + be[:, cols]
                grow = jnp.exp2(pre * pre * half_log2e)
                t = 1.0 / (1.0 + (0.3275911 * root_half) * jnp.abs(pre))
                poly = 0.5 * 1.061405429 * t - 0.5 * 1.453152027
                poly = poly * t + 0.5 * 1.421413741
                poly = poly * t - 0.5 * 0.284496736
                poly = poly * t + 0.5 * 0.254829592
                tail = poly * t * grow
                phi = jnp.where(pre >= 0, 1.0 - tail, tail)
                slope = phi + pre * grow * inv_root_tau
                act_ref[to, cols] = (pre * phi).astype(bf16)
                dhid = (dact_ref[rows, cols] * slope).astype(bf16)
                dhid_ref[to, cols] = dhid
                wide = dhid.astype(f32)
                acc_ref[1, :, cols] += wide[0:8] + wide[8:16]
            return total

        lax.fori_loop(0, STEP // 16, gelu, 0)
        dzed = dot(dhid_ref[at, :], wbd[...], NT)
        normed = norm_ref[...]
        acc_ref[2, :, 0:128] += fold(dzed * normed)
        acc_ref[3, :, 0:128] += fold(dzed)
        dnorm = dzed * gain
        both = jnp.concatenate([dnorm.astype(bf16), (dnorm * normed).astype(bf16)], axis=1)
        means = dot(both, mean2_ref[...], NN)
        dconv = rstd_ref[...] * (dnorm - means[:, 0:128] - normed * means[:, 128:256])
        x_ref[at, :] = dconv
        acc_ref[4, :, 0:128] += fold(dconv)
        return carry

    lax.fori_loop(0, CELLS // STEP, pointwise, 0)
    eg_ref[...] = dot(zed_ref[...], dhid_ref[...], TN)
    pg_ref[...] = dot(wet16[...], act_ref[...], TN)

    def halves(x):
        return x + pltpu.roll(x, 64, axis=1)

    for i in range(N_GROUP):
        c, e = 8 * (i // 2), 128 * (i % 2)
        one, two = [
            ref[c : c + 8, e : e + 128] + ref[64 + c : 72 + c, 256 + e : 384 + e]
            for ref in (eg_ref, pg_ref)
        ]
        pay_b[i] = jnp.concatenate([one, two], axis=0).astype(bf16)

    def scatter(pay, part, ssem, rsem):
        copies = []
        for k in range(1, N_GROUP):
            copies.append(
                pltpu.make_async_remote_copy(
                    src_ref=pay.at[lax.rem(la + k, N_GROUP)],
                    dst_ref=part.at[k],
                    send_sem=ssem.at[k],
                    recv_sem=rsem.at[k],
                    device_id=lat_peer(k),
                    device_id_type=MESH,
                )
            )
            copies[-1].start()
        return copies

    def spread(ref, at, peer, ssem, rsem):
        copies = []
        for k in range(1, N_GROUP):
            copies.append(
                pltpu.make_async_remote_copy(
                    src_ref=ref.at[at],
                    dst_ref=ref.at[at],
                    send_sem=ssem.at[k],
                    recv_sem=rsem.at[k],
                    device_id=peer(k),
                    device_id_type=MESH,
                )
            )
            copies[-1].start()
        return copies

    def scattered(pay, part, gather, copies):
        total = pay[la].astype(f32)
        for k in range(1, N_GROUP):
            copies[k - 1].wait()
            total = total + part[k].astype(f32)
        gather[lo] = total.astype(gather.dtype)

    scale = 1.0 / math.sqrt(ROWS * N_GROUP * COLS * N_GROUP)

    def gathered(gather, out, copies):
        for copy in copies:
            copy.wait()
        total = gather[0].astype(f32)
        for k in range(1, N_GROUP):
            total = total + gather[k].astype(f32)
        out[la] = (total * scale).astype(out.dtype)

    copies_b = scatter(pay_b, part_b, sb1, rb1)

    def place(r, carry):
        d_ext[r + 3, 3 : 3 + PITCH, :] = x_ref[pl.ds(pl.multiple_of(r * PITCH, 8), PITCH), :]
        return carry

    lax.fori_loop(0, ROWS, place, 0)
    exchange(d_ext, 1)
    start_copies(1)

    for b in range(TAPS):

        def tap_step(t, acc):
            at = pl.multiple_of(t * 8, 8)
            x = s_ext[:, pl.ds(at + b, 8), :]
            d = [x_ref[pl.ds(at + r * PITCH, 8), :] for r in range(ROWS)]
            new = []
            for a in range(TAPS):
                s = acc[a]
                for r in range(ROWS):
                    s = s + d[r] * x[r + a]
                new.append(s)
            return tuple(new)

        zero = jnp.zeros((8, 128), f32)
        acc = lax.fori_loop(0, TILES, tap_step, (zero,) * TAPS)
        for a in range(TAPS):
            tap_out[a * TAPS + b] = acc[a]

    first_half = lax.broadcasted_iota(jnp.int32, (1, 128), 1) < 64

    def sums_of(x):
        return halves(jnp.sum(x, axis=0, keepdims=True))

    rows = []
    for i in range(25):
        one = sums_of(tap_out[i])
        two = sums_of(tap_out[25 + i]) if i < 24 else jnp.zeros((1, 128), f32)
        rows.append(jnp.where(first_half, one, two))
    wide = jnp.sum(acc_ref[1], axis=0, keepdims=True)
    wide = wide[:, 0:256] + wide[:, 256:512]
    rows.append(wide[:, 0:128])
    rows.append(wide[:, 128:256])
    rows.append(
        jnp.where(first_half, sums_of(acc_ref[4, :, 0:128]), sums_of(acc_ref[2, :, 0:128]))
    )
    rows.append(
        jnp.where(first_half, sums_of(acc_ref[3, :, 0:128]), sums_of(acc_ref[0, :, 0:128]))
    )
    while len(rows) < 32:
        rows.append(jnp.zeros((1, 128), f32))
    for i in range(N_GROUP):
        pay_s[i, 0:1, :] = rows[2 * i]
        pay_s[i, 1:2, :] = rows[2 * i + 1]

    copies_s = scatter(pay_s, part_s, ss1, rs1)
    scattered(pay_b, part_b, gather_b, copies_b)
    copies_b = spread(gather_b, lo, lon_peer, sb2, rb2)

    finish_copies(d_ext, 1)
    convolve(d_ext, True, None)

    scattered(pay_s, part_s, gather_s, copies_s)
    copies_s = spread(gather_s, lo, lon_peer, ss2, rs2)

    def turn_out(p, carry):
        r = p * 2
        g0 = x_ref[pl.ds(pl.multiple_of(r * PITCH, 8), PITCH), :]
        g1 = x_ref[pl.ds(pl.multiple_of(r * PITCH + PITCH, 8), PITCH), :]
        turned[0:PITCH, :] = jnp.where(half_lane, g0, pltpu.roll(g1, 64, axis=1))
        turned[HALF : HALF + PITCH, :] = jnp.where(half_lane, pltpu.roll(g0, 64, axis=1), g1)
        for k in range(3):
            back = turned[128 * k : 128 * k + 128, :].T
            planes[k, pl.ds(r, CHAN, stride=ROWS), :] = back[0:64]
            planes[k, pl.ds(r + 1, CHAN, stride=ROWS), :] = back[64:128]
        return carry

    lax.fori_loop(0, ROWS // 2, turn_out, 0)

    def write_out(i, carry):
        at = pl.ds(pl.multiple_of(i * 8, 8), 8)
        of = pl.ds(pl.multiple_of(i * 64, 64), 64)
        for k in range(3):
            cols = slice(128 * k, min(128 * k + 128, COLS))
            width = cols.stop - cols.start
            value = planes[k, of, 0:width].reshape(8, 8, width)
            grad_ref[at, :, cols] = (cot_in[at, :, cols].astype(f32) + value).astype(bf16)
        return carry

    lax.fori_loop(0, 8, write_out, 0)

    gathered(gather_b, big_ref, copies_b)
    copies_b = spread(big_ref, la, lat_peer, sb3, rb3)
    gathered(gather_s, small_ref, copies_s)
    copies_s = spread(small_ref, la, lat_peer, ss3, rs3)
    for copy in copies_b + copies_s:
        copy.wait()


def finish(
    grad_ref,
    big_ref,
    small_ref,
    grad_hbm,
    kern_out,
    cb_out,
    gain_out,
    lb_out,
    expand_out,
    be_out,
    project_out,
    bp_out,
    rows_ref,
    sem,
):
    copy = pltpu.make_async_copy(grad_ref, grad_hbm, sem)
    copy.start()
    for i in range(N_GROUP):
        c, e = 8 * (i // 2), 128 * (i % 2)
        both = big_ref[i].astype(f32)
        expand_out[c : c + 8, e : e + 128] = both[0:8]
        project_out[c : c + 8, e : e + 128] = both[8:16]
    for i in range(N_GROUP):
        rows_ref[2 * i : 2 * i + 2, :] = small_ref[i]
    be_out[:, 0:128] = rows_ref[25:26, :]
    be_out[:, 128:256] = rows_ref[26:27, :]
    cb_out[...] = rows_ref[27:28, 0:64]
    gain_out[...] = pltpu.roll(rows_ref[27:28, :], 64, axis=1)[:, 0:64]
    lb_out[...] = rows_ref[28:29, 0:64]
    bp_out[...] = pltpu.roll(rows_ref[28:29, :], 64, axis=1)[:, 0:64]
    rows = rows_ref[0:32, :]
    turned = pltpu.roll(rows, 64, axis=1)
    for i in range(TAPS * TAPS):
        a, b = i // TAPS, i % TAPS
        of, at = (rows, i) if i < 25 else (turned, i - 25)
        kern_out[a, b : b + 1, :] = of[at : at + 1, 0:64]
    copy.wait()


def far(x):
    return pltpu.with_memory_space_constraint(x, pltpu.HBM)


def body(
    state, land_sea, cotangent, kernel, conv_bias, ln_gain, ln_bias, w_expand, b_expand, w_project
):
    vmem = pl.BlockSpec(memory_space=pltpu.VMEM)
    hbm = pl.BlockSpec(memory_space=pltpu.HBM)
    sds = jax.ShapeDtypeStruct
    sem = pltpu.SemaphoreType.DMA
    big = (N_GROUP, 16, 128)
    small = (N_GROUP, 2, 128)
    grad, big_sums, small_sums = pl.pallas_call(
        kernel_body,
        out_shape=(
            sds((CHAN, ROWS, COLS), bf16),
            sds(big, bf16),
            sds(small, f32),
        ),
        in_specs=[hbm] * 10,
        out_specs=(vmem, vmem, vmem),
        scratch_shapes=[
            pltpu.VMEM((CHAN, ROWS, COLS), bf16),
            pltpu.VMEM((CHAN, ROWS, COLS), bf16),
            pltpu.VMEM((ROWS, COLS), jnp.int32),
            pltpu.VMEM((TAPS, TAPS, CHAN), f32),
            pltpu.VMEM((1, CHAN), f32),
            pltpu.VMEM((1, CHAN), f32),
            pltpu.VMEM((1, CHAN), f32),
            pltpu.VMEM((CHAN, EXPAND), bf16),
            pltpu.VMEM((1, EXPAND), f32),
            pltpu.VMEM((CHAN, EXPAND), bf16),
            pltpu.VMEM((3, CHAN * ROWS, 128), f32),
            pltpu.VMEM((384, 128), f32),
            pltpu.VMEM((EXT_ROWS, EXT_COLS, 128), f32),
            pltpu.VMEM((EXT_ROWS, EXT_COLS, 128), f32),
            pltpu.VMEM((CELLS, 128), f32),
            pltpu.VMEM((CELLS, 128), bf16),
            pltpu.VMEM((CELLS, 128), f32),
            pltpu.VMEM((STEP, 128), f32),
            pltpu.VMEM((STEP, 128), f32),
            pltpu.VMEM((CELLS, 128), bf16),
            pltpu.VMEM((STEP, 512), f32),
            pltpu.VMEM((STEP, 512), f32),
            pltpu.VMEM((CELLS, 512), bf16),
            pltpu.VMEM((CELLS, 512), bf16),
            pltpu.VMEM((TAPS * TAPS, 8, 128), f32),
            pltpu.VMEM((128, 512), bf16),
            pltpu.VMEM((128, 512), bf16),
            pltpu.VMEM((256, 128), bf16),
            pltpu.VMEM((256, 256), bf16),
            pltpu.VMEM((128, 512), f32),
            pltpu.VMEM((128, 512), f32),
            pltpu.VMEM((5, 8, 512), f32),
            pltpu.VMEM((TAPS * TAPS, 8, 128), f32),
            pltpu.VMEM(big, bf16),
            pltpu.VMEM(big, bf16),
            pltpu.VMEM(big, bf16),
            pltpu.VMEM(small, f32),
            pltpu.VMEM(small, f32),
            pltpu.VMEM(small, f32),
            pltpu.VMEM((2, 2, 3, EXT_COLS, 128), bf16),
            pltpu.VMEM((2, 2, 3, EXT_COLS, 128), bf16),
            pltpu.VMEM((2, 2, ROWS, 8, 128), f32),
            pltpu.VMEM((2, 2, EXT_ROWS, 8, 128), f32),
            sem((10,)),
            sem((2, 2)),
            sem((2, 2)),
            sem((2, 2, 3)),
            sem((2, 2, 3)),
        ]
        + [sem((N_GROUP,))] * 12,
        compiler_params=pltpu.CompilerParams(
            collective_id=0, has_side_effects=True, vmem_limit_bytes=48 * 2**20
        ),
    )(
        *map(
            far,
            (
                state,
                cotangent,
                land_sea,
                kernel.transpose(1, 2, 0),
                conv_bias[None],
                ln_gain[None],
                ln_bias[None],
                w_expand,
                b_expand[None],
                w_project.T,
            ),
        )
    )
    outs = pl.pallas_call(
        finish,
        out_shape=(
            sds((CHAN, ROWS, COLS), bf16),
            sds((TAPS, TAPS, CHAN), f32),
            sds((1, CHAN), f32),
            sds((1, CHAN), f32),
            sds((1, CHAN), f32),
            sds((CHAN, EXPAND), f32),
            sds((1, EXPAND), f32),
            sds((CHAN, EXPAND), f32),
            sds((1, CHAN), f32),
        ),
        in_specs=[vmem] * 3,
        out_specs=(hbm,) + (vmem,) * 8,
        scratch_shapes=[
            pltpu.VMEM((32, 128), f32),
            sem(()),
        ],
        compiler_params=pltpu.CompilerParams(vmem_limit_bytes=8 * 2**20),
    )(grad, big_sums, small_sums)
    outs = list(outs)
    outs[1] = outs[1].transpose(2, 0, 1)
    outs[7] = outs[7].T
    for i in (2, 3, 4, 6, 8):
        outs[i] = outs[i].reshape(-1)
    return tuple(outs)


def solution(mesh):
    in_specs = (
        P(None, "lat", "lon"),
        P("lat", "lon"),
        P(None, "lat", "lon"),
        P(),
        P(),
        P(),
        P(),
        P(),
        P(),
        P(),
    )
    out_specs = (P(None, "lat", "lon"), P(), P(), P(), P(), P(), P(), P(), P())
    return jax.shard_map(body, mesh=mesh, in_specs=in_specs, out_specs=out_specs, check_vma=False)
```

```python
import math

import jax
import jax.numpy as jnp
from jax import lax
from jax.experimental import pallas as pl
from jax.experimental.pallas import tpu as pltpu
from jax.sharding import PartitionSpec as P

TAPS = 7
CHAN = 64
EXPAND = 256
ROWS = 8
COLS = 270
HALF = 135
PITCH = 136
TILES = 17
CELLS = ROWS * PITCH
EXT_ROWS = 14
EXT_COLS = 144
STEP = 272
PART = 544
GROUP = 32
BACK = 544
N_GROUP = 16
MESH = pl.DeviceIdType.MESH

ln_eps = 1e-06
root_half = 0.7071067811865476
inv_root_tau = 0.3989422804014327
half_log2e = -0.7213475204444817

f32 = jnp.float32
bf16 = jnp.bfloat16


def dot(a, b, dims):
    return lax.dot_general(a, b, (dims, ((), ())), preferred_element_type=f32)


NN = ((1,), (0,))
NT = ((1,), (1,))
TN = ((0,), (0,))


def split(x):
    hi = x.astype(bf16)
    lo = (x - hi.astype(f32)).astype(bf16)
    return jnp.concatenate([hi, lo], axis=1)


def kernel_body(
    state_hbm,
    cot_hbm,
    land_hbm,
    kern_hbm,
    cb_hbm,
    gain_hbm,
    lb_hbm,
    we_hbm,
    be_hbm,
    wp_hbm,
    grad_ref,
    big_ref,
    small_ref,
    state_in,
    cot_in,
    land_ref,
    kern_ref,
    cb_ref,
    gain_ref,
    lb_ref,
    we_ref,
    be_ref,
    wp_ref,
    planes,
    turned,
    s_ext,
    d_ext,
    wet32,
    wet16,
    x_ref,
    norm_ref,
    rstd_ref,
    zed_ref,
    pre_ref,
    dact_ref,
    act_ref,
    dhid_ref,
    taps_ref,
    wbd,
    wpbd,
    mean_ref,
    mean2_ref,
    eg_ref,
    pg_ref,
    acc_ref,
    tap_out,
    pay_b,
    part_b,
    gather_b,
    pay_s,
    part_s,
    gather_s,
    row_send,
    row_recv,
    col_send,
    col_recv,
    hello_sem,
    in_sem,
    row_ssem,
    row_rsem,
    col_ssem,
    col_rsem,
    sb1,
    rb1,
    sb2,
    rb2,
    sb3,
    rb3,
    ss1,
    rs1,
    ss2,
    rs2,
    ss3,
    rs3,
):
    la = lax.axis_index("lat")
    lo = lax.axis_index("lon")
    east = lax.rem(lo + 1, N_GROUP)
    west = lax.rem(lo + N_GROUP - 1, N_GROUP)
    has_north = la > 0
    has_south = la < N_GROUP - 1

    inputs = [
        pltpu.make_async_copy(src, dst, in_sem.at[i])
        for i, (src, dst) in enumerate(
            (
                (state_hbm, state_in),
                (cot_hbm, cot_in),
                (land_hbm, land_ref),
                (kern_hbm, kern_ref),
                (cb_hbm, cb_ref),
                (gain_hbm, gain_ref),
                (lb_hbm, lb_ref),
                (we_hbm, we_ref),
                (be_hbm, be_ref),
                (wp_hbm, wp_ref),
            )
        )
    ]
    for copy in inputs:
        copy.start()

    def lat_peer(k):
        return {"lat": lax.rem(la + k, N_GROUP), "lon": lo}

    def lon_peer(k):
        return {"lat": la, "lon": lax.rem(lo + k, N_GROUP)}

    barrier = pltpu.get_barrier_semaphore()
    for k in (1, N_GROUP - 1):
        pl.semaphore_signal(barrier, inc=1, device_id=lat_peer(k), device_id_type=MESH)
        pl.semaphore_signal(barrier, inc=1, device_id=lon_peer(k), device_id_type=MESH)
    for side in (east, west):

        @pl.when(has_north)
        def _():
            pl.semaphore_signal(
                barrier, inc=1, device_id={"lat": la - 1, "lon": side}, device_id_type=MESH
            )

        @pl.when(has_south)
        def _():
            pl.semaphore_signal(
                barrier, inc=1, device_id={"lat": la + 1, "lon": side}, device_id_type=MESH
            )

    def hello(n):
        for k in (2**n, N_GROUP - 2**n):
            pl.semaphore_signal(
                hello_sem.at[0, n], inc=1, device_id=lat_peer(k), device_id_type=MESH
            )
            pl.semaphore_signal(
                hello_sem.at[1, n], inc=1, device_id=lon_peer(k), device_id_type=MESH
            )

    def heard(n):
        pl.semaphore_wait(hello_sem.at[0, n], 2)
        pl.semaphore_wait(hello_sem.at[1, n], 2)

    lane = lax.broadcasted_iota(jnp.int32, (ROWS, 8, 128), 2)
    sub = lax.broadcasted_iota(jnp.int32, (ROWS, 8, 128), 1)

    s_ext[:, 136:144, :] = jnp.zeros((EXT_ROWS, 8, 128), f32)
    d_ext[:, 136:144, :] = jnp.zeros((EXT_ROWS, 8, 128), f32)
    for ref in (s_ext, d_ext):

        @pl.when(jnp.logical_not(has_north))
        def _():
            ref[0:3] = jnp.zeros((3, EXT_COLS, 128), f32)

        @pl.when(jnp.logical_not(has_south))
        def _():
            ref[11:14] = jnp.zeros((3, EXT_COLS, 128), f32)

    planes[2] = jnp.zeros((CHAN * ROWS, 128), f32)

    def to_planes(load):
        def step(i, carry):
            at = pl.ds(pl.multiple_of(i * 8, 8), 8)
            x = load(at)
            to = pl.ds(pl.multiple_of(i * 64, 64), 64)
            planes[0, to, :] = x[:, :, 0:128].reshape(64, 128)
            planes[1, to, :] = x[:, :, 128:256].reshape(64, 128)
            planes[2, to, 0:14] = x[:, :, 256:270].reshape(64, 14)
            return carry

        lax.fori_loop(0, 8, step, 0)

    half_lane = lax.broadcasted_iota(jnp.int32, (PITCH, 128), 1) < 64

    def turn_in(put):
        def step(p, carry):
            r = p * 2
            for k in range(3):
                both = jnp.concatenate(
                    [
                        planes[k, pl.ds(r, CHAN, stride=ROWS), :],
                        planes[k, pl.ds(r + 1, CHAN, stride=ROWS), :],
                    ],
                    axis=0,
                )
                turned[128 * k : 128 * k + 128, :] = both.T
            h0 = turned[0:PITCH, :]
            h1 = turned[HALF : HALF + PITCH, :]
            put(r, jnp.where(half_lane, h0, pltpu.roll(h1, 64, axis=1)))
            put(r + 1, jnp.where(half_lane, pltpu.roll(h0, 64, axis=1), h1))
            return carry

        lax.fori_loop(0, ROWS // 2, step, 0)

    def exchange(ext, n):
        to_east = pltpu.roll(ext[3:11, 135:143, :], 64, axis=2)
        to_west = pltpu.roll(ext[3:11, 1:9, :], 64, axis=2)
        col_send[n, 0] = to_east
        col_send[n, 1] = to_west
        ext[3:11, 0:8, :] = jnp.where((sub < 3) & (lane >= 64), to_east, ext[3:11, 0:8, :])
        ext[3:11, 136:144, :] = jnp.where(
            (sub >= 2) & (sub < 5) & (lane < 64), to_west, ext[3:11, 136:144, :]
        )
        row_send[n, 0] = ext[3:6].astype(bf16)
        row_send[n, 1] = ext[8:11].astype(bf16)

    def rows_copy(n, way):
        return pltpu.make_async_remote_copy(
            src_ref=row_send.at[n, way],
            dst_ref=row_recv.at[n, way],
            send_sem=row_ssem.at[n, way],
            recv_sem=row_rsem.at[n, way],
            device_id={"lat": la - 1 + 2 * way, "lon": lo},
            device_id_type=MESH,
        )

    def cols_copy(n, way, turn):
        src = col_send.at[n, way]
        dst = col_recv.at[n, way]
        if turn == 1:
            src, dst = src.at[0:3], dst.at[11:14]
        elif turn == 2:
            src, dst = src.at[5:8], dst.at[0:3]
        else:
            dst = dst.at[3:11]
        return pltpu.make_async_remote_copy(
            src_ref=src,
            dst_ref=dst,
            send_sem=col_ssem.at[n, way, turn],
            recv_sem=col_rsem.at[n, way, turn],
            device_id={
                "lat": la + (0, -1, 1)[turn],
                "lon": (east, west)[way],
            },
            device_id_type=MESH,
        )

    def start_copies(n):
        @pl.when(has_north)
        def _():
            rows_copy(n, 0).start()
            cols_copy(n, 0, 1).start()
            cols_copy(n, 1, 1).start()

        @pl.when(has_south)
        def _():
            rows_copy(n, 1).start()
            cols_copy(n, 0, 2).start()
            cols_copy(n, 1, 2).start()

        cols_copy(n, 0, 0).start()
        cols_copy(n, 1, 0).start()

    def finish_copies(ext, n):
        @pl.when(has_north)
        def _():
            rows_copy(n, 0).wait_send()
            cols_copy(n, 0, 1).wait_send()
            cols_copy(n, 1, 1).wait_send()
            rows_copy(n, 1).wait_recv()
            cols_copy(n, 0, 2).wait_recv()
            cols_copy(n, 1, 2).wait_recv()
            ext[0:3] = row_recv[n, 1].astype(f32)

        @pl.when(has_south)
        def _():
            rows_copy(n, 1).wait_send()
            cols_copy(n, 0, 2).wait_send()
            cols_copy(n, 1, 2).wait_send()
            rows_copy(n, 0).wait_recv()
            cols_copy(n, 0, 1).wait_recv()
            cols_copy(n, 1, 1).wait_recv()
            ext[11:14] = row_recv[n, 0].astype(f32)

        cols_copy(n, 0, 0).wait()
        cols_copy(n, 1, 0).wait()

        def fill(first, last):
            from_west = col_recv[n, 0, first:last]
            from_east = col_recv[n, 1, first:last]
            m = last - first
            ext[first:last, 0:8, :] = jnp.where(
                (sub[:m] < 3) & (lane[:m] < 64), from_west, ext[first:last, 0:8, :]
            )
            ext[first:last, 136:144, :] = jnp.where(
                (sub[:m] >= 2) & (sub[:m] < 5) & (lane[:m] >= 64),
                from_east,
                ext[first:last, 136:144, :],
            )

        fill(3, 11)

        @pl.when(has_north)
        def _():
            fill(0, 3)

        @pl.when(has_south)
        def _():
            fill(11, 14)

    def convolve(ext, flip, bias, tiles, stride, part=0):
        def step(t, carry):
            at = pl.multiple_of(t * (8 * stride) + 8 * (stride == 1), 8)
            if part == 2:
                acc = [x_ref[pl.ds(at + r * PITCH, 8), :] for r in range(ROWS)]
            else:
                first = jnp.zeros((8, 128), f32)
                if bias is not None:
                    first = first + bias
                acc = [first] * ROWS
            for b in range(TAPS):
                rows = {
                    i: ext[i, pl.ds(at + b, 8), :]
                    for i in range(EXT_ROWS)
                    if part == 0 or (part == 1) == (3 <= i < 11)
                }
                for a in range(TAPS):
                    i = a * TAPS + b
                    tap = taps_ref[48 - i if flip else i]
                    for r in range(ROWS):
                        if r + a in rows:
                            acc[r] = acc[r] + tap * rows[r + a]
            for r in range(ROWS):
                x_ref[pl.ds(at + r * PITCH, 8), :] = acc[r]
            return carry

        lax.fori_loop(0, tiles, step, 0)

    inputs[0].wait()
    to_planes(lambda at: state_in[at].astype(f32))

    def put_state(r, value):
        s_ext[r + 3, 3 : 3 + PITCH, :] = value

    turn_in(put_state)
    exchange(s_ext, 0)
    pl.semaphore_wait(
        barrier,
        4
        + 2 * has_north.astype(jnp.int32)
        + 2 * has_south.astype(jnp.int32),
    )
    start_copies(0)
    hello(0)

    inputs[1].wait()
    inputs[2].wait()
    land = land_ref[...].astype(f32)
    to_planes(lambda at: cot_in[at].astype(f32) * land[None])

    def put_wet(r, value):
        wet32[pl.ds(pl.multiple_of(r * PITCH, 8), PITCH), :] = value
        wet32[pl.ds(r * PITCH + HALF, 1), :] = jnp.zeros((1, 128), f32)

    turn_in(put_wet)
    acc_ref[...] = jnp.zeros((5, 8, 512), f32)

    def narrow(i, carry):
        at = pl.ds(pl.multiple_of(i * 16, 16), 16)
        w = wet32[at, :]
        wet16[at, :] = w.astype(bf16)
        return carry + w[0:8] + w[8:16]

    acc_ref[0, :, 0:128] = lax.fori_loop(0, CELLS // 16, narrow, jnp.zeros((8, 128), f32))

    for copy in inputs[3:]:
        copy.wait()
    for a in range(TAPS):
        for b in range(TAPS):
            one = kern_ref[a, b : b + 1, :]
            taps_ref[a * TAPS + b] = jnp.broadcast_to(
                jnp.concatenate([one, one], axis=1), (8, 128)
            )
    wbd[...] = jnp.zeros((128, 512), bf16)
    wbd[0:64, 0:256] = we_ref[...]
    wbd[64:128, 256:512] = we_ref[...]
    wpbd[...] = jnp.zeros((128, 512), bf16)
    wpbd[0:64, 0:256] = wp_ref[...]
    wpbd[64:128, 256:512] = wp_ref[...]
    at_row = lax.broadcasted_iota(jnp.int32, (256, 256), 0) // 64
    at_col = lax.broadcasted_iota(jnp.int32, (256, 256), 1) // 64
    mean2_ref[...] = jnp.where(at_row == at_col, 1.0 / CHAN, 0.0).astype(bf16)
    mean_ref[0:128, :] = mean2_ref[0:128, 0:128]
    mean_ref[128:256, :] = mean2_ref[0:128, 0:128]

    def twice(ref):
        return jnp.concatenate([ref[...], ref[...]], axis=1)

    conv_bias = twice(cb_ref)
    gain = twice(gain_ref)
    ln_bias = twice(lb_ref)
    be = twice(be_ref)

    heard(0)
    hello(1)

    def back(q, carry):
        at = pl.ds(pl.multiple_of(q * STEP, STEP), STEP)
        dact_ref[at, :] = dot(wet16[at, :], wpbd[...], NN)
        return carry

    lax.fori_loop(0, CELLS // STEP, back, 0)
    convolve(s_ext, False, conv_bias, TILES - 2, 1, 1)
    heard(1)
    hello(2)
    finish_copies(s_ext, 0)
    convolve(s_ext, False, conv_bias, TILES - 2, 1, 2)
    convolve(s_ext, False, conv_bias, 2, TILES - 1)

    def fold(x):
        return jnp.sum(x.reshape(-1, 8, x.shape[-1]), axis=0)

    def forward(q, carry):
        at = pl.ds(pl.multiple_of(q * PART, PART), PART)
        x = x_ref[at, :]
        cen = x - dot(split(x), mean_ref[...], NN)
        var = dot((cen * cen).astype(bf16), mean_ref[0:128, :], NN)
        rstd = lax.rsqrt(var + ln_eps)
        normed = cen * rstd
        zed = (normed * gain + ln_bias).astype(bf16)
        norm_ref[at, :] = normed
        rstd_ref[at, :] = rstd
        zed_ref[at, :] = zed
        pre_ref[at, :] = dot(zed, wbd[...], NN)
        return carry

    lax.fori_loop(0, CELLS // PART, forward, 0)

    def gelu(i, total):
        rows = pl.ds(pl.multiple_of(i * GROUP, GROUP), GROUP)
        for k in range(4):
            cols = slice(128 * k, 128 * k + 128)
            pre = pre_ref[rows, cols] + be[:, cols]
            grow = jnp.exp2(pre * pre * half_log2e)
            t = 1.0 / (1.0 + (0.3275911 * root_half) * jnp.abs(pre))
            poly = 0.5 * 1.061405429 * t - 0.5 * 1.453152027
            poly = poly * t + 0.5 * 1.421413741
            poly = poly * t - 0.5 * 0.284496736
            poly = poly * t + 0.5 * 0.254829592
            tail = poly * t * grow
            phi = jnp.where(pre >= 0, 1.0 - tail, tail)
            slope = phi + pre * grow * inv_root_tau
            act_ref[rows, cols] = (pre * phi).astype(bf16)
            dhid = (dact_ref[rows, cols] * slope).astype(bf16)
            dhid_ref[rows, cols] = dhid
            acc_ref[1, :, cols] += fold(dhid.astype(f32))
        return total

    lax.fori_loop(0, CELLS // GROUP, gelu, 0)

    def backward(q, carry):
        at = pl.ds(pl.multiple_of(q * BACK, BACK), BACK)
        dzed = dot(dhid_ref[at, :], wbd[...], NT)
        normed = norm_ref[at, :]
        acc_ref[2, :, 0:128] += fold(dzed * normed)
        acc_ref[3, :, 0:128] += fold(dzed)
        dnorm = dzed * gain
        both = jnp.concatenate([dnorm.astype(bf16), (dnorm * normed).astype(bf16)], axis=1)
        means = dot(both, mean2_ref[...], NN)
        dconv = rstd_ref[at, :] * (dnorm - means[:, 0:128] - normed * means[:, 128:256])
        x_ref[at, :] = dconv
        acc_ref[4, :, 0:128] += fold(dconv)
        return carry

    eg_ref[...] = dot(zed_ref[...], dhid_ref[...], TN)
    pg_ref[...] = dot(wet16[...], act_ref[...], TN)

    def halves(x):
        return x + pltpu.roll(x, 64, axis=1)

    for i in range(N_GROUP):
        c, e = 8 * (i // 2), 128 * (i % 2)
        one, two = [
            ref[c : c + 8, e : e + 128] + ref[64 + c : 72 + c, 256 + e : 384 + e]
            for ref in (eg_ref, pg_ref)
        ]
        pay_b[i] = jnp.concatenate([one, two], axis=0).astype(bf16)

    def scatter(pay, part, ssem, rsem):
        copies = []
        for k in range(1, N_GROUP):
            copies.append(
                pltpu.make_async_remote_copy(
                    src_ref=pay.at[lax.rem(la + k, N_GROUP)],
                    dst_ref=part.at[k],
                    send_sem=ssem.at[k],
                    recv_sem=rsem.at[k],
                    device_id=lat_peer(k),
                    device_id_type=MESH,
                )
            )
            copies[-1].start()
        return copies

    def spread(ref, at, peer, ssem, rsem):
        copies = []
        for k in range(1, N_GROUP):
            copies.append(
                pltpu.make_async_remote_copy(
                    src_ref=ref.at[at],
                    dst_ref=ref.at[at],
                    send_sem=ssem.at[k],
                    recv_sem=rsem.at[k],
                    device_id=peer(k),
                    device_id_type=MESH,
                )
            )
            copies[-1].start()
        return copies

    def scattered(pay, part, gather, copies):
        total = pay[la].astype(f32)
        for k in range(1, N_GROUP):
            copies[k - 1].wait()
            total = total + part[k].astype(f32)
        gather[lo] = total.astype(gather.dtype)

    scale = 1.0 / math.sqrt(ROWS * N_GROUP * COLS * N_GROUP)

    def gathered(gather, out, copies):
        for copy in copies:
            copy.wait()
        total = gather[0].astype(f32)
        for k in range(1, N_GROUP):
            total = total + gather[k].astype(f32)
        out[la] = (total * scale).astype(out.dtype)

    heard(2)
    copies_b = scatter(pay_b, part_b, sb1, rb1)
    lax.fori_loop(0, CELLS // BACK, backward, 0)

    for group in ((0, 1, 2), (3, 4), (5, 6)):

        def tap_step(t, acc):
            at = pl.multiple_of(t * 8, 8)
            d = [x_ref[pl.ds(at + r * PITCH, 8), :] for r in range(ROWS)]
            new = list(acc)
            for n, b in enumerate(group):
                for i in range(EXT_ROWS):
                    x = s_ext[i, pl.ds(at + b, 8), :]
                    for a in range(TAPS):
                        if 0 <= i - a < ROWS:
                            new[n * TAPS + a] = new[n * TAPS + a] + d[i - a] * x
            return tuple(new)

        zero = jnp.zeros((8, 128), f32)
        acc = lax.fori_loop(0, TILES, tap_step, (zero,) * (TAPS * len(group)))
        for n, b in enumerate(group):
            for a in range(TAPS):
                tap_out[a * TAPS + b] = acc[n * TAPS + a]

    first_half = lax.broadcasted_iota(jnp.int32, (1, 128), 1) < 64

    def sums_of(x):
        return halves(jnp.sum(x, axis=0, keepdims=True))

    rows = []
    for i in range(25):
        one = sums_of(tap_out[i])
        two = sums_of(tap_out[25 + i]) if i < 24 else jnp.zeros((1, 128), f32)
        rows.append(jnp.where(first_half, one, two))
    wide = jnp.sum(acc_ref[1], axis=0, keepdims=True)
    wide = wide[:, 0:256] + wide[:, 256:512]
    rows.append(wide[:, 0:128])
    rows.append(wide[:, 128:256])
    rows.append(
        jnp.where(first_half, sums_of(acc_ref[4, :, 0:128]), sums_of(acc_ref[2, :, 0:128]))
    )
    rows.append(
        jnp.where(first_half, sums_of(acc_ref[3, :, 0:128]), sums_of(acc_ref[0, :, 0:128]))
    )
    while len(rows) < 32:
        rows.append(jnp.zeros((1, 128), f32))
    for i in range(N_GROUP):
        pay_s[i, 0:1, :] = rows[2 * i]
        pay_s[i, 1:2, :] = rows[2 * i + 1]

    copies_s = scatter(pay_s, part_s, ss1, rs1)
    def place(r, carry):
        d_ext[r + 3, 3 : 3 + PITCH, :] = x_ref[pl.ds(pl.multiple_of(r * PITCH, 8), PITCH), :]
        return carry

    lax.fori_loop(0, ROWS, place, 0)
    exchange(d_ext, 1)
    start_copies(1)

    scattered(pay_b, part_b, gather_b, copies_b)
    copies_b = spread(gather_b, lo, lon_peer, sb2, rb2)
    scattered(pay_s, part_s, gather_s, copies_s)
    copies_s = spread(gather_s, lo, lon_peer, ss2, rs2)

    finish_copies(d_ext, 1)
    convolve(d_ext, True, None, 1, TILES)
    convolve(d_ext, True, None, TILES - 1, 1)
    gathered(gather_b, big_ref, copies_b)
    copies_b = spread(big_ref, la, lat_peer, sb3, rb3)

    def turn_out(p, carry):
        r = p * 2
        g0 = x_ref[pl.ds(pl.multiple_of(r * PITCH, 8), PITCH), :]
        g1 = x_ref[pl.ds(pl.multiple_of(r * PITCH + PITCH, 8), PITCH), :]
        turned[0:PITCH, :] = jnp.where(half_lane, g0, pltpu.roll(g1, 64, axis=1))
        turned[HALF : HALF + PITCH, :] = jnp.where(half_lane, pltpu.roll(g0, 64, axis=1), g1)
        for k in range(3):
            back = turned[128 * k : 128 * k + 128, :].T
            planes[k, pl.ds(r, CHAN, stride=ROWS), :] = back[0:64]
            planes[k, pl.ds(r + 1, CHAN, stride=ROWS), :] = back[64:128]
        return carry

    lax.fori_loop(0, ROWS // 2, turn_out, 0)

    def write_out(i, carry):
        at = pl.ds(pl.multiple_of(i * 8, 8), 8)
        of = pl.ds(pl.multiple_of(i * 64, 64), 64)
        for k in range(3):
            cols = slice(128 * k, min(128 * k + 128, COLS))
            width = cols.stop - cols.start
            value = planes[k, of, 0:width].reshape(8, 8, width)
            grad_ref[at, :, cols] = (cot_in[at, :, cols].astype(f32) + value).astype(bf16)
        return carry

    lax.fori_loop(0, 8, write_out, 0)

    gathered(gather_s, small_ref, copies_s)
    copies_s = spread(small_ref, la, lat_peer, ss3, rs3)
    for copy in copies_b + copies_s:
        copy.wait()


def finish(
    grad_ref,
    big_ref,
    small_ref,
    grad_hbm,
    kern_out,
    cb_out,
    gain_out,
    lb_out,
    expand_out,
    be_out,
    project_out,
    bp_out,
    rows_ref,
    sem,
):
    copy = pltpu.make_async_copy(grad_ref, grad_hbm, sem)
    copy.start()
    for i in range(N_GROUP):
        c, e = 8 * (i // 2), 128 * (i % 2)
        both = big_ref[i].astype(f32)
        expand_out[c : c + 8, e : e + 128] = both[0:8]
        project_out[c : c + 8, e : e + 128] = both[8:16]
    for i in range(N_GROUP):
        rows_ref[2 * i : 2 * i + 2, :] = small_ref[i]
    be_out[:, 0:128] = rows_ref[25:26, :]
    be_out[:, 128:256] = rows_ref[26:27, :]
    cb_out[...] = rows_ref[27:28, 0:64]
    gain_out[...] = pltpu.roll(rows_ref[27:28, :], 64, axis=1)[:, 0:64]
    lb_out[...] = rows_ref[28:29, 0:64]
    bp_out[...] = pltpu.roll(rows_ref[28:29, :], 64, axis=1)[:, 0:64]
    rows = rows_ref[0:32, :]
    turned = pltpu.roll(rows, 64, axis=1)
    for i in range(TAPS * TAPS):
        a, b = i // TAPS, i % TAPS
        of, at = (rows, i) if i < 25 else (turned, i - 25)
        kern_out[a, b : b + 1, :] = of[at : at + 1, 0:64]
    copy.wait()


def far(x):
    return pltpu.with_memory_space_constraint(x, pltpu.HBM)


def body(
    state, land_sea, cotangent, kernel, conv_bias, ln_gain, ln_bias, w_expand, b_expand, w_project
):
    vmem = pl.BlockSpec(memory_space=pltpu.VMEM)
    hbm = pl.BlockSpec(memory_space=pltpu.HBM)
    sds = jax.ShapeDtypeStruct
    sem = pltpu.SemaphoreType.DMA
    big = (N_GROUP, 16, 128)
    small = (N_GROUP, 2, 128)
    grad, big_sums, small_sums = pl.pallas_call(
        kernel_body,
        out_shape=(
            sds((CHAN, ROWS, COLS), bf16),
            sds(big, bf16),
            sds(small, f32),
        ),
        in_specs=[hbm] * 10,
        out_specs=(vmem, vmem, vmem),
        scratch_shapes=[
            pltpu.VMEM((CHAN, ROWS, COLS), bf16),
            pltpu.VMEM((CHAN, ROWS, COLS), bf16),
            pltpu.VMEM((ROWS, COLS), jnp.int32),
            pltpu.VMEM((TAPS, TAPS, CHAN), f32),
            pltpu.VMEM((1, CHAN), f32),
            pltpu.VMEM((1, CHAN), f32),
            pltpu.VMEM((1, CHAN), f32),
            pltpu.VMEM((CHAN, EXPAND), bf16),
            pltpu.VMEM((1, EXPAND), f32),
            pltpu.VMEM((CHAN, EXPAND), bf16),
            pltpu.VMEM((3, CHAN * ROWS, 128), f32),
            pltpu.VMEM((384, 128), f32),
            pltpu.VMEM((EXT_ROWS, EXT_COLS, 128), f32),
            pltpu.VMEM((EXT_ROWS, EXT_COLS, 128), f32),
            pltpu.VMEM((CELLS, 128), f32),
            pltpu.VMEM((CELLS, 128), bf16),
            pltpu.VMEM((CELLS, 128), f32),
            pltpu.VMEM((CELLS, 128), f32),
            pltpu.VMEM((CELLS, 128), f32),
            pltpu.VMEM((CELLS, 128), bf16),
            pltpu.VMEM((CELLS, 512), f32),
            pltpu.VMEM((CELLS, 512), f32),
            pltpu.VMEM((CELLS, 512), bf16),
            pltpu.VMEM((CELLS, 512), bf16),
            pltpu.VMEM((TAPS * TAPS, 8, 128), f32),
            pltpu.VMEM((128, 512), bf16),
            pltpu.VMEM((128, 512), bf16),
            pltpu.VMEM((256, 128), bf16),
            pltpu.VMEM((256, 256), bf16),
            pltpu.VMEM((128, 512), f32),
            pltpu.VMEM((128, 512), f32),
            pltpu.VMEM((5, 8, 512), f32),
            pltpu.VMEM((TAPS * TAPS, 8, 128), f32),
            pltpu.VMEM(big, bf16),
            pltpu.VMEM(big, bf16),
            pltpu.VMEM(big, bf16),
            pltpu.VMEM(small, f32),
            pltpu.VMEM(small, f32),
            pltpu.VMEM(small, f32),
            pltpu.VMEM((2, 2, 3, EXT_COLS, 128), bf16),
            pltpu.VMEM((2, 2, 3, EXT_COLS, 128), bf16),
            pltpu.VMEM((2, 2, ROWS, 8, 128), f32),
            pltpu.VMEM((2, 2, EXT_ROWS, 8, 128), f32),
            pltpu.SemaphoreType.REGULAR((2, 3)),
            sem((10,)),
            sem((2, 2)),
            sem((2, 2)),
            sem((2, 2, 3)),
            sem((2, 2, 3)),
        ]
        + [sem((N_GROUP,))] * 12,
        compiler_params=pltpu.CompilerParams(
            collective_id=0, has_side_effects=True, vmem_limit_bytes=48 * 2**20
        ),
    )(
        *map(
            far,
            (
                state,
                cotangent,
                land_sea,
                kernel.transpose(1, 2, 0),
                conv_bias[None],
                ln_gain[None],
                ln_bias[None],
                w_expand,
                b_expand[None],
                w_project.T,
            ),
        )
    )
    outs = pl.pallas_call(
        finish,
        out_shape=(
            sds((CHAN, ROWS, COLS), bf16),
            sds((TAPS, TAPS, CHAN), f32),
            sds((1, CHAN), f32),
            sds((1, CHAN), f32),
            sds((1, CHAN), f32),
            sds((CHAN, EXPAND), f32),
            sds((1, EXPAND), f32),
            sds((CHAN, EXPAND), f32),
            sds((1, CHAN), f32),
        ),
        in_specs=[vmem] * 3,
        out_specs=(hbm,) + (vmem,) * 8,
        scratch_shapes=[
            pltpu.VMEM((32, 128), f32),
            sem(()),
        ],
        compiler_params=pltpu.CompilerParams(vmem_limit_bytes=8 * 2**20),
    )(grad, big_sums, small_sums)
    outs = list(outs)
    outs[1] = outs[1].transpose(2, 0, 1)
    outs[7] = outs[7].T
    for i in (2, 3, 4, 6, 8):
        outs[i] = outs[i].reshape(-1)
    return tuple(outs)


def solution(mesh):
    in_specs = (
        P(None, "lat", "lon"),
        P("lat", "lon"),
        P(None, "lat", "lon"),
        P(),
        P(),
        P(),
        P(),
        P(),
        P(),
        P(),
    )
    out_specs = (P(None, "lat", "lon"), P(), P(), P(), P(), P(), P(), P(), P())
    return jax.shard_map(body, mesh=mesh, in_specs=in_specs, out_specs=out_specs, check_vma=False)
```

```python
import math

import jax
import jax.numpy as jnp
from jax import lax
from jax.experimental import pallas as pl
from jax.experimental.pallas import tpu as pltpu
from jax.sharding import PartitionSpec as P

TAPS = 7
CHAN = 64
EXPAND = 256
ROWS = 8
COLS = 270
HALF = 135
PITCH = 136
TILES = 17
CELLS = ROWS * PITCH
EXT_ROWS = 14
EXT_COLS = 144
STEP = 272
PART = 1088
GROUP = 272
BACK = 1088
UA = 3
UB = 5
UE = 2
N_GROUP = 16
MESH = pl.DeviceIdType.MESH

ln_eps = 1e-06
root_half = 0.7071067811865476
inv_root_tau = 0.3989422804014327
half_log2e = -0.7213475204444817

f32 = jnp.float32
bf16 = jnp.bfloat16


def dot(a, b, dims):
    return lax.dot_general(a, b, (dims, ((), ())), preferred_element_type=f32)


NN = ((1,), (0,))
NT = ((1,), (1,))
TN = ((0,), (0,))


def split(x):
    hi = x.astype(bf16)
    lo = (x - hi.astype(f32)).astype(bf16)
    return jnp.concatenate([hi, lo], axis=1)


def kernel_body(
    state_hbm,
    cot_hbm,
    land_hbm,
    kern_hbm,
    cb_hbm,
    gain_hbm,
    lb_hbm,
    we_hbm,
    be_hbm,
    wp_hbm,
    grad_ref,
    big_ref,
    small_ref,
    state_in,
    cot_in,
    land_ref,
    kern_ref,
    cb_ref,
    gain_ref,
    lb_ref,
    we_ref,
    be_ref,
    wp_ref,
    planes,
    turned,
    s_ext,
    d_ext,
    wet16,
    x_ref,
    norm_ref,
    rstd_ref,
    zed_ref,
    pre_ref,
    dact_ref,
    act_ref,
    dhid_ref,
    taps_ref,
    wbd,
    wpbd,
    mean_ref,
    mean2_ref,
    eg_ref,
    pg_ref,
    acc_ref,
    tap_out,
    pay_b,
    part_b,
    gather_b,
    pay_s,
    part_s,
    gather_s,
    row_send,
    row_recv,
    col_send,
    col_recv,
    hello_sem,
    in_sem,
    row_ssem,
    row_rsem,
    col_ssem,
    col_rsem,
    sb1,
    rb1,
    sb2,
    rb2,
    sb3,
    rb3,
    ss1,
    rs1,
    ss2,
    rs2,
    ss3,
    rs3,
):
    la = lax.axis_index("lat")
    lo = lax.axis_index("lon")
    east = lax.rem(lo + 1, N_GROUP)
    west = lax.rem(lo + N_GROUP - 1, N_GROUP)
    has_north = la > 0
    has_south = la < N_GROUP - 1

    inputs = [
        pltpu.make_async_copy(src, dst, in_sem.at[i])
        for i, (src, dst) in enumerate(
            (
                (state_hbm, state_in),
                (cot_hbm, cot_in),
                (land_hbm, land_ref),
                (kern_hbm, kern_ref),
                (cb_hbm, cb_ref),
                (gain_hbm, gain_ref),
                (lb_hbm, lb_ref),
                (we_hbm, we_ref),
                (be_hbm, be_ref),
                (wp_hbm, wp_ref),
            )
        )
    ]
    for copy in inputs:
        copy.start()

    def lat_peer(k):
        return {"lat": lax.rem(la + k, N_GROUP), "lon": lo}

    def lon_peer(k):
        return {"lat": la, "lon": lax.rem(lo + k, N_GROUP)}

    barrier = pltpu.get_barrier_semaphore()
    for k in (1, N_GROUP - 1):
        pl.semaphore_signal(barrier, inc=1, device_id=lat_peer(k), device_id_type=MESH)
        pl.semaphore_signal(barrier, inc=1, device_id=lon_peer(k), device_id_type=MESH)
    for side in (east, west):

        @pl.when(has_north)
        def _():
            pl.semaphore_signal(
                barrier, inc=1, device_id={"lat": la - 1, "lon": side}, device_id_type=MESH
            )

        @pl.when(has_south)
        def _():
            pl.semaphore_signal(
                barrier, inc=1, device_id={"lat": la + 1, "lon": side}, device_id_type=MESH
            )

    def hello(n):
        for k in (2**n, N_GROUP - 2**n):
            pl.semaphore_signal(
                hello_sem.at[0, n], inc=1, device_id=lat_peer(k), device_id_type=MESH
            )
            pl.semaphore_signal(
                hello_sem.at[1, n], inc=1, device_id=lon_peer(k), device_id_type=MESH
            )

    def heard(n):
        pl.semaphore_wait(hello_sem.at[0, n], 2)
        pl.semaphore_wait(hello_sem.at[1, n], 2)

    lane = lax.broadcasted_iota(jnp.int32, (ROWS, 8, 128), 2)
    sub = lax.broadcasted_iota(jnp.int32, (ROWS, 8, 128), 1)

    s_ext[:, 136:144, :] = jnp.zeros((EXT_ROWS, 8, 128), f32)
    d_ext[:, 136:144, :] = jnp.zeros((EXT_ROWS, 8, 128), f32)
    for ref in (s_ext, d_ext):

        @pl.when(jnp.logical_not(has_north))
        def _():
            ref[0:3] = jnp.zeros((3, EXT_COLS, 128), f32)

        @pl.when(jnp.logical_not(has_south))
        def _():
            ref[11:14] = jnp.zeros((3, EXT_COLS, 128), f32)

    planes[2] = jnp.zeros((CHAN * ROWS, 128), f32)

    def to_planes(load):
        def step(i, carry):
            at = pl.ds(pl.multiple_of(i * 8, 8), 8)
            x = load(at)
            to = pl.ds(pl.multiple_of(i * 64, 64), 64)
            planes[0, to, :] = x[:, :, 0:128].reshape(64, 128)
            planes[1, to, :] = x[:, :, 128:256].reshape(64, 128)
            planes[2, to, 0:14] = x[:, :, 256:270].reshape(64, 14)
            return carry

        lax.fori_loop(0, 8, step, 0)

    def fold(x):
        return jnp.sum(x.reshape(-1, 8, x.shape[-1]), axis=0)

    half_lane = lax.broadcasted_iota(jnp.int32, (PITCH, 128), 1) < 64

    def turn_in(put):
        def step(p, carry):
            r = p * 2
            for k in range(3):
                both = jnp.concatenate(
                    [
                        planes[k, pl.ds(r, CHAN, stride=ROWS), :],
                        planes[k, pl.ds(r + 1, CHAN, stride=ROWS), :],
                    ],
                    axis=0,
                )
                turned[128 * k : 128 * k + 128, :] = both.astype(bf16).T.astype(f32)
            h0 = turned[0:PITCH, :]
            h1 = turned[HALF : HALF + PITCH, :]
            put(
                r,
                jnp.where(half_lane, h0, pltpu.roll(h1, 64, axis=1)),
                jnp.where(half_lane, pltpu.roll(h0, 64, axis=1), h1),
            )
            return carry

        lax.fori_loop(0, ROWS // 2, step, 0)

    def exchange(ext, n):
        to_east = pltpu.roll(ext[3:11, 135:143, :], 64, axis=2)
        to_west = pltpu.roll(ext[3:11, 1:9, :], 64, axis=2)
        col_send[n, 0] = to_east
        col_send[n, 1] = to_west
        ext[3:11, 0:8, :] = jnp.where((sub < 3) & (lane >= 64), to_east, ext[3:11, 0:8, :])
        ext[3:11, 136:144, :] = jnp.where(
            (sub >= 2) & (sub < 5) & (lane < 64), to_west, ext[3:11, 136:144, :]
        )
        row_send[n, 0] = ext[3:6].astype(bf16)
        row_send[n, 1] = ext[8:11].astype(bf16)

    def rows_copy(n, way):
        return pltpu.make_async_remote_copy(
            src_ref=row_send.at[n, way],
            dst_ref=row_recv.at[n, way],
            send_sem=row_ssem.at[n, way],
            recv_sem=row_rsem.at[n, way],
            device_id={"lat": la - 1 + 2 * way, "lon": lo},
            device_id_type=MESH,
        )

    def cols_copy(n, way, turn):
        src = col_send.at[n, way]
        dst = col_recv.at[n, way]
        if turn == 1:
            src, dst = src.at[0:3], dst.at[11:14]
        elif turn == 2:
            src, dst = src.at[5:8], dst.at[0:3]
        else:
            dst = dst.at[3:11]
        return pltpu.make_async_remote_copy(
            src_ref=src,
            dst_ref=dst,
            send_sem=col_ssem.at[n, way, turn],
            recv_sem=col_rsem.at[n, way, turn],
            device_id={
                "lat": la + (0, -1, 1)[turn],
                "lon": (east, west)[way],
            },
            device_id_type=MESH,
        )

    def start_copies(n):
        @pl.when(has_north)
        def _():
            rows_copy(n, 0).start()
            cols_copy(n, 0, 1).start()
            cols_copy(n, 1, 1).start()

        @pl.when(has_south)
        def _():
            rows_copy(n, 1).start()
            cols_copy(n, 0, 2).start()
            cols_copy(n, 1, 2).start()

        cols_copy(n, 0, 0).start()
        cols_copy(n, 1, 0).start()

    def finish_copies(ext, n):
        @pl.when(has_north)
        def _():
            rows_copy(n, 0).wait_send()
            cols_copy(n, 0, 1).wait_send()
            cols_copy(n, 1, 1).wait_send()
            rows_copy(n, 1).wait_recv()
            cols_copy(n, 0, 2).wait_recv()
            cols_copy(n, 1, 2).wait_recv()
            ext[0:3] = row_recv[n, 1].astype(f32)

        @pl.when(has_south)
        def _():
            rows_copy(n, 1).wait_send()
            cols_copy(n, 0, 2).wait_send()
            cols_copy(n, 1, 2).wait_send()
            rows_copy(n, 0).wait_recv()
            cols_copy(n, 0, 1).wait_recv()
            cols_copy(n, 1, 1).wait_recv()
            ext[11:14] = row_recv[n, 0].astype(f32)

        cols_copy(n, 0, 0).wait()
        cols_copy(n, 1, 0).wait()

        def fill(first, last):
            from_west = col_recv[n, 0, first:last]
            from_east = col_recv[n, 1, first:last]
            m = last - first
            ext[first:last, 0:8, :] = jnp.where(
                (sub[:m] < 3) & (lane[:m] < 64), from_west, ext[first:last, 0:8, :]
            )
            ext[first:last, 136:144, :] = jnp.where(
                (sub[:m] >= 2) & (sub[:m] < 5) & (lane[:m] >= 64),
                from_east,
                ext[first:last, 136:144, :],
            )

        fill(3, 11)

        @pl.when(has_north)
        def _():
            fill(0, 3)

        @pl.when(has_south)
        def _():
            fill(11, 14)

    def convolve(ext, flip, bias, tiles, stride, part=0, unroll=1):
        def one(t):
            at = pl.multiple_of(t * (8 * stride) + 8 * (stride == 1), 8)
            if part == 2:
                acc = [x_ref[pl.ds(at + r * PITCH, 8), :] for r in range(ROWS)]
            else:
                first = jnp.zeros((8, 128), f32)
                if bias is not None:
                    first = first + bias
                acc = [first] * ROWS
            for b in range(TAPS):
                rows = {
                    i: ext[i, pl.ds(at + b, 8), :]
                    for i in range(EXT_ROWS)
                    if part == 0 or (part == 1) == (3 <= i < 11)
                }
                for a in range(TAPS):
                    i = a * TAPS + b
                    tap = taps_ref[48 - i if flip else i]
                    for r in range(ROWS):
                        if r + a in rows:
                            acc[r] = acc[r] + tap * rows[r + a]
            for r in range(ROWS):
                x_ref[pl.ds(at + r * PITCH, 8), :] = acc[r]

        def step(t, carry):
            for u in range(unroll):
                one(t * unroll + u)
            return carry

        lax.fori_loop(0, tiles // unroll, step, 0)

    inputs[0].wait()
    to_planes(lambda at: state_in[at].astype(f32))

    def put_state(r, one, two):
        s_ext[r + 3, 3 : 3 + PITCH, :] = one
        s_ext[r + 4, 3 : 3 + PITCH, :] = two

    turn_in(put_state)
    exchange(s_ext, 0)
    pl.semaphore_wait(
        barrier,
        4
        + 2 * has_north.astype(jnp.int32)
        + 2 * has_south.astype(jnp.int32),
    )
    start_copies(0)
    hello(0)

    inputs[1].wait()
    inputs[2].wait()
    land = land_ref[...].astype(f32)
    to_planes(lambda at: cot_in[at].astype(f32) * land[None])

    acc_ref[...] = jnp.zeros((5, 8, 512), f32)
    own = lax.broadcasted_iota(jnp.int32, (PITCH, 128), 0) < HALF

    def put_wet(r, one, two):
        both = jnp.concatenate([jnp.where(own, one, 0.0), jnp.where(own, two, 0.0)], axis=0)
        wet16[pl.ds(pl.multiple_of(r * PITCH, STEP), STEP), :] = both.astype(bf16)
        acc_ref[0, :, 0:128] += fold(both)

    turn_in(put_wet)

    for copy in inputs[3:]:
        copy.wait()
    for a in range(TAPS):
        for b in range(TAPS):
            one = kern_ref[a, b : b + 1, :]
            taps_ref[a * TAPS + b] = jnp.broadcast_to(
                jnp.concatenate([one, one], axis=1), (8, 128)
            )
    wbd[...] = jnp.zeros((128, 512), bf16)
    wbd[0:64, 0:256] = we_ref[...]
    wbd[64:128, 256:512] = we_ref[...]
    wpbd[...] = jnp.zeros((128, 512), bf16)
    wpbd[0:64, 0:256] = wp_ref[...]
    wpbd[64:128, 256:512] = wp_ref[...]
    at_row = lax.broadcasted_iota(jnp.int32, (256, 256), 0) // 64
    at_col = lax.broadcasted_iota(jnp.int32, (256, 256), 1) // 64
    mean2_ref[...] = jnp.where(at_row == at_col, 1.0 / CHAN, 0.0).astype(bf16)
    mean_ref[0:128, :] = mean2_ref[0:128, 0:128]
    mean_ref[128:256, :] = mean2_ref[0:128, 0:128]

    def twice(ref):
        return jnp.concatenate([ref[...], ref[...]], axis=1)

    conv_bias = twice(cb_ref)
    gain = twice(gain_ref)
    ln_bias = twice(lb_ref)
    be = twice(be_ref)

    heard(0)
    hello(1)

    def back(q, carry):
        at = pl.ds(pl.multiple_of(q * STEP, STEP), STEP)
        dact_ref[at, :] = dot(wet16[at, :], wpbd[...], NN)
        return carry

    lax.fori_loop(0, CELLS // STEP, back, 0)
    convolve(s_ext, False, conv_bias, TILES - 2, 1, 1, UA)
    heard(1)
    hello(2)
    finish_copies(s_ext, 0)
    convolve(s_ext, False, conv_bias, TILES - 2, 1, 2, UB)
    convolve(s_ext, False, conv_bias, 2, TILES - 1, 0, UE)

    def forward(q, carry):
        at = pl.ds(pl.multiple_of(q * PART, PART), PART)
        x = x_ref[at, :]
        cen = x - dot(split(x), mean_ref[...], NN)
        var = dot((cen * cen).astype(bf16), mean_ref[0:128, :], NN)
        rstd = lax.rsqrt(var + ln_eps)
        normed = cen * rstd
        zed = (normed * gain + ln_bias).astype(bf16)
        norm_ref[at, :] = normed
        rstd_ref[at, :] = rstd
        zed_ref[at, :] = zed
        pre_ref[at, :] = dot(zed, wbd[...], NN)
        return carry

    lax.fori_loop(0, CELLS // PART, forward, 0)

    def gelu(i, total):
        rows = pl.ds(pl.multiple_of(i * GROUP, GROUP), GROUP)
        for k in range(4):
            cols = slice(128 * k, 128 * k + 128)
            pre = pre_ref[rows, cols] + be[:, cols]
            grow = jnp.exp2(pre * pre * half_log2e)
            phi = 0.5 + 0.5 * lax.erf(pre * root_half)
            slope = phi + pre * grow * inv_root_tau
            act_ref[rows, cols] = (pre * phi).astype(bf16)
            dhid = (dact_ref[rows, cols] * slope).astype(bf16)
            dhid_ref[rows, cols] = dhid
            acc_ref[1, :, cols] += fold(dhid.astype(f32))
        return total

    lax.fori_loop(0, CELLS // GROUP, gelu, 0)

    def backward(q, carry):
        at = pl.ds(pl.multiple_of(q * BACK, BACK), BACK)
        dzed = dot(dhid_ref[at, :], wbd[...], NT)
        normed = norm_ref[at, :]
        acc_ref[2, :, 0:128] += fold(dzed * normed)
        acc_ref[3, :, 0:128] += fold(dzed)
        dnorm = dzed * gain
        both = jnp.concatenate([dnorm.astype(bf16), (dnorm * normed).astype(bf16)], axis=1)
        means = dot(both, mean2_ref[...], NN)
        dconv = rstd_ref[at, :] * (dnorm - means[:, 0:128] - normed * means[:, 128:256])
        x_ref[at, :] = dconv
        acc_ref[4, :, 0:128] += fold(dconv)
        return carry

    eg_ref[...] = dot(zed_ref[...], dhid_ref[...], TN)
    pg_ref[...] = dot(wet16[...], act_ref[...], TN)
    backward(0, 0)

    def halves(x):
        return x + pltpu.roll(x, 64, axis=1)

    for i in range(N_GROUP):
        c, e = 8 * (i // 2), 128 * (i % 2)
        one, two = [
            ref[c : c + 8, e : e + 128] + ref[64 + c : 72 + c, 256 + e : 384 + e]
            for ref in (eg_ref, pg_ref)
        ]
        pay_b[i] = jnp.concatenate([one, two], axis=0).astype(bf16)

    def scatter(pay, part, ssem, rsem):
        copies = []
        for k in range(1, N_GROUP):
            copies.append(
                pltpu.make_async_remote_copy(
                    src_ref=pay.at[lax.rem(la + k, N_GROUP)],
                    dst_ref=part.at[k],
                    send_sem=ssem.at[k],
                    recv_sem=rsem.at[k],
                    device_id=lat_peer(k),
                    device_id_type=MESH,
                )
            )
            copies[-1].start()
        return copies

    def spread(ref, at, peer, ssem, rsem):
        copies = []
        for k in range(1, N_GROUP):
            copies.append(
                pltpu.make_async_remote_copy(
                    src_ref=ref.at[at],
                    dst_ref=ref.at[at],
                    send_sem=ssem.at[k],
                    recv_sem=rsem.at[k],
                    device_id=peer(k),
                    device_id_type=MESH,
                )
            )
            copies[-1].start()
        return copies

    def scattered(pay, part, gather, copies):
        total = pay[la].astype(f32)
        for k in range(1, N_GROUP):
            copies[k - 1].wait()
            total = total + part[k].astype(f32)
        gather[lo] = total.astype(gather.dtype)

    scale = 1.0 / math.sqrt(ROWS * N_GROUP * COLS * N_GROUP)

    def gathered(gather, out, copies):
        for copy in copies:
            copy.wait()
        total = gather[0].astype(f32)
        for k in range(1, N_GROUP):
            total = total + gather[k].astype(f32)
        out[la] = (total * scale).astype(out.dtype)

    heard(2)
    copies_b = scatter(pay_b, part_b, sb1, rb1)
    def place(r, carry):
        d_ext[r + 3, 3 : 3 + PITCH, :] = x_ref[pl.ds(pl.multiple_of(r * PITCH, 8), PITCH), :]
        return carry

    lax.fori_loop(0, ROWS, place, 0)
    exchange(d_ext, 1)
    start_copies(1)

    for group in ((0, 1, 2), (3, 4), (5, 6)):

        def tap_step(t, acc):
            at = pl.multiple_of(t * 8, 8)
            d = [x_ref[pl.ds(at + r * PITCH, 8), :] for r in range(ROWS)]
            new = list(acc)
            for n, b in enumerate(group):
                for i in range(EXT_ROWS):
                    x = s_ext[i, pl.ds(at + b, 8), :]
                    for a in range(TAPS):
                        if 0 <= i - a < ROWS:
                            new[n * TAPS + a] = new[n * TAPS + a] + d[i - a] * x
            return tuple(new)

        zero = jnp.zeros((8, 128), f32)
        acc = lax.fori_loop(0, TILES, tap_step, (zero,) * (TAPS * len(group)))
        for n, b in enumerate(group):
            for a in range(TAPS):
                tap_out[a * TAPS + b] = acc[n * TAPS + a]

    first_half = lax.broadcasted_iota(jnp.int32, (1, 128), 1) < 64

    def sums_of(x):
        return halves(jnp.sum(x, axis=0, keepdims=True))

    rows = []
    for i in range(25):
        one = sums_of(tap_out[i])
        two = sums_of(tap_out[25 + i]) if i < 24 else jnp.zeros((1, 128), f32)
        rows.append(jnp.where(first_half, one, two))
    wide = jnp.sum(acc_ref[1], axis=0, keepdims=True)
    wide = wide[:, 0:256] + wide[:, 256:512]
    rows.append(wide[:, 0:128])
    rows.append(wide[:, 128:256])
    rows.append(
        jnp.where(first_half, sums_of(acc_ref[4, :, 0:128]), sums_of(acc_ref[2, :, 0:128]))
    )
    rows.append(
        jnp.where(first_half, sums_of(acc_ref[3, :, 0:128]), sums_of(acc_ref[0, :, 0:128]))
    )
    while len(rows) < 32:
        rows.append(jnp.zeros((1, 128), f32))
    for i in range(N_GROUP):
        pay_s[i, 0:1, :] = rows[2 * i]
        pay_s[i, 1:2, :] = rows[2 * i + 1]

    copies_s = scatter(pay_s, part_s, ss1, rs1)

    scattered(pay_b, part_b, gather_b, copies_b)
    copies_b = spread(gather_b, lo, lon_peer, sb2, rb2)
    scattered(pay_s, part_s, gather_s, copies_s)
    copies_s = spread(gather_s, lo, lon_peer, ss2, rs2)

    finish_copies(d_ext, 1)
    convolve(d_ext, True, None, 1, TILES)
    convolve(d_ext, True, None, TILES - 1, 1)
    gathered(gather_b, big_ref, copies_b)
    copies_b = spread(big_ref, la, lat_peer, sb3, rb3)

    def turn_out(p, carry):
        r = p * 2
        g0 = x_ref[pl.ds(pl.multiple_of(r * PITCH, 8), PITCH), :]
        g1 = x_ref[pl.ds(pl.multiple_of(r * PITCH + PITCH, 8), PITCH), :]
        turned[0:PITCH, :] = jnp.where(half_lane, g0, pltpu.roll(g1, 64, axis=1))
        turned[HALF : HALF + PITCH, :] = jnp.where(half_lane, pltpu.roll(g0, 64, axis=1), g1)
        for k in range(3):
            back = turned[128 * k : 128 * k + 128, :].T
            planes[k, pl.ds(r, CHAN, stride=ROWS), :] = back[0:64]
            planes[k, pl.ds(r + 1, CHAN, stride=ROWS), :] = back[64:128]
        return carry

    lax.fori_loop(0, ROWS // 2, turn_out, 0)

    def write_out(i, carry):
        at = pl.ds(pl.multiple_of(i * 8, 8), 8)
        of = pl.ds(pl.multiple_of(i * 64, 64), 64)
        for k in range(3):
            cols = slice(128 * k, min(128 * k + 128, COLS))
            width = cols.stop - cols.start
            value = planes[k, of, 0:width].reshape(8, 8, width)
            grad_ref[at, :, cols] = (cot_in[at, :, cols].astype(f32) + value).astype(bf16)
        return carry

    lax.fori_loop(0, 8, write_out, 0)

    gathered(gather_s, small_ref, copies_s)
    copies_s = spread(small_ref, la, lat_peer, ss3, rs3)
    for copy in copies_b + copies_s:
        copy.wait()


def finish(grad_ref, big_ref, small_ref, *refs):
    outs, staged, sems = refs[0:9], refs[9:17], refs[17]
    kern_out, cb_out, gain_out, lb_out, expand_out, be_out, project_out, bp_out = staged
    copies = [
        pltpu.make_async_copy(src, dst, sems.at[i])
        for i, (src, dst) in enumerate(zip((grad_ref,) + tuple(staged), outs))
    ]
    copies[0].start()
    for i in range(N_GROUP):
        c, e = 8 * (i // 2), 128 * (i % 2)
        both = big_ref[i].astype(f32)
        expand_out[c : c + 8, e : e + 128] = both[0:8]
        project_out[c : c + 8, e : e + 128] = both[8:16]
    copies[5].start()
    copies[7].start()

    def row(i):
        return small_ref[i // 2, i % 2 : i % 2 + 1, :]

    def turned(i):
        return pltpu.roll(row(i), 64, axis=1)

    for i in range(TAPS * TAPS):
        a, b = i // TAPS, i % TAPS
        kern_out[a, b : b + 1, :] = (row(i) if i < 25 else turned(i - 25))[:, 0:64]
    copies[1].start()
    cb_out[...] = row(27)[:, 0:64]
    gain_out[...] = turned(27)[:, 0:64]
    lb_out[...] = row(28)[:, 0:64]
    be_out[:, 0:128] = row(25)
    be_out[:, 128:256] = row(26)
    bp_out[...] = turned(28)[:, 0:64]
    for i in (2, 3, 4, 6, 8):
        copies[i].start()
    for copy in copies:
        copy.wait()


def far(x):
    return pltpu.with_memory_space_constraint(x, pltpu.HBM)


def body(
    state, land_sea, cotangent, kernel, conv_bias, ln_gain, ln_bias, w_expand, b_expand, w_project
):
    vmem = pl.BlockSpec(memory_space=pltpu.VMEM)
    hbm = pl.BlockSpec(memory_space=pltpu.HBM)
    sds = jax.ShapeDtypeStruct
    sem = pltpu.SemaphoreType.DMA
    big = (N_GROUP, 16, 128)
    small = (N_GROUP, 2, 128)
    grad, big_sums, small_sums = pl.pallas_call(
        kernel_body,
        out_shape=(
            sds((CHAN, ROWS, COLS), bf16),
            sds(big, bf16),
            sds(small, f32),
        ),
        in_specs=[hbm] * 10,
        out_specs=(vmem, vmem, vmem),
        scratch_shapes=[
            pltpu.VMEM((CHAN, ROWS, COLS), bf16),
            pltpu.VMEM((CHAN, ROWS, COLS), bf16),
            pltpu.VMEM((ROWS, COLS), jnp.int32),
            pltpu.VMEM((TAPS, TAPS, CHAN), f32),
            pltpu.VMEM((1, CHAN), f32),
            pltpu.VMEM((1, CHAN), f32),
            pltpu.VMEM((1, CHAN), f32),
            pltpu.VMEM((CHAN, EXPAND), bf16),
            pltpu.VMEM((1, EXPAND), f32),
            pltpu.VMEM((CHAN, EXPAND), bf16),
            pltpu.VMEM((3, CHAN * ROWS, 128), f32),
            pltpu.VMEM((384, 128), f32),
            pltpu.VMEM((EXT_ROWS, EXT_COLS, 128), f32),
            pltpu.VMEM((EXT_ROWS, EXT_COLS, 128), f32),
            pltpu.VMEM((CELLS, 128), bf16),
            pltpu.VMEM((CELLS, 128), f32),
            pltpu.VMEM((CELLS, 128), f32),
            pltpu.VMEM((CELLS, 128), f32),
            pltpu.VMEM((CELLS, 128), bf16),
            pltpu.VMEM((CELLS, 512), f32),
            pltpu.VMEM((CELLS, 512), f32),
            pltpu.VMEM((CELLS, 512), bf16),
            pltpu.VMEM((CELLS, 512), bf16),
            pltpu.VMEM((TAPS * TAPS, 8, 128), f32),
            pltpu.VMEM((128, 512), bf16),
            pltpu.VMEM((128, 512), bf16),
            pltpu.VMEM((256, 128), bf16),
            pltpu.VMEM((256, 256), bf16),
            pltpu.VMEM((128, 512), f32),
            pltpu.VMEM((128, 512), f32),
            pltpu.VMEM((5, 8, 512), f32),
            pltpu.VMEM((TAPS * TAPS, 8, 128), f32),
            pltpu.VMEM(big, bf16),
            pltpu.VMEM(big, bf16),
            pltpu.VMEM(big, bf16),
            pltpu.VMEM(small, f32),
            pltpu.VMEM(small, f32),
            pltpu.VMEM(small, f32),
            pltpu.VMEM((2, 2, 3, EXT_COLS, 128), bf16),
            pltpu.VMEM((2, 2, 3, EXT_COLS, 128), bf16),
            pltpu.VMEM((2, 2, ROWS, 8, 128), f32),
            pltpu.VMEM((2, 2, EXT_ROWS, 8, 128), f32),
            pltpu.SemaphoreType.REGULAR((2, 3)),
            sem((10,)),
            sem((2, 2)),
            sem((2, 2)),
            sem((2, 2, 3)),
            sem((2, 2, 3)),
        ]
        + [sem((N_GROUP,))] * 12,
        compiler_params=pltpu.CompilerParams(
            collective_id=0, has_side_effects=True, vmem_limit_bytes=48 * 2**20
        ),
    )(
        *map(
            far,
            (
                state,
                cotangent,
                land_sea,
                kernel.transpose(1, 2, 0),
                conv_bias[None],
                ln_gain[None],
                ln_bias[None],
                w_expand,
                b_expand[None],
                w_project.T,
            ),
        )
    )
    outs = pl.pallas_call(
        finish,
        out_shape=(
            sds((CHAN, ROWS, COLS), bf16),
            sds((TAPS, TAPS, CHAN), f32),
            sds((1, CHAN), f32),
            sds((1, CHAN), f32),
            sds((1, CHAN), f32),
            sds((CHAN, EXPAND), f32),
            sds((1, EXPAND), f32),
            sds((CHAN, EXPAND), f32),
            sds((1, CHAN), f32),
        ),
        in_specs=[vmem] * 3,
        out_specs=(hbm,) * 9,
        scratch_shapes=[
            pltpu.VMEM((TAPS, TAPS, CHAN), f32),
            pltpu.VMEM((1, CHAN), f32),
            pltpu.VMEM((1, CHAN), f32),
            pltpu.VMEM((1, CHAN), f32),
            pltpu.VMEM((CHAN, EXPAND), f32),
            pltpu.VMEM((1, EXPAND), f32),
            pltpu.VMEM((CHAN, EXPAND), f32),
            pltpu.VMEM((1, CHAN), f32),
            sem((9,)),
        ],
        compiler_params=pltpu.CompilerParams(vmem_limit_bytes=8 * 2**20),
    )(grad, big_sums, small_sums)
    outs = list(outs)
    outs[1] = outs[1].transpose(2, 0, 1)
    outs[7] = outs[7].T
    for i in (2, 3, 4, 6, 8):
        outs[i] = outs[i].reshape(-1)
    return tuple(outs)


def solution(mesh):
    in_specs = (
        P(None, "lat", "lon"),
        P("lat", "lon"),
        P(None, "lat", "lon"),
        P(),
        P(),
        P(),
        P(),
        P(),
        P(),
        P(),
    )
    out_specs = (P(None, "lat", "lon"), P(), P(), P(), P(), P(), P(), P(), P())
    return jax.shard_map(body, mesh=mesh, in_specs=in_specs, out_specs=out_specs, check_vma=False)
```

```python
import math

import jax
import jax.numpy as jnp
from jax import lax
from jax.experimental import pallas as pl
from jax.experimental.pallas import tpu as pltpu
from jax.sharding import PartitionSpec as P

TAPS = 7
CHAN = 64
EXPAND = 256
ROWS = 8
COLS = 270
HALF = 135
PITCH = 136
TILES = 17
CELLS = ROWS * PITCH
EXT_ROWS = 14
EXT_COLS = 144
STEP = 272
PART = 1088
GROUP = 272
BACK = 1088
UA = 3
UT = 4
GROUPS = ((0, 1, 2, 3), (4, 5, 6))
UB = 5
UE = 2
N_GROUP = 16
MESH = pl.DeviceIdType.MESH

ln_eps = 1e-06
root_half = 0.7071067811865476
inv_root_tau = 0.3989422804014327
half_log2e = -0.7213475204444817

f32 = jnp.float32
bf16 = jnp.bfloat16


def dot(a, b, dims):
    return lax.dot_general(a, b, (dims, ((), ())), preferred_element_type=f32)


NN = ((1,), (0,))
NT = ((1,), (1,))
TN = ((0,), (0,))


def split(x):
    hi = x.astype(bf16)
    lo = (x - hi.astype(f32)).astype(bf16)
    return jnp.concatenate([hi, lo], axis=1)


def kernel_body(
    state_hbm,
    cot_hbm,
    land_hbm,
    kern_hbm,
    cb_hbm,
    gain_hbm,
    lb_hbm,
    we_hbm,
    be_hbm,
    wp_hbm,
    grad_ref,
    big_ref,
    small_ref,
    state_in,
    cot_in,
    land_ref,
    kern_ref,
    cb_ref,
    gain_ref,
    lb_ref,
    we_ref,
    be_ref,
    wp_ref,
    planes,
    turned,
    s_ext,
    d_ext,
    wet16,
    x_ref,
    norm_ref,
    rstd_ref,
    zed_ref,
    pre_ref,
    dact_ref,
    act_ref,
    dhid_ref,
    taps_ref,
    wbd,
    wpbd,
    mean_ref,
    mean2_ref,
    eg_ref,
    pg_ref,
    acc_ref,
    tap_out,
    pay_b,
    part_b,
    gather_b,
    pay_s,
    part_s,
    gather_s,
    row_send,
    row_recv,
    col_send,
    col_recv,
    hello_sem,
    in_sem,
    row_ssem,
    row_rsem,
    col_ssem,
    col_rsem,
    sb1,
    rb1,
    sb2,
    rb2,
    sb3,
    rb3,
    ss1,
    rs1,
    ss2,
    rs2,
    ss3,
    rs3,
):
    la = lax.axis_index("lat")
    lo = lax.axis_index("lon")
    east = lax.rem(lo + 1, N_GROUP)
    west = lax.rem(lo + N_GROUP - 1, N_GROUP)
    has_north = la > 0
    has_south = la < N_GROUP - 1

    inputs = [
        pltpu.make_async_copy(src, dst, in_sem.at[i])
        for i, (src, dst) in enumerate(
            (
                (state_hbm, state_in),
                (cot_hbm, cot_in),
                (land_hbm, land_ref),
                (kern_hbm, kern_ref),
                (cb_hbm, cb_ref),
                (gain_hbm, gain_ref),
                (lb_hbm, lb_ref),
                (we_hbm, we_ref),
                (be_hbm, be_ref),
                (wp_hbm, wp_ref),
            )
        )
    ]
    for copy in inputs:
        copy.start()

    def lat_peer(k):
        return {"lat": lax.rem(la + k, N_GROUP), "lon": lo}

    def lon_peer(k):
        return {"lat": la, "lon": lax.rem(lo + k, N_GROUP)}

    barrier = pltpu.get_barrier_semaphore()
    for k in (1, N_GROUP - 1):
        pl.semaphore_signal(barrier, inc=1, device_id=lat_peer(k), device_id_type=MESH)
        pl.semaphore_signal(barrier, inc=1, device_id=lon_peer(k), device_id_type=MESH)
    for side in (east, west):

        @pl.when(has_north)
        def _():
            pl.semaphore_signal(
                barrier, inc=1, device_id={"lat": la - 1, "lon": side}, device_id_type=MESH
            )

        @pl.when(has_south)
        def _():
            pl.semaphore_signal(
                barrier, inc=1, device_id={"lat": la + 1, "lon": side}, device_id_type=MESH
            )

    def hello(n):
        for k in (2**n, N_GROUP - 2**n):
            pl.semaphore_signal(
                hello_sem.at[0, n], inc=1, device_id=lat_peer(k), device_id_type=MESH
            )
            pl.semaphore_signal(
                hello_sem.at[1, n], inc=1, device_id=lon_peer(k), device_id_type=MESH
            )

    def heard(n):
        pl.semaphore_wait(hello_sem.at[0, n], 2)
        pl.semaphore_wait(hello_sem.at[1, n], 2)

    lane = lax.broadcasted_iota(jnp.int32, (ROWS, 8, 128), 2)
    sub = lax.broadcasted_iota(jnp.int32, (ROWS, 8, 128), 1)

    s_ext[:, 136:144, :] = jnp.zeros((EXT_ROWS, 8, 128), f32)
    d_ext[:, 136:144, :] = jnp.zeros((EXT_ROWS, 8, 128), f32)
    for ref in (s_ext, d_ext):

        @pl.when(jnp.logical_not(has_north))
        def _():
            ref[0:3] = jnp.zeros((3, EXT_COLS, 128), f32)

        @pl.when(jnp.logical_not(has_south))
        def _():
            ref[11:14] = jnp.zeros((3, EXT_COLS, 128), f32)

    planes[2] = jnp.zeros((CHAN * ROWS, 128), f32)

    def to_planes(load):
        def step(i, carry):
            at = pl.ds(pl.multiple_of(i * 8, 8), 8)
            x = load(at)
            to = pl.ds(pl.multiple_of(i * 64, 64), 64)
            planes[0, to, :] = x[:, :, 0:128].reshape(64, 128)
            planes[1, to, :] = x[:, :, 128:256].reshape(64, 128)
            planes[2, to, 0:14] = x[:, :, 256:270].reshape(64, 14)
            return carry

        lax.fori_loop(0, 8, step, 0)

    def fold(x):
        return jnp.sum(x.reshape(-1, 8, x.shape[-1]), axis=0)

    half_lane = lax.broadcasted_iota(jnp.int32, (PITCH, 128), 1) < 64

    def turn_in(put):
        def step(p, carry):
            r = p * 2
            for k in range(3):
                both = jnp.concatenate(
                    [
                        planes[k, pl.ds(r, CHAN, stride=ROWS), :],
                        planes[k, pl.ds(r + 1, CHAN, stride=ROWS), :],
                    ],
                    axis=0,
                )
                turned[128 * k : 128 * k + 128, :] = both.astype(bf16).T.astype(f32)
            h0 = turned[0:PITCH, :]
            h1 = turned[HALF : HALF + PITCH, :]
            put(
                r,
                jnp.where(half_lane, h0, pltpu.roll(h1, 64, axis=1)),
                jnp.where(half_lane, pltpu.roll(h0, 64, axis=1), h1),
            )
            return carry

        lax.fori_loop(0, ROWS // 2, step, 0)

    def exchange(ext, n):
        to_east = pltpu.roll(ext[3:11, 135:143, :], 64, axis=2)
        to_west = pltpu.roll(ext[3:11, 1:9, :], 64, axis=2)
        col_send[n, 0] = to_east
        col_send[n, 1] = to_west
        ext[3:11, 0:8, :] = jnp.where((sub < 3) & (lane >= 64), to_east, ext[3:11, 0:8, :])
        ext[3:11, 136:144, :] = jnp.where(
            (sub >= 2) & (sub < 5) & (lane < 64), to_west, ext[3:11, 136:144, :]
        )
        row_send[n, 0] = ext[3:6].astype(bf16)
        row_send[n, 1] = ext[8:11].astype(bf16)

    def rows_copy(n, way):
        return pltpu.make_async_remote_copy(
            src_ref=row_send.at[n, way],
            dst_ref=row_recv.at[n, way],
            send_sem=row_ssem.at[n, way],
            recv_sem=row_rsem.at[n, way],
            device_id={"lat": la - 1 + 2 * way, "lon": lo},
            device_id_type=MESH,
        )

    def cols_copy(n, way, turn):
        src = col_send.at[n, way]
        dst = col_recv.at[n, way]
        if turn == 1:
            src, dst = src.at[0:3], dst.at[11:14]
        elif turn == 2:
            src, dst = src.at[5:8], dst.at[0:3]
        else:
            dst = dst.at[3:11]
        return pltpu.make_async_remote_copy(
            src_ref=src,
            dst_ref=dst,
            send_sem=col_ssem.at[n, way, turn],
            recv_sem=col_rsem.at[n, way, turn],
            device_id={
                "lat": la + (0, -1, 1)[turn],
                "lon": (east, west)[way],
            },
            device_id_type=MESH,
        )

    def start_copies(n):
        @pl.when(has_north)
        def _():
            rows_copy(n, 0).start()
            cols_copy(n, 0, 1).start()
            cols_copy(n, 1, 1).start()

        @pl.when(has_south)
        def _():
            rows_copy(n, 1).start()
            cols_copy(n, 0, 2).start()
            cols_copy(n, 1, 2).start()

        cols_copy(n, 0, 0).start()
        cols_copy(n, 1, 0).start()

    def finish_copies(ext, n):
        @pl.when(has_north)
        def _():
            rows_copy(n, 0).wait_send()
            cols_copy(n, 0, 1).wait_send()
            cols_copy(n, 1, 1).wait_send()
            rows_copy(n, 1).wait_recv()
            cols_copy(n, 0, 2).wait_recv()
            cols_copy(n, 1, 2).wait_recv()
            ext[0:3] = row_recv[n, 1].astype(f32)

        @pl.when(has_south)
        def _():
            rows_copy(n, 1).wait_send()
            cols_copy(n, 0, 2).wait_send()
            cols_copy(n, 1, 2).wait_send()
            rows_copy(n, 0).wait_recv()
            cols_copy(n, 0, 1).wait_recv()
            cols_copy(n, 1, 1).wait_recv()
            ext[11:14] = row_recv[n, 0].astype(f32)

        cols_copy(n, 0, 0).wait()
        cols_copy(n, 1, 0).wait()

        def fill(first, last):
            from_west = col_recv[n, 0, first:last]
            from_east = col_recv[n, 1, first:last]
            m = last - first
            ext[first:last, 0:8, :] = jnp.where(
                (sub[:m] < 3) & (lane[:m] < 64), from_west, ext[first:last, 0:8, :]
            )
            ext[first:last, 136:144, :] = jnp.where(
                (sub[:m] >= 2) & (sub[:m] < 5) & (lane[:m] >= 64),
                from_east,
                ext[first:last, 136:144, :],
            )

        fill(3, 11)

        @pl.when(has_north)
        def _():
            fill(0, 3)

        @pl.when(has_south)
        def _():
            fill(11, 14)

    def convolve(ext, flip, bias, tiles, stride, part=0, unroll=1):
        def one(t):
            at = pl.multiple_of(t * (8 * stride) + 8 * (stride == 1), 8)
            if part == 2:
                acc = [x_ref[pl.ds(at + r * PITCH, 8), :] for r in range(ROWS)]
            else:
                first = jnp.zeros((8, 128), f32)
                if bias is not None:
                    first = first + bias
                acc = [first] * ROWS
            for b in range(TAPS):
                rows = {
                    i: ext[i, pl.ds(at + b, 8), :]
                    for i in range(EXT_ROWS)
                    if part == 0 or (part == 1) == (3 <= i < 11)
                }
                for a in range(TAPS):
                    i = a * TAPS + b
                    tap = taps_ref[48 - i if flip else i]
                    for r in range(ROWS):
                        if r + a in rows:
                            acc[r] = acc[r] + tap * rows[r + a]
            for r in range(ROWS):
                x_ref[pl.ds(at + r * PITCH, 8), :] = acc[r]

        def step(t, carry):
            for u in range(unroll):
                one(t * unroll + u)
            return carry

        lax.fori_loop(0, tiles // unroll, step, 0)

    inputs[0].wait()
    to_planes(lambda at: state_in[at].astype(f32))

    def put_state(r, one, two):
        s_ext[r + 3, 3 : 3 + PITCH, :] = one
        s_ext[r + 4, 3 : 3 + PITCH, :] = two

    turn_in(put_state)
    exchange(s_ext, 0)
    pl.semaphore_wait(
        barrier,
        4
        + 2 * has_north.astype(jnp.int32)
        + 2 * has_south.astype(jnp.int32),
    )
    start_copies(0)
    hello(0)

    inputs[1].wait()
    inputs[2].wait()
    land = land_ref[...].astype(f32)
    to_planes(lambda at: cot_in[at].astype(f32) * land[None])

    acc_ref[...] = jnp.zeros((5, 8, 512), f32)
    own = lax.broadcasted_iota(jnp.int32, (PITCH, 128), 0) < HALF

    def put_wet(r, one, two):
        both = jnp.concatenate([jnp.where(own, one, 0.0), jnp.where(own, two, 0.0)], axis=0)
        wet16[pl.ds(pl.multiple_of(r * PITCH, STEP), STEP), :] = both.astype(bf16)
        acc_ref[0, :, 0:128] += fold(both)

    turn_in(put_wet)

    for copy in inputs[3:]:
        copy.wait()
    for a in range(TAPS):
        for b in range(TAPS):
            one = kern_ref[a, b : b + 1, :]
            taps_ref[a * TAPS + b] = jnp.broadcast_to(
                jnp.concatenate([one, one], axis=1), (8, 128)
            )
    wbd[...] = jnp.zeros((128, 512), bf16)
    wbd[0:64, 0:256] = we_ref[...]
    wbd[64:128, 256:512] = we_ref[...]
    wpbd[...] = jnp.zeros((128, 512), bf16)
    wpbd[0:64, 0:256] = wp_ref[...]
    wpbd[64:128, 256:512] = wp_ref[...]
    at_row = lax.broadcasted_iota(jnp.int32, (256, 256), 0) // 64
    at_col = lax.broadcasted_iota(jnp.int32, (256, 256), 1) // 64
    mean2_ref[...] = jnp.where(at_row == at_col, 1.0 / CHAN, 0.0).astype(bf16)
    mean_ref[0:128, :] = mean2_ref[0:128, 0:128]
    mean_ref[128:256, :] = mean2_ref[0:128, 0:128]

    def twice(ref):
        return jnp.concatenate([ref[...], ref[...]], axis=1)

    conv_bias = twice(cb_ref)
    gain = twice(gain_ref)
    ln_bias = twice(lb_ref)
    be = twice(be_ref)

    heard(0)
    hello(1)

    def back(q, carry):
        at = pl.ds(pl.multiple_of(q * STEP, STEP), STEP)
        dact_ref[at, :] = dot(wet16[at, :], wpbd[...], NN)
        return carry

    lax.fori_loop(0, CELLS // STEP, back, 0)
    convolve(s_ext, False, conv_bias, TILES - 2, 1, 1, UA)
    heard(1)
    hello(2)
    finish_copies(s_ext, 0)
    convolve(s_ext, False, conv_bias, TILES - 2, 1, 2, UB)
    convolve(s_ext, False, conv_bias, 2, TILES - 1, 0, UE)

    def forward(q, carry):
        at = pl.ds(pl.multiple_of(q * PART, PART), PART)
        x = x_ref[at, :]
        cen = x - dot(split(x), mean_ref[...], NN)
        var = dot((cen * cen).astype(bf16), mean_ref[0:128, :], NN)
        rstd = lax.rsqrt(var + ln_eps)
        normed = cen * rstd
        zed = (normed * gain + ln_bias).astype(bf16)
        norm_ref[at, :] = normed
        rstd_ref[at, :] = rstd
        zed_ref[at, :] = zed
        pre_ref[at, :] = dot(zed, wbd[...], NN)
        return carry

    lax.fori_loop(0, CELLS // PART, forward, 0)

    def gelu(i, total):
        rows = pl.ds(pl.multiple_of(i * GROUP, GROUP), GROUP)
        for k in range(4):
            cols = slice(128 * k, 128 * k + 128)
            pre = pre_ref[rows, cols] + be[:, cols]
            grow = jnp.exp2(pre * pre * half_log2e)
            phi = 0.5 + 0.5 * lax.erf(pre * root_half)
            slope = phi + pre * grow * inv_root_tau
            act_ref[rows, cols] = (pre * phi).astype(bf16)
            dhid = (dact_ref[rows, cols] * slope).astype(bf16)
            dhid_ref[rows, cols] = dhid
            acc_ref[1, :, cols] += fold(dhid.astype(f32))
        return total

    lax.fori_loop(0, CELLS // GROUP, gelu, 0)

    def backward(q, carry):
        at = pl.ds(pl.multiple_of(q * BACK, BACK), BACK)
        dzed = dot(dhid_ref[at, :], wbd[...], NT)
        normed = norm_ref[at, :]
        acc_ref[2, :, 0:128] += fold(dzed * normed)
        acc_ref[3, :, 0:128] += fold(dzed)
        dnorm = dzed * gain
        both = jnp.concatenate([dnorm.astype(bf16), (dnorm * normed).astype(bf16)], axis=1)
        means = dot(both, mean2_ref[...], NN)
        dconv = rstd_ref[at, :] * (dnorm - means[:, 0:128] - normed * means[:, 128:256])
        x_ref[at, :] = dconv
        acc_ref[4, :, 0:128] += fold(dconv)
        return carry

    eg_ref[...] = dot(zed_ref[...], dhid_ref[...], TN)
    pg_ref[...] = dot(wet16[...], act_ref[...], TN)
    backward(0, 0)

    for i in range(N_GROUP):
        c, e = 8 * (i // 2), 128 * (i % 2)
        one, two = [
            ref[c : c + 8, e : e + 128] + ref[64 + c : 72 + c, 256 + e : 384 + e]
            for ref in (eg_ref, pg_ref)
        ]
        pay_b[i] = jnp.concatenate([one, two], axis=0).astype(bf16)

    def scatter(pay, part, ssem, rsem):
        copies = []
        for k in range(1, N_GROUP):
            copies.append(
                pltpu.make_async_remote_copy(
                    src_ref=pay.at[lax.rem(la + k, N_GROUP)],
                    dst_ref=part.at[k],
                    send_sem=ssem.at[k],
                    recv_sem=rsem.at[k],
                    device_id=lat_peer(k),
                    device_id_type=MESH,
                )
            )
            copies[-1].start()
        return copies

    def spread(ref, at, peer, ssem, rsem):
        copies = []
        for k in range(1, N_GROUP):
            copies.append(
                pltpu.make_async_remote_copy(
                    src_ref=ref.at[at],
                    dst_ref=ref.at[at],
                    send_sem=ssem.at[k],
                    recv_sem=rsem.at[k],
                    device_id=peer(k),
                    device_id_type=MESH,
                )
            )
            copies[-1].start()
        return copies

    def scattered(pay, part, gather, copies):
        total = pay[la].astype(f32)
        for k in range(1, N_GROUP):
            copies[k - 1].wait()
            total = total + part[k].astype(f32)
        gather[lo] = total.astype(gather.dtype)

    scale = 1.0 / math.sqrt(ROWS * N_GROUP * COLS * N_GROUP)

    def gathered(gather, out, copies):
        for copy in copies:
            copy.wait()
        total = gather[0].astype(f32)
        for k in range(1, N_GROUP):
            total = total + gather[k].astype(f32)
        out[la] = (total * scale).astype(out.dtype)

    heard(2)
    copies_b = scatter(pay_b, part_b, sb1, rb1)
    def place(r, carry):
        d_ext[r + 3, 3 : 3 + PITCH, :] = x_ref[pl.ds(pl.multiple_of(r * PITCH, 8), PITCH), :]
        return carry

    lax.fori_loop(0, ROWS, place, 0)
    exchange(d_ext, 1)
    start_copies(1)

    for group in GROUPS:

        def tap_tile(t, acc):
            at = t * 8 if isinstance(t, int) else pl.multiple_of(t * 8, 8)
            d = [x_ref[pl.ds(at + r * PITCH, 8), :] for r in range(ROWS)]
            new = list(acc)
            for n, b in enumerate(group):
                for i in range(EXT_ROWS):
                    x = s_ext[i, pl.ds(at + b, 8), :]
                    for a in range(TAPS):
                        if 0 <= i - a < ROWS:
                            new[n * TAPS + a] = new[n * TAPS + a] + d[i - a] * x
            return tuple(new)

        def tap_step(t, acc):
            for u in range(UT):
                acc = tap_tile(t * UT + 1 + u, acc)
            return acc

        zero = jnp.zeros((8, 128), f32)
        acc = tap_tile(0, (zero,) * (TAPS * len(group)))
        acc = lax.fori_loop(0, (TILES - 1) // UT, tap_step, acc)
        for n, b in enumerate(group):
            for a in range(TAPS):
                tap_out[a * TAPS + b] = acc[n * TAPS + a]

    first_half = lax.broadcasted_iota(jnp.int32, (8, 128), 1) < 64

    def pair(one, two):
        both = jnp.where(first_half, one, two)
        return jnp.sum(
            both + pltpu.roll(jnp.where(first_half, two, one), 64, axis=1), axis=0, keepdims=True
        )

    blank = jnp.zeros((8, 128), f32)
    rows = [pair(tap_out[i], tap_out[25 + i] if i < 24 else blank) for i in range(25)]
    wide = jnp.sum(acc_ref[1], axis=0, keepdims=True)
    wide = wide[:, 0:256] + wide[:, 256:512]
    rows.append(wide[:, 0:128])
    rows.append(wide[:, 128:256])
    rows.append(pair(acc_ref[4, :, 0:128], acc_ref[2, :, 0:128]))
    rows.append(pair(acc_ref[3, :, 0:128], acc_ref[0, :, 0:128]))
    while len(rows) < 32:
        rows.append(jnp.zeros((1, 128), f32))
    for i in range(N_GROUP):
        pay_s[i, 0:1, :] = rows[2 * i]
        pay_s[i, 1:2, :] = rows[2 * i + 1]

    copies_s = scatter(pay_s, part_s, ss1, rs1)

    scattered(pay_b, part_b, gather_b, copies_b)
    copies_b = spread(gather_b, lo, lon_peer, sb2, rb2)
    scattered(pay_s, part_s, gather_s, copies_s)
    copies_s = spread(gather_s, lo, lon_peer, ss2, rs2)

    finish_copies(d_ext, 1)
    convolve(d_ext, True, None, 1, TILES)
    convolve(d_ext, True, None, TILES - 1, 1)
    gathered(gather_b, big_ref, copies_b)
    copies_b = spread(big_ref, la, lat_peer, sb3, rb3)

    def turn_out(p, carry):
        r = p * 2
        g0 = x_ref[pl.ds(pl.multiple_of(r * PITCH, 8), PITCH), :]
        g1 = x_ref[pl.ds(pl.multiple_of(r * PITCH + PITCH, 8), PITCH), :]
        turned[0:PITCH, :] = jnp.where(half_lane, g0, pltpu.roll(g1, 64, axis=1))
        turned[HALF : HALF + PITCH, :] = jnp.where(half_lane, pltpu.roll(g0, 64, axis=1), g1)
        for k in range(3):
            back = turned[128 * k : 128 * k + 128, :].T
            planes[k, pl.ds(r, CHAN, stride=ROWS), :] = back[0:64]
            planes[k, pl.ds(r + 1, CHAN, stride=ROWS), :] = back[64:128]
        return carry

    lax.fori_loop(0, ROWS // 2, turn_out, 0)

    def write_out(i, carry):
        at = pl.ds(pl.multiple_of(i * 8, 8), 8)
        of = pl.ds(pl.multiple_of(i * 64, 64), 64)
        for k in range(3):
            cols = slice(128 * k, min(128 * k + 128, COLS))
            width = cols.stop - cols.start
            value = planes[k, of, 0:width].reshape(8, 8, width)
            grad_ref[at, :, cols] = (cot_in[at, :, cols].astype(f32) + value).astype(bf16)
        return carry

    lax.fori_loop(0, 8, write_out, 0)

    gathered(gather_s, small_ref, copies_s)
    copies_s = spread(small_ref, la, lat_peer, ss3, rs3)
    for copy in copies_b + copies_s:
        copy.wait()


def finish(grad_ref, big_ref, small_ref, *refs):
    outs, staged, sems = refs[0:9], refs[9:17], refs[17]
    kern_out, cb_out, gain_out, lb_out, expand_out, be_out, project_out, bp_out = staged
    copies = [
        pltpu.make_async_copy(src, dst, sems.at[i])
        for i, (src, dst) in enumerate(zip((grad_ref,) + tuple(staged), outs))
    ]
    copies[0].start()
    for i in range(N_GROUP):
        c, e = 8 * (i // 2), 128 * (i % 2)
        both = big_ref[i].astype(f32)
        expand_out[c : c + 8, e : e + 128] = both[0:8]
        project_out[c : c + 8, e : e + 128] = both[8:16]
    copies[5].start()
    copies[7].start()

    def row(i):
        return small_ref[i // 2, i % 2 : i % 2 + 1, :]

    def turned(i):
        return pltpu.roll(row(i), 64, axis=1)

    for i in range(TAPS * TAPS):
        a, b = i // TAPS, i % TAPS
        kern_out[a, b : b + 1, :] = (row(i) if i < 25 else turned(i - 25))[:, 0:64]
    copies[1].start()
    cb_out[...] = row(27)[:, 0:64]
    gain_out[...] = turned(27)[:, 0:64]
    lb_out[...] = row(28)[:, 0:64]
    be_out[:, 0:128] = row(25)
    be_out[:, 128:256] = row(26)
    bp_out[...] = turned(28)[:, 0:64]
    for i in (2, 3, 4, 6, 8):
        copies[i].start()
    for copy in copies:
        copy.wait()


def far(x):
    return pltpu.with_memory_space_constraint(x, pltpu.HBM)


def body(
    state, land_sea, cotangent, kernel, conv_bias, ln_gain, ln_bias, w_expand, b_expand, w_project
):
    vmem = pl.BlockSpec(memory_space=pltpu.VMEM)
    hbm = pl.BlockSpec(memory_space=pltpu.HBM)
    sds = jax.ShapeDtypeStruct
    sem = pltpu.SemaphoreType.DMA
    big = (N_GROUP, 16, 128)
    small = (N_GROUP, 2, 128)
    grad, big_sums, small_sums = pl.pallas_call(
        kernel_body,
        out_shape=(
            sds((CHAN, ROWS, COLS), bf16),
            sds(big, bf16),
            sds(small, f32),
        ),
        in_specs=[hbm] * 10,
        out_specs=(vmem, vmem, vmem),
        scratch_shapes=[
            pltpu.VMEM((CHAN, ROWS, COLS), bf16),
            pltpu.VMEM((CHAN, ROWS, COLS), bf16),
            pltpu.VMEM((ROWS, COLS), jnp.int32),
            pltpu.VMEM((TAPS, TAPS, CHAN), f32),
            pltpu.VMEM((1, CHAN), f32),
            pltpu.VMEM((1, CHAN), f32),
            pltpu.VMEM((1, CHAN), f32),
            pltpu.VMEM((CHAN, EXPAND), bf16),
            pltpu.VMEM((1, EXPAND), f32),
            pltpu.VMEM((CHAN, EXPAND), bf16),
            pltpu.VMEM((3, CHAN * ROWS, 128), f32),
            pltpu.VMEM((384, 128), f32),
            pltpu.VMEM((EXT_ROWS, EXT_COLS, 128), f32),
            pltpu.VMEM((EXT_ROWS, EXT_COLS, 128), f32),
            pltpu.VMEM((CELLS, 128), bf16),
            pltpu.VMEM((CELLS, 128), f32),
            pltpu.VMEM((CELLS, 128), f32),
            pltpu.VMEM((CELLS, 128), f32),
            pltpu.VMEM((CELLS, 128), bf16),
            pltpu.VMEM((CELLS, 512), f32),
            pltpu.VMEM((CELLS, 512), f32),
            pltpu.VMEM((CELLS, 512), bf16),
            pltpu.VMEM((CELLS, 512), bf16),
            pltpu.VMEM((TAPS * TAPS, 8, 128), f32),
            pltpu.VMEM((128, 512), bf16),
            pltpu.VMEM((128, 512), bf16),
            pltpu.VMEM((256, 128), bf16),
            pltpu.VMEM((256, 256), bf16),
            pltpu.VMEM((128, 512), f32),
            pltpu.VMEM((128, 512), f32),
            pltpu.VMEM((5, 8, 512), f32),
            pltpu.VMEM((TAPS * TAPS, 8, 128), f32),
            pltpu.VMEM(big, bf16),
            pltpu.VMEM(big, bf16),
            pltpu.VMEM(big, bf16),
            pltpu.VMEM(small, f32),
            pltpu.VMEM(small, f32),
            pltpu.VMEM(small, f32),
            pltpu.VMEM((2, 2, 3, EXT_COLS, 128), bf16),
            pltpu.VMEM((2, 2, 3, EXT_COLS, 128), bf16),
            pltpu.VMEM((2, 2, ROWS, 8, 128), f32),
            pltpu.VMEM((2, 2, EXT_ROWS, 8, 128), f32),
            pltpu.SemaphoreType.REGULAR((2, 3)),
            sem((10,)),
            sem((2, 2)),
            sem((2, 2)),
            sem((2, 2, 3)),
            sem((2, 2, 3)),
        ]
        + [sem((N_GROUP,))] * 12,
        compiler_params=pltpu.CompilerParams(
            collective_id=0, has_side_effects=True, vmem_limit_bytes=48 * 2**20
        ),
    )(
        *map(
            far,
            (
                state,
                cotangent,
                land_sea,
                kernel.transpose(1, 2, 0),
                conv_bias[None],
                ln_gain[None],
                ln_bias[None],
                w_expand,
                b_expand[None],
                w_project.T,
            ),
        )
    )
    outs = pl.pallas_call(
        finish,
        out_shape=(
            sds((CHAN, ROWS, COLS), bf16),
            sds((TAPS, TAPS, CHAN), f32),
            sds((1, CHAN), f32),
            sds((1, CHAN), f32),
            sds((1, CHAN), f32),
            sds((CHAN, EXPAND), f32),
            sds((1, EXPAND), f32),
            sds((CHAN, EXPAND), f32),
            sds((1, CHAN), f32),
        ),
        in_specs=[vmem] * 3,
        out_specs=(hbm,) * 9,
        scratch_shapes=[
            pltpu.VMEM((TAPS, TAPS, CHAN), f32),
            pltpu.VMEM((1, CHAN), f32),
            pltpu.VMEM((1, CHAN), f32),
            pltpu.VMEM((1, CHAN), f32),
            pltpu.VMEM((CHAN, EXPAND), f32),
            pltpu.VMEM((1, EXPAND), f32),
            pltpu.VMEM((CHAN, EXPAND), f32),
            pltpu.VMEM((1, CHAN), f32),
            sem((9,)),
        ],
        compiler_params=pltpu.CompilerParams(vmem_limit_bytes=8 * 2**20),
    )(grad, big_sums, small_sums)
    outs = list(outs)
    outs[1] = outs[1].transpose(2, 0, 1)
    outs[7] = outs[7].T
    for i in (2, 3, 4, 6, 8):
        outs[i] = outs[i].reshape(-1)
    return tuple(outs)


def solution(mesh):
    in_specs = (
        P(None, "lat", "lon"),
        P("lat", "lon"),
        P(None, "lat", "lon"),
        P(),
        P(),
        P(),
        P(),
        P(),
        P(),
        P(),
    )
    out_specs = (P(None, "lat", "lon"), P(), P(), P(), P(), P(), P(), P(), P())
    return jax.shard_map(body, mesh=mesh, in_specs=in_specs, out_specs=out_specs, check_vma=False)
```

```python
import math

import jax
import jax.numpy as jnp
from jax import lax
from jax.experimental import pallas as pl
from jax.experimental.pallas import tpu as pltpu
from jax.sharding import PartitionSpec as P

TAPS = 7
CHAN = 64
EXPAND = 256
ROWS = 8
COLS = 270
HALF = 135
PITCH = 136
TILES = 17
CELLS = ROWS * PITCH
EXT_ROWS = 14
EXT_COLS = 144
STEP = 272
PART = 1088
GROUP = 272
BACK = 1088
UA = 3
UT = 8
GROUPS = ((0, 1, 2, 3), (4, 5, 6))
UB = 5
UE = 2
N_GROUP = 16
MESH = pl.DeviceIdType.MESH

ln_eps = 1e-06
root_half = 0.7071067811865476
inv_root_tau = 0.3989422804014327
half_log2e = -0.7213475204444817

f32 = jnp.float32
bf16 = jnp.bfloat16


def dot(a, b, dims):
    return lax.dot_general(a, b, (dims, ((), ())), preferred_element_type=f32)


NN = ((1,), (0,))
NT = ((1,), (1,))
TN = ((0,), (0,))


def split(x):
    hi = x.astype(bf16)
    lo = (x - hi.astype(f32)).astype(bf16)
    return jnp.concatenate([hi, lo], axis=1)


def kernel_body(
    state_hbm,
    cot_hbm,
    land_hbm,
    kern_hbm,
    cb_hbm,
    gain_hbm,
    lb_hbm,
    we_hbm,
    be_hbm,
    wp_hbm,
    grad_ref,
    big_ref,
    small_ref,
    state_in,
    cot_in,
    land_ref,
    kern_ref,
    cb_ref,
    gain_ref,
    lb_ref,
    we_ref,
    be_ref,
    wp_ref,
    planes,
    turned,
    s_ext,
    d_ext,
    wet16,
    x_ref,
    norm_ref,
    rstd_ref,
    zed_ref,
    pre_ref,
    dact_ref,
    act_ref,
    dhid_ref,
    taps_ref,
    wbd,
    wpbd,
    mean_ref,
    mean2_ref,
    eg_ref,
    pg_ref,
    acc_ref,
    tap_out,
    pay_b,
    part_b,
    gather_b,
    pay_s,
    part_s,
    gather_s,
    row_send,
    row_recv,
    col_send,
    col_recv,
    hello_sem,
    in_sem,
    row_ssem,
    row_rsem,
    col_ssem,
    col_rsem,
    sb1,
    rb1,
    sb2,
    rb2,
    sb3,
    rb3,
    ss1,
    rs1,
    ss2,
    rs2,
    ss3,
    rs3,
):
    la = lax.axis_index("lat")
    lo = lax.axis_index("lon")
    east = lax.rem(lo + 1, N_GROUP)
    west = lax.rem(lo + N_GROUP - 1, N_GROUP)
    has_north = la > 0
    has_south = la < N_GROUP - 1

    inputs = [
        pltpu.make_async_copy(src, dst, in_sem.at[i])
        for i, (src, dst) in enumerate(
            (
                (state_hbm, state_in),
                (cot_hbm, cot_in),
                (land_hbm, land_ref),
                (kern_hbm, kern_ref),
                (cb_hbm, cb_ref),
                (gain_hbm, gain_ref),
                (lb_hbm, lb_ref),
                (we_hbm, we_ref),
                (be_hbm, be_ref),
                (wp_hbm, wp_ref),
            )
        )
    ]
    for copy in inputs:
        copy.start()

    def lat_peer(k):
        return {"lat": lax.rem(la + k, N_GROUP), "lon": lo}

    def lon_peer(k):
        return {"lat": la, "lon": lax.rem(lo + k, N_GROUP)}

    barrier = pltpu.get_barrier_semaphore()
    for k in (1, N_GROUP - 1):
        pl.semaphore_signal(barrier, inc=1, device_id=lat_peer(k), device_id_type=MESH)
        pl.semaphore_signal(barrier, inc=1, device_id=lon_peer(k), device_id_type=MESH)
    for side in (east, west):

        @pl.when(has_north)
        def _():
            pl.semaphore_signal(
                barrier, inc=1, device_id={"lat": la - 1, "lon": side}, device_id_type=MESH
            )

        @pl.when(has_south)
        def _():
            pl.semaphore_signal(
                barrier, inc=1, device_id={"lat": la + 1, "lon": side}, device_id_type=MESH
            )

    def hello(n):
        for k in (2**n, N_GROUP - 2**n):
            pl.semaphore_signal(
                hello_sem.at[0, n], inc=1, device_id=lat_peer(k), device_id_type=MESH
            )
            pl.semaphore_signal(
                hello_sem.at[1, n], inc=1, device_id=lon_peer(k), device_id_type=MESH
            )

    def heard(n):
        pl.semaphore_wait(hello_sem.at[0, n], 2)
        pl.semaphore_wait(hello_sem.at[1, n], 2)

    lane = lax.broadcasted_iota(jnp.int32, (ROWS, 8, 128), 2)
    sub = lax.broadcasted_iota(jnp.int32, (ROWS, 8, 128), 1)

    s_ext[:, 136:144, :] = jnp.zeros((EXT_ROWS, 8, 128), f32)
    d_ext[:, 136:144, :] = jnp.zeros((EXT_ROWS, 8, 128), f32)
    for ref in (s_ext, d_ext):

        @pl.when(jnp.logical_not(has_north))
        def _():
            ref[0:3] = jnp.zeros((3, EXT_COLS, 128), f32)

        @pl.when(jnp.logical_not(has_south))
        def _():
            ref[11:14] = jnp.zeros((3, EXT_COLS, 128), f32)

    planes[2] = jnp.zeros((CHAN * ROWS, 128), f32)

    def to_planes(load):
        def step(i, carry):
            at = pl.ds(pl.multiple_of(i * 8, 8), 8)
            x = load(at)
            to = pl.ds(pl.multiple_of(i * 64, 64), 64)
            planes[0, to, :] = x[:, :, 0:128].reshape(64, 128)
            planes[1, to, :] = x[:, :, 128:256].reshape(64, 128)
            planes[2, to, 0:14] = x[:, :, 256:270].reshape(64, 14)
            return carry

        lax.fori_loop(0, 8, step, 0)

    def fold(x):
        return jnp.sum(x.reshape(-1, 8, x.shape[-1]), axis=0)

    half_lane = lax.broadcasted_iota(jnp.int32, (PITCH, 128), 1) < 64

    def turn_in(put):
        def step(p, carry):
            r = p * 2
            for k in range(3):
                both = jnp.concatenate(
                    [
                        planes[k, pl.ds(r, CHAN, stride=ROWS), :],
                        planes[k, pl.ds(r + 1, CHAN, stride=ROWS), :],
                    ],
                    axis=0,
                )
                turned[128 * k : 128 * k + 128, :] = both.astype(bf16).T.astype(f32)
            h0 = turned[0:PITCH, :]
            h1 = turned[HALF : HALF + PITCH, :]
            put(
                r,
                jnp.where(half_lane, h0, pltpu.roll(h1, 64, axis=1)),
                jnp.where(half_lane, pltpu.roll(h0, 64, axis=1), h1),
            )
            return carry

        lax.fori_loop(0, ROWS // 2, step, 0)

    def exchange(ext, n):
        to_east = pltpu.roll(ext[3:11, 135:143, :], 64, axis=2)
        to_west = pltpu.roll(ext[3:11, 1:9, :], 64, axis=2)
        col_send[n, 0] = to_east
        col_send[n, 1] = to_west
        ext[3:11, 0:8, :] = jnp.where((sub < 3) & (lane >= 64), to_east, ext[3:11, 0:8, :])
        ext[3:11, 136:144, :] = jnp.where(
            (sub >= 2) & (sub < 5) & (lane < 64), to_west, ext[3:11, 136:144, :]
        )
        row_send[n, 0] = ext[3:6].astype(bf16)
        row_send[n, 1] = ext[8:11].astype(bf16)

    def rows_copy(n, way):
        return pltpu.make_async_remote_copy(
            src_ref=row_send.at[n, way],
            dst_ref=row_recv.at[n, way],
            send_sem=row_ssem.at[n, way],
            recv_sem=row_rsem.at[n, way],
            device_id={"lat": la - 1 + 2 * way, "lon": lo},
            device_id_type=MESH,
        )

    def cols_copy(n, way, turn):
        src = col_send.at[n, way]
        dst = col_recv.at[n, way]
        if turn == 1:
            src, dst = src.at[0:3], dst.at[11:14]
        elif turn == 2:
            src, dst = src.at[5:8], dst.at[0:3]
        else:
            dst = dst.at[3:11]
        return pltpu.make_async_remote_copy(
            src_ref=src,
            dst_ref=dst,
            send_sem=col_ssem.at[n, way, turn],
            recv_sem=col_rsem.at[n, way, turn],
            device_id={
                "lat": la + (0, -1, 1)[turn],
                "lon": (east, west)[way],
            },
            device_id_type=MESH,
        )

    def start_copies(n):
        @pl.when(has_north)
        def _():
            rows_copy(n, 0).start()
            cols_copy(n, 0, 1).start()
            cols_copy(n, 1, 1).start()

        @pl.when(has_south)
        def _():
            rows_copy(n, 1).start()
            cols_copy(n, 0, 2).start()
            cols_copy(n, 1, 2).start()

        cols_copy(n, 0, 0).start()
        cols_copy(n, 1, 0).start()

    def finish_copies(ext, n):
        @pl.when(has_north)
        def _():
            rows_copy(n, 0).wait_send()
            cols_copy(n, 0, 1).wait_send()
            cols_copy(n, 1, 1).wait_send()
            rows_copy(n, 1).wait_recv()
            cols_copy(n, 0, 2).wait_recv()
            cols_copy(n, 1, 2).wait_recv()
            ext[0:3] = row_recv[n, 1].astype(f32)

        @pl.when(has_south)
        def _():
            rows_copy(n, 1).wait_send()
            cols_copy(n, 0, 2).wait_send()
            cols_copy(n, 1, 2).wait_send()
            rows_copy(n, 0).wait_recv()
            cols_copy(n, 0, 1).wait_recv()
            cols_copy(n, 1, 1).wait_recv()
            ext[11:14] = row_recv[n, 0].astype(f32)

        cols_copy(n, 0, 0).wait()
        cols_copy(n, 1, 0).wait()

        def fill(first, last):
            from_west = col_recv[n, 0, first:last]
            from_east = col_recv[n, 1, first:last]
            m = last - first
            ext[first:last, 0:8, :] = jnp.where(
                (sub[:m] < 3) & (lane[:m] < 64), from_west, ext[first:last, 0:8, :]
            )
            ext[first:last, 136:144, :] = jnp.where(
                (sub[:m] >= 2) & (sub[:m] < 5) & (lane[:m] >= 64),
                from_east,
                ext[first:last, 136:144, :],
            )

        fill(3, 11)

        @pl.when(has_north)
        def _():
            fill(0, 3)

        @pl.when(has_south)
        def _():
            fill(11, 14)

    def convolve(ext, flip, bias, tiles, stride, part=0, unroll=1):
        def one(t):
            at = pl.multiple_of(t * (8 * stride) + 8 * (stride == 1), 8)
            if part == 2:
                acc = [x_ref[pl.ds(at + r * PITCH, 8), :] for r in range(ROWS)]
            else:
                first = jnp.zeros((8, 128), f32)
                if bias is not None:
                    first = first + bias
                acc = [first] * ROWS
            for b in range(TAPS):
                rows = {
                    i: ext[i, pl.ds(at + b, 8), :]
                    for i in range(EXT_ROWS)
                    if part == 0 or (part == 1) == (3 <= i < 11)
                }
                for a in range(TAPS):
                    i = a * TAPS + b
                    tap = taps_ref[48 - i if flip else i]
                    for r in range(ROWS):
                        if r + a in rows:
                            acc[r] = acc[r] + tap * rows[r + a]
            for r in range(ROWS):
                x_ref[pl.ds(at + r * PITCH, 8), :] = acc[r]

        def step(t, carry):
            for u in range(unroll):
                one(t * unroll + u)
            return carry

        lax.fori_loop(0, tiles // unroll, step, 0)

    inputs[0].wait()
    to_planes(lambda at: state_in[at].astype(f32))

    def put_state(r, one, two):
        s_ext[r + 3, 3 : 3 + PITCH, :] = one
        s_ext[r + 4, 3 : 3 + PITCH, :] = two

    turn_in(put_state)
    exchange(s_ext, 0)
    pl.semaphore_wait(
        barrier,
        4
        + 2 * has_north.astype(jnp.int32)
        + 2 * has_south.astype(jnp.int32),
    )
    start_copies(0)
    hello(0)

    inputs[1].wait()
    inputs[2].wait()
    land = land_ref[...].astype(f32)
    to_planes(lambda at: cot_in[at].astype(f32) * land[None])

    acc_ref[...] = jnp.zeros((5, 8, 512), f32)
    own = lax.broadcasted_iota(jnp.int32, (PITCH, 128), 0) < HALF

    def put_wet(r, one, two):
        both = jnp.concatenate([jnp.where(own, one, 0.0), jnp.where(own, two, 0.0)], axis=0)
        wet16[pl.ds(pl.multiple_of(r * PITCH, STEP), STEP), :] = both.astype(bf16)
        acc_ref[0, :, 0:128] += fold(both)

    turn_in(put_wet)

    for copy in inputs[3:]:
        copy.wait()
    for a in range(TAPS):
        for b in range(TAPS):
            one = kern_ref[a, b : b + 1, :]
            taps_ref[a * TAPS + b] = jnp.broadcast_to(
                jnp.concatenate([one, one], axis=1), (8, 128)
            )
    wbd[...] = jnp.zeros((128, 512), bf16)
    wbd[0:64, 0:256] = we_ref[...]
    wbd[64:128, 256:512] = we_ref[...]
    wpbd[...] = jnp.zeros((128, 512), bf16)
    wpbd[0:64, 0:256] = wp_ref[...]
    wpbd[64:128, 256:512] = wp_ref[...]
    at_row = lax.broadcasted_iota(jnp.int32, (256, 256), 0) // 64
    at_col = lax.broadcasted_iota(jnp.int32, (256, 256), 1) // 64
    mean2_ref[...] = jnp.where(at_row == at_col, 1.0 / CHAN, 0.0).astype(bf16)
    mean_ref[0:128, :] = mean2_ref[0:128, 0:128]
    mean_ref[128:256, :] = mean2_ref[0:128, 0:128]

    def twice(ref):
        return jnp.concatenate([ref[...], ref[...]], axis=1)

    conv_bias = twice(cb_ref)
    gain = twice(gain_ref)
    ln_bias = twice(lb_ref)
    be = twice(be_ref)

    heard(0)
    hello(1)

    def back(q, carry):
        at = pl.ds(pl.multiple_of(q * STEP, STEP), STEP)
        dact_ref[at, :] = dot(wet16[at, :], wpbd[...], NN)
        return carry

    lax.fori_loop(0, CELLS // STEP, back, 0)
    convolve(s_ext, False, conv_bias, TILES - 2, 1, 1, UA)
    heard(1)
    hello(2)
    finish_copies(s_ext, 0)
    convolve(s_ext, False, conv_bias, TILES - 2, 1, 2, UB)
    convolve(s_ext, False, conv_bias, 2, TILES - 1, 0, UE)

    def forward(q, carry):
        at = pl.ds(pl.multiple_of(q * PART, PART), PART)
        x = x_ref[at, :]
        cen = x - dot(split(x), mean_ref[...], NN)
        var = dot((cen * cen).astype(bf16), mean_ref[0:128, :], NN)
        rstd = lax.rsqrt(var + ln_eps)
        normed = cen * rstd
        zed = (normed * gain + ln_bias).astype(bf16)
        norm_ref[at, :] = normed
        rstd_ref[at, :] = rstd
        zed_ref[at, :] = zed
        pre_ref[at, :] = dot(zed, wbd[...], NN)
        return carry

    lax.fori_loop(0, CELLS // PART, forward, 0)

    def gelu(i, total):
        rows = pl.ds(pl.multiple_of(i * GROUP, GROUP), GROUP)
        for k in range(4):
            cols = slice(128 * k, 128 * k + 128)
            pre = pre_ref[rows, cols] + be[:, cols]
            grow = jnp.exp2(pre * pre * half_log2e)
            phi = 0.5 + 0.5 * lax.erf(pre * root_half)
            slope = phi + pre * grow * inv_root_tau
            act_ref[rows, cols] = (pre * phi).astype(bf16)
            dhid = (dact_ref[rows, cols] * slope).astype(bf16)
            dhid_ref[rows, cols] = dhid
            acc_ref[1, :, cols] += fold(dhid.astype(f32))
        return total

    lax.fori_loop(0, CELLS // GROUP, gelu, 0)

    def backward(q, carry):
        at = pl.ds(pl.multiple_of(q * BACK, BACK), BACK)
        dzed = dot(dhid_ref[at, :], wbd[...], NT)
        normed = norm_ref[at, :]
        acc_ref[2, :, 0:128] += fold(dzed * normed)
        acc_ref[3, :, 0:128] += fold(dzed)
        dnorm = dzed * gain
        both = jnp.concatenate([dnorm.astype(bf16), (dnorm * normed).astype(bf16)], axis=1)
        means = dot(both, mean2_ref[...], NN)
        dconv = rstd_ref[at, :] * (dnorm - means[:, 0:128] - normed * means[:, 128:256])
        x_ref[at, :] = dconv
        acc_ref[4, :, 0:128] += fold(dconv)
        return carry

    eg_ref[...] = dot(zed_ref[...], dhid_ref[...], TN)
    pg_ref[...] = dot(wet16[...], act_ref[...], TN)
    backward(0, 0)

    for i in range(N_GROUP):
        c, e = 8 * (i // 2), 128 * (i % 2)
        one, two = [
            ref[c : c + 8, e : e + 128] + ref[64 + c : 72 + c, 256 + e : 384 + e]
            for ref in (eg_ref, pg_ref)
        ]
        pay_b[i] = jnp.concatenate([one, two], axis=0).astype(bf16)

    def scatter(pay, part, ssem, rsem):
        copies = []
        for k in range(1, N_GROUP):
            copies.append(
                pltpu.make_async_remote_copy(
                    src_ref=pay.at[lax.rem(la + k, N_GROUP)],
                    dst_ref=part.at[k],
                    send_sem=ssem.at[k],
                    recv_sem=rsem.at[k],
                    device_id=lat_peer(k),
                    device_id_type=MESH,
                )
            )
            copies[-1].start()
        return copies

    def spread(ref, at, peer, ssem, rsem):
        copies = []
        for k in range(1, N_GROUP):
            copies.append(
                pltpu.make_async_remote_copy(
                    src_ref=ref.at[at],
                    dst_ref=ref.at[at],
                    send_sem=ssem.at[k],
                    recv_sem=rsem.at[k],
                    device_id=peer(k),
                    device_id_type=MESH,
                )
            )
            copies[-1].start()
        return copies

    def scattered(pay, part, gather, copies):
        total = pay[la].astype(f32)
        for k in range(1, N_GROUP):
            copies[k - 1].wait()
            total = total + part[k].astype(f32)
        gather[lo] = total.astype(gather.dtype)

    scale = 1.0 / math.sqrt(ROWS * N_GROUP * COLS * N_GROUP)

    def gathered(gather, out, copies):
        for copy in copies:
            copy.wait()
        total = gather[0].astype(f32)
        for k in range(1, N_GROUP):
            total = total + gather[k].astype(f32)
        out[la] = (total * scale).astype(out.dtype)

    heard(2)
    copies_b = scatter(pay_b, part_b, sb1, rb1)
    def place(r, carry):
        d_ext[r + 3, 3 : 3 + PITCH, :] = x_ref[pl.ds(pl.multiple_of(r * PITCH, 8), PITCH), :]
        return carry

    lax.fori_loop(0, ROWS, place, 0)
    exchange(d_ext, 1)
    start_copies(1)

    for group in GROUPS:

        def tap_tile(t, acc):
            at = t * 8 if isinstance(t, int) else pl.multiple_of(t * 8, 8)
            d = [x_ref[pl.ds(at + r * PITCH, 8), :] for r in range(ROWS)]
            new = list(acc)
            for n, b in enumerate(group):
                for i in range(EXT_ROWS):
                    x = s_ext[i, pl.ds(at + b, 8), :]
                    for a in range(TAPS):
                        if 0 <= i - a < ROWS:
                            new[n * TAPS + a] = new[n * TAPS + a] + d[i - a] * x
            return tuple(new)

        def tap_step(t, acc):
            for u in range(UT):
                acc = tap_tile(t * UT + 1 + u, acc)
            return acc

        zero = jnp.zeros((8, 128), f32)
        acc = tap_tile(0, (zero,) * (TAPS * len(group)))
        acc = lax.fori_loop(0, (TILES - 1) // UT, tap_step, acc)
        for n, b in enumerate(group):
            for a in range(TAPS):
                tap_out[a * TAPS + b] = acc[n * TAPS + a]

    first_half = lax.broadcasted_iota(jnp.int32, (8, 128), 1) < 64

    def pair(one, two):
        both = jnp.where(first_half, one, two)
        return jnp.sum(
            both + pltpu.roll(jnp.where(first_half, two, one), 64, axis=1), axis=0, keepdims=True
        )

    blank = jnp.zeros((8, 128), f32)
    rows = [pair(tap_out[i], tap_out[25 + i] if i < 24 else blank) for i in range(25)]
    wide = jnp.sum(acc_ref[1], axis=0, keepdims=True)
    wide = wide[:, 0:256] + wide[:, 256:512]
    rows.append(wide[:, 0:128])
    rows.append(wide[:, 128:256])
    rows.append(pair(acc_ref[4, :, 0:128], acc_ref[2, :, 0:128]))
    rows.append(pair(acc_ref[3, :, 0:128], acc_ref[0, :, 0:128]))
    while len(rows) < 32:
        rows.append(jnp.zeros((1, 128), f32))
    for i in range(N_GROUP):
        pay_s[i, 0:1, :] = rows[2 * i]
        pay_s[i, 1:2, :] = rows[2 * i + 1]

    copies_s = scatter(pay_s, part_s, ss1, rs1)

    scattered(pay_b, part_b, gather_b, copies_b)
    copies_b = spread(gather_b, lo, lon_peer, sb2, rb2)
    scattered(pay_s, part_s, gather_s, copies_s)
    copies_s = spread(gather_s, lo, lon_peer, ss2, rs2)

    finish_copies(d_ext, 1)
    convolve(d_ext, True, None, 1, TILES)
    convolve(d_ext, True, None, TILES - 1, 1)
    gathered(gather_b, big_ref, copies_b)
    copies_b = spread(big_ref, la, lat_peer, sb3, rb3)

    def turn_out(p, carry):
        r = p * 2
        g0 = x_ref[pl.ds(pl.multiple_of(r * PITCH, 8), PITCH), :]
        g1 = x_ref[pl.ds(pl.multiple_of(r * PITCH + PITCH, 8), PITCH), :]
        turned[0:PITCH, :] = jnp.where(half_lane, g0, pltpu.roll(g1, 64, axis=1))
        turned[HALF : HALF + PITCH, :] = jnp.where(half_lane, pltpu.roll(g0, 64, axis=1), g1)
        for k in range(3):
            back = turned[128 * k : 128 * k + 128, :].T
            planes[k, pl.ds(r, CHAN, stride=ROWS), :] = back[0:64]
            planes[k, pl.ds(r + 1, CHAN, stride=ROWS), :] = back[64:128]
        return carry

    lax.fori_loop(0, ROWS // 2, turn_out, 0)

    def write_out(i, carry):
        at = pl.ds(pl.multiple_of(i * 8, 8), 8)
        of = pl.ds(pl.multiple_of(i * 64, 64), 64)
        for k in range(3):
            cols = slice(128 * k, min(128 * k + 128, COLS))
            width = cols.stop - cols.start
            value = planes[k, of, 0:width].reshape(8, 8, width)
            grad_ref[at, :, cols] = (cot_in[at, :, cols].astype(f32) + value).astype(bf16)
        return carry

    lax.fori_loop(0, 8, write_out, 0)

    gathered(gather_s, small_ref, copies_s)
    copies_s = spread(small_ref, la, lat_peer, ss3, rs3)
    for copy in copies_b + copies_s:
        copy.wait()


def finish(grad_ref, big_ref, small_ref, *refs):
    outs, staged, sems = refs[0:9], refs[9:17], refs[17]
    kern_out, cb_out, gain_out, lb_out, expand_out, be_out, project_out, bp_out = staged
    copies = [
        pltpu.make_async_copy(src, dst, sems.at[i])
        for i, (src, dst) in enumerate(zip((grad_ref,) + tuple(staged), outs))
    ]
    copies[0].start()
    for i in range(N_GROUP):
        c, e = 8 * (i // 2), 128 * (i % 2)
        both = big_ref[i].astype(f32)
        expand_out[c : c + 8, e : e + 128] = both[0:8]
        project_out[c : c + 8, e : e + 128] = both[8:16]
    copies[5].start()
    copies[7].start()

    def row(i):
        return small_ref[i // 2, i % 2 : i % 2 + 1, :]

    def turned(i):
        return pltpu.roll(row(i), 64, axis=1)

    for i in range(TAPS * TAPS):
        a, b = i // TAPS, i % TAPS
        kern_out[a, b : b + 1, :] = (row(i) if i < 25 else turned(i - 25))[:, 0:64]
    copies[1].start()
    cb_out[...] = row(27)[:, 0:64]
    gain_out[...] = turned(27)[:, 0:64]
    lb_out[...] = row(28)[:, 0:64]
    be_out[:, 0:128] = row(25)
    be_out[:, 128:256] = row(26)
    bp_out[...] = turned(28)[:, 0:64]
    for i in (2, 3, 4, 6, 8):
        copies[i].start()
    for copy in copies:
        copy.wait()


def far(x):
    return pltpu.with_memory_space_constraint(x, pltpu.HBM)


def body(
    state, land_sea, cotangent, kernel, conv_bias, ln_gain, ln_bias, w_expand, b_expand, w_project
):
    vmem = pl.BlockSpec(memory_space=pltpu.VMEM)
    hbm = pl.BlockSpec(memory_space=pltpu.HBM)
    sds = jax.ShapeDtypeStruct
    sem = pltpu.SemaphoreType.DMA
    big = (N_GROUP, 16, 128)
    small = (N_GROUP, 2, 128)
    grad, big_sums, small_sums = pl.pallas_call(
        kernel_body,
        out_shape=(
            sds((CHAN, ROWS, COLS), bf16),
            sds(big, bf16),
            sds(small, f32),
        ),
        in_specs=[hbm] * 10,
        out_specs=(vmem, vmem, vmem),
        scratch_shapes=[
            pltpu.VMEM((CHAN, ROWS, COLS), bf16),
            pltpu.VMEM((CHAN, ROWS, COLS), bf16),
            pltpu.VMEM((ROWS, COLS), jnp.int32),
            pltpu.VMEM((TAPS, TAPS, CHAN), f32),
            pltpu.VMEM((1, CHAN), f32),
            pltpu.VMEM((1, CHAN), f32),
            pltpu.VMEM((1, CHAN), f32),
            pltpu.VMEM((CHAN, EXPAND), bf16),
            pltpu.VMEM((1, EXPAND), f32),
            pltpu.VMEM((CHAN, EXPAND), bf16),
            pltpu.VMEM((3, CHAN * ROWS, 128), f32),
            pltpu.VMEM((384, 128), f32),
            pltpu.VMEM((EXT_ROWS, EXT_COLS, 128), f32),
            pltpu.VMEM((EXT_ROWS, EXT_COLS, 128), f32),
            pltpu.VMEM((CELLS, 128), bf16),
            pltpu.VMEM((CELLS, 128), f32),
            pltpu.VMEM((CELLS, 128), f32),
            pltpu.VMEM((CELLS, 128), f32),
            pltpu.VMEM((CELLS, 128), bf16),
            pltpu.VMEM((CELLS, 512), f32),
            pltpu.VMEM((CELLS, 512), f32),
            pltpu.VMEM((CELLS, 512), bf16),
            pltpu.VMEM((CELLS, 512), bf16),
            pltpu.VMEM((TAPS * TAPS, 8, 128), f32),
            pltpu.VMEM((128, 512), bf16),
            pltpu.VMEM((128, 512), bf16),
            pltpu.VMEM((256, 128), bf16),
            pltpu.VMEM((256, 256), bf16),
            pltpu.VMEM((128, 512), f32),
            pltpu.VMEM((128, 512), f32),
            pltpu.VMEM((5, 8, 512), f32),
            pltpu.VMEM((TAPS * TAPS, 8, 128), f32),
            pltpu.VMEM(big, bf16),
            pltpu.VMEM(big, bf16),
            pltpu.VMEM(big, bf16),
            pltpu.VMEM(small, f32),
            pltpu.VMEM(small, f32),
            pltpu.VMEM(small, f32),
            pltpu.VMEM((2, 2, 3, EXT_COLS, 128), bf16),
            pltpu.VMEM((2, 2, 3, EXT_COLS, 128), bf16),
            pltpu.VMEM((2, 2, ROWS, 8, 128), f32),
            pltpu.VMEM((2, 2, EXT_ROWS, 8, 128), f32),
            pltpu.SemaphoreType.REGULAR((2, 3)),
            sem((10,)),
            sem((2, 2)),
            sem((2, 2)),
            sem((2, 2, 3)),
            sem((2, 2, 3)),
        ]
        + [sem((N_GROUP,))] * 12,
        compiler_params=pltpu.CompilerParams(
            collective_id=0, has_side_effects=True, vmem_limit_bytes=48 * 2**20
        ),
    )(
        *map(
            far,
            (
                state,
                cotangent,
                land_sea,
                kernel.transpose(1, 2, 0),
                conv_bias[None],
                ln_gain[None],
                ln_bias[None],
                w_expand,
                b_expand[None],
                w_project.T,
            ),
        )
    )
    outs = pl.pallas_call(
        finish,
        out_shape=(
            sds((CHAN, ROWS, COLS), bf16),
            sds((TAPS, TAPS, CHAN), f32),
            sds((1, CHAN), f32),
            sds((1, CHAN), f32),
            sds((1, CHAN), f32),
            sds((CHAN, EXPAND), f32),
            sds((1, EXPAND), f32),
            sds((CHAN, EXPAND), f32),
            sds((1, CHAN), f32),
        ),
        in_specs=[vmem] * 3,
        out_specs=(hbm,) * 9,
        scratch_shapes=[
            pltpu.VMEM((TAPS, TAPS, CHAN), f32),
            pltpu.VMEM((1, CHAN), f32),
            pltpu.VMEM((1, CHAN), f32),
            pltpu.VMEM((1, CHAN), f32),
            pltpu.VMEM((CHAN, EXPAND), f32),
            pltpu.VMEM((1, EXPAND), f32),
            pltpu.VMEM((CHAN, EXPAND), f32),
            pltpu.VMEM((1, CHAN), f32),
            sem((9,)),
        ],
        compiler_params=pltpu.CompilerParams(vmem_limit_bytes=8 * 2**20),
    )(grad, big_sums, small_sums)
    outs = list(outs)
    outs[1] = outs[1].transpose(2, 0, 1)
    outs[7] = outs[7].T
    for i in (2, 3, 4, 6, 8):
        outs[i] = outs[i].reshape(-1)
    return tuple(outs)


def solution(mesh):
    in_specs = (
        P(None, "lat", "lon"),
        P("lat", "lon"),
        P(None, "lat", "lon"),
        P(),
        P(),
        P(),
        P(),
        P(),
        P(),
        P(),
    )
    out_specs = (P(None, "lat", "lon"), P(), P(), P(), P(), P(), P(), P(), P())
    return jax.shard_map(body, mesh=mesh, in_specs=in_specs, out_specs=out_specs, check_vma=False)
```
